32 devices in a mesh: study: 8 (over y, x, core), inner: 4 (over z).
Axes of the slice: x: 2, y: 2, z: 4, core: 2. Of those that a mesh axis runs over, the one named last changes fastest.
Arguments:
- trial_count_per_study: int32 [8], P('study'), may hold values from 4 to 1024, as said below
- study_tile_mask: int32 [8, 4], P('study'), may hold values 0 or 1
- sep_order: int32 [512], replicated, may hold values from 0 to 511, each once
- stacked_study_factor: float32 [8192, 1024], P(('study', 'inner')), may hold values from -0.09375 to 0.09375
- diagonal_block_inverses: float32 [8192, 256], P(('study', 'inner')), may hold values from -4 to 4
- coupling: float32 [8192, 512], P(('study', 'inner')), may hold values from -0.25 to 0.25
- targets: float32 [8192, 128], P(('study', 'inner')), may hold values from -6 to 6
- sep_prior: float32 [512, 512], replicated, may hold values from -1 to 2, as said below
Outputs:
- sep_factor: float32 [512, 512], replicated
- sep_solve: float32 [512, 128], replicated
The draws below stay inside these ranges and needn't reach their ends.
Inputs may be any that keep to these rules, and one draw needn't show every extreme that they name: `trial_count_per_study`: some study has exactly 1024 trials. `sep_prior`: symmetric positive definite.
All inputs are finite; a program needn't handle non-finite values. No bound on the sum of `study_tile_mask` on one device may be relied on, other than what follows from the above.
Results may differ from the reference program's by a relative error of at most 0.0003.
Values sent between devices are 32-bit elements; how exact they have to be, the bound alone decides.
No kernel may reach another device: no remote copies, remote signals or barrier semaphores. Data moves between devices by JAX's collectives and lax.ppermute only.
A program may use at most 64 MiB of HBM per device.

```python
import jax
import jax.numpy as jnp
from jax import lax

SEPARATOR_POINTS = 512
TILE = 128
RIGHT_SIDES = 128
DEVICE_SLOTS = 256
COUPLING_TILES = 4
STUDY_SLOTS = 1024
STUDY_COUNT = 8


def draw_trial_count_per_study(key, part):
    first_term, second_term = jax.random.split(key)
    least = STUDY_SLOTS // DEVICE_SLOTS
    base_offset = jax.random.randint(first_term, (STUDY_COUNT,), least, max(least + 1, 2 * STUDY_SLOTS // 3))
    picked_entry = jax.random.randint(second_term, (), 0, STUDY_COUNT)
    return jnp.where(jnp.arange(STUDY_COUNT) == picked_entry, STUDY_SLOTS, base_offset).astype(jnp.int32)


def draw_diagonal_block_inverses(key, part):
    first_term, second_term = jax.random.split(key, 2)
    row_index_list = jnp.arange(STUDY_COUNT * STUDY_SLOTS)[:, None]
    col_ids = jnp.arange(DEVICE_SLOTS)[None, :]
    on_diagonal = row_index_list % DEVICE_SLOTS == col_ids
    diagonal_entries = jax.random.uniform(first_term, (STUDY_COUNT * STUDY_SLOTS, DEVICE_SLOTS), jnp.float32, 0.6, 1.4)
    spread_values = jnp.clip(jax.random.normal(second_term, (STUDY_COUNT * STUDY_SLOTS, DEVICE_SLOTS), jnp.float32), -6.0, 6.0) * (0.4 / DEVICE_SLOTS ** 0.5)
    return jnp.where(on_diagonal, diagonal_entries, spread_values).astype(jnp.float32)


def draw_sep_prior(key, part):
    first_term, second_term = jax.random.split(key)
    raw = jax.random.uniform(first_term, (SEPARATOR_POINTS, SEPARATOR_POINTS), jnp.float32, -1.0, 1.0)
    off = (raw + raw.T) * (0.1 / SEPARATOR_POINTS)
    diagonal_entries = jax.random.uniform(second_term, (SEPARATOR_POINTS,), jnp.float32, 0.5, 1.0)
    eye = jnp.eye(SEPARATOR_POINTS, dtype=jnp.float32)
    return (off * (1.0 - eye) + eye * diagonal_entries[None, :]).astype(jnp.float32)


def set_ends(values, key, smallest, largest):
    longest = values.shape.index(max(values.shape))
    spots = []
    for shift in (0, 1):
        where = [jax.random.randint(jax.random.fold_in(key, axis), (), 0, length) for axis, length in enumerate(values.shape)]
        where[longest] = (where[longest] + shift) % values.shape[longest]
        spots.append(tuple(where))
    return values.at[spots[0]].set(smallest).at[spots[1]].set(largest)


def levels(key, shape, pieces, smallest, largest):
    def one(axis_at, parts):
        draws = jax.random.uniform(jax.random.fold_in(jax.random.fold_in(key, 6), axis_at), (parts,), jnp.float32, smallest / len(pieces), largest / len(pieces))
        return jnp.repeat(jnp.exp(draws), shape[axis_at] // parts).reshape((-1,) + (1,) * (len(shape) - axis_at - 1))

    loudness = one(*pieces[0])
    for cut in pieces[1:]:
        loudness = loudness * one(*cut)
    return loudness


def bell_draw(rng, shape, scale, bound, pieces=(), kind=jnp.bfloat16):
    loudness = levels(rng, shape, pieces, -0.22, 0.18) if pieces else 1.0
    values = jax.random.normal(rng, shape, jnp.float32) * scale * loudness
    return jnp.minimum(jnp.maximum(values, -bound), bound).astype(kind)


def setup_inputs(seed: int = 0) -> dict:
    key_of = jax.random.split(jax.random.key(seed), 9)
    trial_count_per_study = draw_trial_count_per_study(jax.random.fold_in(key_of[8], 71), 0)
    study_tile_mask = set_ends((jax.random.randint(key_of[1], (STUDY_COUNT, COUPLING_TILES), 0, 4) < 3).astype(jnp.int32), jax.random.fold_in(key_of[1], 1), 0, 1)
    sep_order = jax.random.permutation(key_of[2], SEPARATOR_POINTS).astype(jnp.int32)
    stacked_study_factor = bell_draw(key_of[3], (STUDY_COUNT * STUDY_SLOTS, STUDY_SLOTS), (4 * STUDY_SLOTS) ** -0.5, 0.09375, ((0, 32),), jnp.float32)
    diagonal_block_inverses = draw_diagonal_block_inverses(jax.random.fold_in(key_of[8], 71), 0)
    coupling = bell_draw(key_of[5], (STUDY_COUNT * STUDY_SLOTS, SEPARATOR_POINTS), (STUDY_COUNT * STUDY_SLOTS // 16) ** -0.5, 0.25, ((0, 32),), jnp.float32)
    targets = bell_draw(key_of[6], (STUDY_COUNT * STUDY_SLOTS, RIGHT_SIDES), 1.0, 6.0, ((0, 32),), jnp.float32)
    sep_prior = draw_sep_prior(jax.random.fold_in(key_of[8], 71), 0)
    return dict(trial_count_per_study=trial_count_per_study, study_tile_mask=study_tile_mask, sep_order=sep_order, stacked_study_factor=stacked_study_factor, diagonal_block_inverses=diagonal_block_inverses, coupling=coupling, targets=targets, sep_prior=sep_prior)


def reference(trial_count_per_study, study_tile_mask, sep_order, stacked_study_factor, diagonal_block_inverses, coupling, targets, sep_prior):
    highest = lax.Precision.HIGHEST
    block_count = STUDY_SLOTS // DEVICE_SLOTS

    def single_study(items):
        count, mask_row, factor_rows, inverse_rows, couple_rows, target_rows = items
        slot_ids = jnp.arange(STUDY_SLOTS, dtype=jnp.int32)
        position = slot_ids % DEVICE_SLOTS * block_count + slot_ids // DEVICE_SLOTS
        live = (position < count).astype(jnp.float32)[:, None]
        column_mask = jnp.repeat(mask_row.astype(jnp.float32), TILE)[None, :]
        rhs = jnp.concatenate([couple_rows * column_mask, target_rows], axis=1) * live
        solved = []
        for k in range(block_count):
            lower = k * DEVICE_SLOTS
            upper = (k + 1) * DEVICE_SLOTS
            acc = rhs[lower:upper]
            for j in range(k):
                acc = acc - jnp.dot(factor_rows[lower:upper, j * DEVICE_SLOTS:(j + 1) * DEVICE_SLOTS], solved[j], precision=highest)
            block_live = live[lower:upper]
            solved.append(block_live * jnp.dot(inverse_rows[lower:upper], block_live * acc, precision=highest))
        whole = jnp.concatenate(solved, axis=0)
        return jnp.dot(whole[:, :SEPARATOR_POINTS].T, whole, precision=highest)
    term_list = lax.map(single_study, (trial_count_per_study, study_tile_mask, stacked_study_factor.reshape(STUDY_COUNT, STUDY_SLOTS, STUDY_SLOTS), diagonal_block_inverses.reshape(STUDY_COUNT, STUDY_SLOTS, DEVICE_SLOTS), coupling.reshape(STUDY_COUNT, STUDY_SLOTS, SEPARATOR_POINTS), targets.reshape(STUDY_COUNT, STUDY_SLOTS, RIGHT_SIDES)))
    total = jnp.sum(term_list, axis=0)
    precision_block = sep_prior + total[:, :SEPARATOR_POINTS]
    ordered = precision_block[sep_order][:, sep_order]
    sep_factor = jnp.linalg.cholesky(ordered)
    sep_solve = jax.scipy.linalg.solve_triangular(sep_factor, total[sep_order, SEPARATOR_POINTS:], lower=True)
    return (sep_factor, sep_solve)
```

```python
import jax
import jax.numpy as jnp
from jax import lax
from jax.sharding import PartitionSpec as P

HIGHEST = lax.Precision.HIGHEST
HUB = 2


def dot(a, b):
    return jnp.dot(a, b, precision=HIGHEST)


def send(block, source, target):
    return lax.ppermute(block, "inner", [(source, target)])


def swap(block, bit):
    count = lax.axis_size("study")
    return lax.ppermute(block, "study", [(i, i ^ (1 << bit)) for i in range(count)])


def lower_tiles(width, tile):
    count = width // tile
    return [(i, j) for j in range(count) for i in range(j, count + 1)]


def halve(block, bit, me):
    mine = (me >> bit) & 1
    halves = block.reshape(2, block.shape[0] // 2, block.shape[1])
    gone = lax.dynamic_index_in_dim(halves, 1 - mine, 0, keepdims=False)
    kept = lax.dynamic_index_in_dim(halves, mine, 0, keepdims=False)
    return kept, gone


def join(block, other, bit, me):
    mine = (me >> bit) & 1
    first = jnp.where(mine == 0, block, other)
    second = jnp.where(mine == 0, other, block)
    return jnp.concatenate([first, second], axis=0)


def total_over_studies(rows, place):
    me = lax.axis_index("study")
    bits = (lax.axis_size("study") - 1).bit_length()
    kept, gone = halve(rows, 0, me)
    kept = kept + swap(gone, 0)
    orders = [list(range(1, bits)), list(range(bits - 1, 0, -1))]
    parts = list(jnp.split(kept, 2, axis=0))
    for step in range(bits - 1):
        halves = [halve(part, order[step], me) for part, order in zip(parts, orders)]
        come = [swap(half[1], order[step]) for half, order in zip(halves, orders)]
        parts = [half[0] + new for half, new in zip(halves, come)]
    both = jnp.concatenate(parts, axis=0)
    group = lax.axis_size("inner")
    copies = [send(both, HUB, other) for other in range(group) if other != HUB]
    both = jnp.where(place == HUB, both, sum(copies))
    parts = list(jnp.split(both, 2, axis=0))
    for step in range(bits - 2, -1, -1):
        come = [swap(part, order[step]) for part, order in zip(parts, orders)]
        parts = [join(part, new, order[step], me) for part, new, order in zip(parts, come, orders)]
    both = jnp.concatenate(parts, axis=0)
    return join(both, swap(both, 0), 0, me)


def on_device(
    trial_count_per_study,
    study_tile_mask,
    sep_order,
    stacked_study_factor,
    diagonal_block_inverses,
    coupling,
    targets,
    sep_prior,
):
    group_size = lax.axis_size("inner")
    place = lax.axis_index("inner")
    slots = diagonal_block_inverses.shape[0]
    width = sep_prior.shape[0]
    tile_count = study_tile_mask.shape[1]
    tile_width = width // tile_count
    position = jnp.arange(slots, dtype=jnp.int32) * group_size + place
    live = (position < trial_count_per_study[0]).astype(jnp.float32)
    column_mask = jnp.repeat(study_tile_mask[0].astype(jnp.float32), tile_width)[None, :]
    pick = (jnp.arange(width, dtype=jnp.int32)[:, None] == sep_order[None, :]).astype(jnp.float32)
    rhs = jnp.concatenate([dot(coupling * column_mask, pick), targets], axis=1)
    inverse = diagonal_block_inverses * live[:, None] * live[None, :]
    own = dot(inverse, rhs)
    steps = -dot(inverse, stacked_study_factor[:, : (group_size - 1) * slots])
    steps_1 = send(steps[:, :slots], 1, HUB)
    own_0 = send(own, 0, HUB)
    own_1 = send(own, 1, HUB)
    steps_3 = send(steps, 3, HUB)
    own_3 = send(own, 3, HUB)
    prior = dot(dot(pick.T, sep_prior), pick)
    solved = [own_0]
    solved.append(own_1 + dot(steps_1, own_0))
    solved.append(own + dot(steps[:, : 2 * slots], jnp.concatenate(solved, axis=0)))
    solved.append(own_3 + dot(steps_3, jnp.concatenate(solved, axis=0)))
    whole = jnp.concatenate(solved, axis=0)
    gram = dot(whole.T, whole[:, :width])
    t = tile_width
    tiles = lower_tiles(width, t)
    rows = jnp.concatenate([gram[i * t : (i + 1) * t, j * t : (j + 1) * t] for i, j in tiles], axis=0)
    unit = 16 * lax.axis_size("study")
    padded = -(-rows.shape[0] // unit) * unit
    rows = jnp.pad(rows, ((0, padded - rows.shape[0]), (0, 0)))
    total = total_over_studies(rows, place)
    block = {ij: total[k * t : (k + 1) * t] for k, ij in enumerate(tiles)}
    zero = jnp.zeros((t, t), jnp.float32)
    full = jnp.concatenate(
        [jnp.concatenate([block.get((i, j), zero) for j in range(tile_count)], axis=1) for i in range(tile_count + 1)],
        axis=0,
    )
    ordered = prior + full[:width]
    sep_factor = jnp.tril(lax.linalg.cholesky(ordered, symmetrize_input=False))
    sep_solve = jax.scipy.linalg.solve_triangular(sep_factor, full[width:].T, lower=True)
    return (sep_factor, sep_solve)


def solution(mesh):
    return jax.shard_map(
        on_device,
        mesh=mesh,
        in_specs=(
            P("study"),
            P("study", None),
            P(),
            P(("study", "inner"), None),
            P(("study", "inner"), None),
            P(("study", "inner"), None),
            P(("study", "inner"), None),
            P(),
        ),
        out_specs=(P(), P()),
        check_vma=False,
    )
```

```python
import jax
import jax.numpy as jnp
from jax import lax
from jax.experimental import pallas as pl
from jax.experimental.pallas import tpu as pltpu
from jax.sharding import PartitionSpec as P

HIGHEST = lax.Precision.HIGHEST
HUB = 2
PANEL = 16


def dot(a, b):
    return jnp.dot(a, b, precision=HIGHEST)


def send(block, source, target):
    return lax.ppermute(block, "inner", [(source, target)])


def swap(block, bit):
    count = lax.axis_size("study")
    return lax.ppermute(block, "study", [(i, i ^ (1 << bit)) for i in range(count)])


def upper_tiles(width, tile):
    count = width // tile
    return [(i, j) for i in range(count) for j in range(i, count + 1)]


def outer(a, b):
    return lax.dot_general(a, b, (((0,), (0,)), ((), ())), precision=HIGHEST, preferred_element_type=jnp.float32)


def eliminate(block, lane, tile):
    depth, wide = block.shape
    row = lax.broadcasted_iota(jnp.int32, (depth, 1), 0)
    columns = [jnp.broadcast_to(block[:, lane + k : lane + k + 1], (depth, tile)) for k in range(depth)]
    for i in range(depth):
        scale = lax.rsqrt(columns[i][i : i + 1])
        below = jnp.where(row > i, columns[i], 0.0) * scale
        for k in range(i + 1, depth):
            columns[k] = columns[k] - below * (columns[k][i : i + 1] * scale)
        final = block[i : i + 1] * jnp.tile(scale, (1, wide // tile))
        block = jnp.where(row == i, final, block - jnp.tile(below, (1, wide // tile)) * final)
    return block


def factor_kernel(total_ref, prior_ref, factor_ref, solve_ref, upper_ref, work_ref):
    width = prior_ref.shape[0]
    tile = work_ref.shape[0]
    count = width // tile
    where_tile = {ij: k for k, ij in enumerate(upper_tiles(width, tile))}
    upper = lax.broadcasted_iota(jnp.int32, (tile, tile), 0) <= lax.broadcasted_iota(jnp.int32, (tile, tile), 1)
    for i in range(count):
        rows = slice(i * tile, (i + 1) * tile)
        for j in range(i, count + 1):
            k = where_tile[i, j]
            block = total_ref[k * tile : (k + 1) * tile]
            if j < count:
                block = block + prior_ref[rows, j * tile : (j + 1) * tile]
            work_ref[:, j * tile : (j + 1) * tile] = block
        if i:
            done = slice(0, i * tile)
            work_ref[:, i * tile :] = work_ref[:, i * tile :] - outer(upper_ref[done, rows], upper_ref[done, i * tile :])
        for start in range(0, tile, PANEL):
            stop = start + PANEL
            panel = eliminate(work_ref[start:stop, i * tile :], start, tile)
            upper_ref[i * tile + start : i * tile + stop, i * tile :] = panel
            if stop < tile:
                work_ref[stop:, i * tile :] = work_ref[stop:, i * tile :] - outer(panel[:, :tile], panel)[stop:]
        for j in range(count):
            columns = slice(j * tile, (j + 1) * tile)
            if j < i:
                factor_ref[columns, rows] = jnp.zeros((tile, tile), jnp.float32)
            else:
                block = upper_ref[rows, columns]
                factor_ref[columns, rows] = (jnp.where(upper, block, 0.0) if i == j else block).T
        solve_ref[rows] = upper_ref[rows, width:]


def factor_and_solve(total, prior, tile):
    width = prior.shape[0]
    vmem = pl.BlockSpec(memory_space=pltpu.VMEM)
    return pl.pallas_call(
        factor_kernel,
        out_shape=(
            jax.ShapeDtypeStruct((width, width), jnp.float32),
            jax.ShapeDtypeStruct((width, tile), jnp.float32),
        ),
        in_specs=[vmem, vmem],
        out_specs=(vmem, vmem),
        scratch_shapes=[
            pltpu.VMEM((width, width + tile), jnp.float32),
            pltpu.VMEM((tile, width + tile), jnp.float32),
        ],
        compiler_params=pltpu.CompilerParams(vmem_limit_bytes=32 << 20),
        name="factor_and_solve",
    )(total, prior)


def halve(block, bit, me):
    mine = (me >> bit) & 1
    halves = block.reshape(2, block.shape[0] // 2, block.shape[1])
    gone = lax.dynamic_index_in_dim(halves, 1 - mine, 0, keepdims=False)
    kept = lax.dynamic_index_in_dim(halves, mine, 0, keepdims=False)
    return kept, gone


def join(block, other, bit, me):
    mine = (me >> bit) & 1
    first = jnp.where(mine == 0, block, other)
    second = jnp.where(mine == 0, other, block)
    return jnp.concatenate([first, second], axis=0)


def total_over_studies(rows, place):
    me = lax.axis_index("study")
    bits = (lax.axis_size("study") - 1).bit_length()
    kept, gone = halve(rows, 0, me)
    kept = kept + swap(gone, 0)
    orders = [list(range(1, bits)), list(range(bits - 1, 0, -1))]
    parts = list(jnp.split(kept, 2, axis=0))
    for step in range(bits - 1):
        halves = [halve(part, order[step], me) for part, order in zip(parts, orders)]
        come = [swap(half[1], order[step]) for half, order in zip(halves, orders)]
        parts = [half[0] + new for half, new in zip(halves, come)]
    both = jnp.concatenate(parts, axis=0)
    group = lax.axis_size("inner")
    copies = [send(both, HUB, other) for other in range(group) if other != HUB]
    both = jnp.where(place == HUB, both, sum(copies))
    parts = list(jnp.split(both, 2, axis=0))
    for step in range(bits - 2, -1, -1):
        come = [swap(part, order[step]) for part, order in zip(parts, orders)]
        parts = [join(part, new, order[step], me) for part, new, order in zip(parts, come, orders)]
    both = jnp.concatenate(parts, axis=0)
    return join(both, swap(both, 0), 0, me)


def on_device(
    trial_count_per_study,
    study_tile_mask,
    sep_order,
    stacked_study_factor,
    diagonal_block_inverses,
    coupling,
    targets,
    sep_prior,
):
    group_size = lax.axis_size("inner")
    place = lax.axis_index("inner")
    slots = diagonal_block_inverses.shape[0]
    width = sep_prior.shape[0]
    tile_count = study_tile_mask.shape[1]
    tile_width = width // tile_count
    position = jnp.arange(slots, dtype=jnp.int32) * group_size + place
    live = (position < trial_count_per_study[0]).astype(jnp.float32)
    column_mask = jnp.repeat(study_tile_mask[0].astype(jnp.float32), tile_width)[None, :]
    pick = (jnp.arange(width, dtype=jnp.int32)[:, None] == sep_order[None, :]).astype(jnp.float32)
    rhs = jnp.concatenate([dot(coupling * column_mask, pick), targets], axis=1)
    inverse = diagonal_block_inverses * live[:, None] * live[None, :]
    own = dot(inverse, rhs)
    steps = -dot(inverse, stacked_study_factor[:, : (group_size - 1) * slots])
    steps_1 = send(steps[:, :slots], 1, HUB)
    own_0 = send(own, 0, HUB)
    own_1 = send(own, 1, HUB)
    steps_3 = send(steps, 3, HUB)
    own_3 = send(own, 3, HUB)
    prior = dot(dot(pick.T, sep_prior), pick)
    solved = [own_0]
    solved.append(own_1 + dot(steps_1, own_0))
    solved.append(own + dot(steps[:, : 2 * slots], jnp.concatenate(solved, axis=0)))
    solved.append(own_3 + dot(steps_3, jnp.concatenate(solved, axis=0)))
    whole = jnp.concatenate(solved, axis=0)
    gram = dot(whole[:, :width].T, whole)
    t = tile_width
    rows = jnp.concatenate([gram[i * t : (i + 1) * t, j * t : (j + 1) * t] for i, j in upper_tiles(width, t)], axis=0)
    unit = 16 * lax.axis_size("study")
    padded = -(-rows.shape[0] // unit) * unit
    rows = jnp.pad(rows, ((0, padded - rows.shape[0]), (0, 0)))
    total = total_over_studies(rows, place)
    return factor_and_solve(total, prior, t)


def solution(mesh):
    return jax.shard_map(
        on_device,
        mesh=mesh,
        in_specs=(
            P("study"),
            P("study", None),
            P(),
            P(("study", "inner"), None),
            P(("study", "inner"), None),
            P(("study", "inner"), None),
            P(("study", "inner"), None),
            P(),
        ),
        out_specs=(P(), P()),
        check_vma=False,
    )
```

```python
import functools

import jax
import jax.numpy as jnp
from jax import lax
from jax.experimental import pallas as pl
from jax.experimental.pallas import tpu as pltpu
from jax.sharding import PartitionSpec as P

HIGHEST = lax.Precision.HIGHEST
HUB = 2
PANEL = 16


NN = (((1,), (0,)), ((), ()))
TN = (((0,), (0,)), ((), ()))
VMEM = pl.BlockSpec(memory_space=pltpu.VMEM)
SMEM = pl.BlockSpec(memory_space=pltpu.SMEM)
ANY = pl.BlockSpec(memory_space=pl.ANY)
HBM = pl.BlockSpec(memory_space=pltpu.HBM)


def call(kernel, name, out_shape, in_specs, flops, scratch_shapes=()):
    many = isinstance(out_shape, tuple)
    return pl.pallas_call(
        kernel,
        out_shape=out_shape,
        in_specs=in_specs,
        out_specs=(VMEM,) * len(out_shape) if many else VMEM,
        scratch_shapes=scratch_shapes,
        cost_estimate=pl.CostEstimate(flops=flops, bytes_accessed=1 << 20, transcendentals=0),
        compiler_params=pltpu.CompilerParams(vmem_limit_bytes=16 << 20),
        name=name,
    )


def floats(*shape):
    return jax.ShapeDtypeStruct(shape, jnp.float32)


def split(x):
    high = x.astype(jnp.bfloat16)
    return high, (x - high.astype(jnp.float32)).astype(jnp.bfloat16)


def product(a, b, dims=NN):
    def one(x, y):
        return lax.dot_general(x, y, dims, preferred_element_type=jnp.float32)

    return one(a[0], b[0]) + (one(a[0], b[1]) + one(a[1], b[0]))


def exchange(block, mask):
    count = lax.axis_size("study")
    return lax.ppermute(block, "study", [(i, i ^ mask) for i in range(count)])


def send(block, source, target):
    return lax.ppermute(block, "inner", [(source, target)])


def upper_tiles(width, tile):
    count = width // tile
    return [(i, j) for i in range(count) for j in range(i, count + 1)]


def outer(a, b):
    return lax.dot_general(a, b, (((0,), (0,)), ((), ())), precision=HIGHEST, preferred_element_type=jnp.float32)


def eliminate(block, lane, tile):
    depth, wide = block.shape
    row = lax.broadcasted_iota(jnp.int32, (depth, 1), 0)
    columns = [jnp.broadcast_to(block[:, lane + k : lane + k + 1], (depth, tile)) for k in range(depth)]
    for i in range(depth):
        scale = lax.rsqrt(columns[i][i : i + 1])
        below = jnp.where(row > i, columns[i], 0.0) * scale
        for k in range(i + 1, depth):
            columns[k] = columns[k] - below * (columns[k][i : i + 1] * scale)
        final = block[i : i + 1] * jnp.tile(scale, (1, wide // tile))
        block = jnp.where(row == i, final, block - jnp.tile(below, (1, wide // tile)) * final)
    return block


def factor_kernel(total_ref, prior_ref, factor_ref, solve_ref, upper_ref, work_ref):
    width = prior_ref.shape[0]
    tile = work_ref.shape[0]
    count = width // tile
    where_tile = {ij: k for k, ij in enumerate(upper_tiles(width, tile))}
    upper = lax.broadcasted_iota(jnp.int32, (tile, tile), 0) <= lax.broadcasted_iota(jnp.int32, (tile, tile), 1)
    for i in range(count):
        rows = slice(i * tile, (i + 1) * tile)
        for j in range(i, count + 1):
            k = where_tile[i, j]
            block = total_ref[k * tile : (k + 1) * tile]
            if j < count:
                block = block + prior_ref[rows, j * tile : (j + 1) * tile]
            work_ref[:, j * tile : (j + 1) * tile] = block
        if i:
            done = slice(0, i * tile)
            work_ref[:, i * tile :] = work_ref[:, i * tile :] - outer(upper_ref[done, rows], upper_ref[done, i * tile :])
        for start in range(0, tile, PANEL):
            stop = start + PANEL
            panel = eliminate(work_ref[start:stop, i * tile :], start, tile)
            upper_ref[i * tile + start : i * tile + stop, i * tile :] = panel
            if stop < tile:
                work_ref[stop:, i * tile :] = work_ref[stop:, i * tile :] - outer(panel[:, :tile], panel)[stop:]
        for j in range(count):
            columns = slice(j * tile, (j + 1) * tile)
            if j < i:
                factor_ref[columns, rows] = jnp.zeros((tile, tile), jnp.float32)
            else:
                block = upper_ref[rows, columns]
                factor_ref[columns, rows] = (jnp.where(upper, block, 0.0) if i == j else block).T
        solve_ref[rows] = upper_ref[rows, width:]


def live_inverse(count_ref, inverse):
    slots = inverse.shape[0]
    place, places = lax.axis_index("inner"), lax.axis_size("inner")

    def live(shape, axis):
        position = lax.broadcasted_iota(jnp.int32, shape, axis) * places + place
        return (position < count_ref[0]).astype(jnp.float32)

    return inverse * live((slots, 1), 0) * live((1, slots), 1)


def picker(order_ref):
    width = order_ref.shape[1]
    return (lax.broadcasted_iota(jnp.int32, (width, width), 0) == order_ref[...]).astype(jnp.float32)


def steps_kernel(count_ref, inverse_hbm, factor_hbm, first_ref, steps_ref, inverse_ref, factor_ref, sems):
    slots, reach = factor_ref.shape
    inverse_copy = pltpu.make_async_copy(inverse_hbm, inverse_ref, sems.at[0])
    factor_copy = pltpu.make_async_copy(factor_hbm.at[:, :reach], factor_ref, sems.at[1])
    inverse_copy.start()
    factor_copy.start()
    inverse_copy.wait()
    inverse = split(-live_inverse(count_ref, inverse_ref[...]))
    factor_copy.wait()
    steps = product(inverse, split(factor_ref[...]))
    steps_ref[...] = steps
    first_ref[...] = steps[:, :slots]


def own_kernel(count_ref, mask_ref, order_ref, inverse_ref, coupling_ref, targets_ref, after_ref, own_ref):
    width, tile = coupling_ref.shape[1], coupling_ref.shape[1] // mask_ref.shape[1]
    inverse = split(live_inverse(count_ref, inverse_ref[...]))
    lane_tile = lax.broadcasted_iota(jnp.int32, (1, width), 1) // tile
    column_mask = jnp.zeros((1, width), jnp.float32)
    for t in range(width // tile):
        column_mask = jnp.where(lane_tile == t, mask_ref[0, t].astype(jnp.float32), column_mask)
    pick = picker(order_ref).astype(jnp.bfloat16)

    def ordered(x):
        return lax.dot_general(x, pick, NN, preferred_element_type=jnp.float32).astype(jnp.bfloat16)

    high, low = split(coupling_ref[...] * column_mask)
    own_ref[:, :width] = product(inverse, (ordered(high), ordered(low)))
    own_ref[:, width:] = product(inverse, split(targets_ref[...]))


def chain_kernel(order_ref, prior_ref, steps_ref, steps_1_ref, steps_3_ref, high_ref, low_ref, ordered_ref):
    slots = steps_1_ref.shape[0]
    cut = [slice(k * slots, (k + 1) * slots) for k in range(3)]
    step_10 = steps_1_ref[...]
    step_21 = steps_ref[:, cut[1]]
    step_31, step_32 = split(steps_3_ref[:, cut[1]]), split(steps_3_ref[:, cut[2]])
    step_20 = steps_ref[:, cut[0]] + product(split(step_21), split(step_10))
    zero = jnp.zeros_like(step_10)
    chained = [
        [step_10, zero, zero],
        [step_20, step_21, zero],
        [
            steps_3_ref[:, cut[0]] + product(step_31, split(step_10)) + product(step_32, split(step_20)),
            steps_3_ref[:, cut[1]] + product(step_32, split(step_21)),
            steps_3_ref[:, cut[2]],
        ],
    ]
    for row in range(3):
        for column in range(3):
            high_ref[cut[row], cut[column]], low_ref[cut[row], cut[column]] = split(chained[row][column])
    pick = picker(order_ref)
    rows = lax.dot_general(pick, prior_ref[...], TN, precision=HIGHEST, preferred_element_type=jnp.float32)
    ordered_ref[...] = jnp.dot(rows, pick, precision=HIGHEST, preferred_element_type=jnp.float32)


def gram_kernel(tile, high_ref, low_ref, own_0_ref, own_1_ref, own_2_ref, own_3_ref, rows_ref):
    slots, wide = own_0_ref.shape
    own = [own_0_ref[...], own_1_ref[...], own_2_ref[...], own_3_ref[...]]
    known = [split(x) for x in own[:3]]
    high, low = (jnp.concatenate([x[side] for x in known], axis=0) for side in range(2))
    solved = [known[0]]
    for k in range(3):
        rows, columns = slice(k * slots, (k + 1) * slots), slice(0, (k + 1) * slots)
        step = product((high_ref[rows, columns], low_ref[rows, columns]), (high[columns], low[columns]))
        solved.append(split(own[k + 1] + step))
    high, low = (jnp.concatenate([x[side] for x in solved], axis=0) for side in range(2))
    count = wide // tile - 1
    where_tile = {ij: k for k, ij in enumerate(upper_tiles(count * tile, tile))}
    pair = 2
    for first in range(0, count, pair):
        left, right = slice(first * tile, (first + pair) * tile), slice(first * tile, wide)
        block = product((high[:, left], low[:, left]), (high[:, right], low[:, right]), TN)
        for i in range(first, first + pair):
            for j in range(i, count + 1):
                k = where_tile[i, j]
                a, b = (i - first) * tile, (j - first) * tile
                rows_ref[k * tile : (k + 1) * tile] = block[a : a + tile, b : b + tile]
    used = len(where_tile) * tile
    if rows_ref.shape[0] > used:
        rows_ref[used:] = jnp.zeros((rows_ref.shape[0] - used, tile), jnp.float32)


def stages():
    bits = (lax.axis_size("study") - 1).bit_length()
    return [(0, 1)] + [(low, min(2, bits - low)) for low in range(1, bits, 2)]


def pieces_of(block, low, size, me):
    count = 1 << size
    mine = (me >> low) & (count - 1)
    parts = block.reshape(count, block.shape[0] // count, block.shape[1])
    return [lax.dynamic_index_in_dim(parts, mine ^ m, 0, keepdims=False) for m in range(count)]


def total_over_studies(block, place):
    me = lax.axis_index("study")
    for low, size in stages():
        pieces = pieces_of(block, low, size, me)
        come = [exchange(pieces[m], m << low) for m in range(len(pieces) - 1, 0, -1)]
        block = sum(come, pieces[0])
    copies = [send(block, HUB, other) for other in range(lax.axis_size("inner")) if other != HUB]
    block = jnp.where(place == HUB, block, sum(copies))
    for low, size in reversed(stages()):
        pieces = [block] + [None] * ((1 << size) - 1)
        for m in range(len(pieces) - 1, 0, -1):
            pieces[m] = exchange(block, m << low)
        for bit in range(size):
            swap = ((me >> (low + bit)) & 1) == 1
            pieces = [jnp.where(swap, pieces[m ^ (1 << bit)], pieces[m]) for m in range(len(pieces))]
        block = jnp.concatenate(pieces, axis=0)
    return block


def on_device(
    trial_count_per_study,
    study_tile_mask,
    sep_order,
    stacked_study_factor,
    diagonal_block_inverses,
    coupling,
    targets,
    sep_prior,
):
    place = lax.axis_index("inner")
    slots = diagonal_block_inverses.shape[0]
    width = sep_prior.shape[0]
    tile = width // study_tile_mask.shape[1]
    wide = width + targets.shape[1]
    reach = (lax.axis_size("inner") - 1) * slots
    order = sep_order[None, :]
    first, steps = call(
        steps_kernel,
        "steps",
        (floats(slots, slots), floats(slots, reach)),
        [SMEM, HBM, HBM],
        6 * slots * slots * reach,
        [
            pltpu.VMEM((slots, slots), jnp.float32),
            pltpu.VMEM((slots, reach), jnp.float32),
            pltpu.SemaphoreType.DMA((2,)),
        ],
    )(trial_count_per_study, diagonal_block_inverses, stacked_study_factor)
    steps_1 = send(first, 1, HUB)
    steps_3 = send(steps, 3, HUB)
    own = call(own_kernel, "own", floats(slots, wide), [SMEM, SMEM, VMEM, VMEM, VMEM, VMEM, ANY], 6 * slots * slots * wide)(
        trial_count_per_study, study_tile_mask, order, diagonal_block_inverses, coupling, targets, first
    )
    own_1 = send(own, 1, HUB)
    own_0 = send(own, 0, HUB)
    own_3 = send(own, 3, HUB)
    half = jax.ShapeDtypeStruct((reach, reach), jnp.bfloat16)
    high, low, prior = call(chain_kernel, "chain", (half, half, floats(width, width)), [VMEM] * 5, 12 * width**3)(
        order, sep_prior, steps, steps_1, steps_3
    )
    tiles = len(upper_tiles(width, tile))
    unit = 8 * lax.axis_size("study")
    padded = -(-tiles * tile // unit) * unit
    rows = call(
        functools.partial(gram_kernel, tile), "gram", floats(padded, tile), [VMEM] * 6, 12 * reach * width * wide
    )(high, low, own_0, own_1, own, own_3)
    total = total_over_studies(rows, place)
    return call(
        factor_kernel,
        "factor_and_solve",
        (floats(width, width), floats(width, tile)),
        [VMEM, VMEM],
        width**3,
        [pltpu.VMEM((width, wide), jnp.float32), pltpu.VMEM((tile, wide), jnp.float32)],
    )(total, prior)


def solution(mesh):
    return jax.shard_map(
        on_device,
        mesh=mesh,
        in_specs=(
            P("study"),
            P("study", None),
            P(),
            P(("study", "inner"), None),
            P(("study", "inner"), None),
            P(("study", "inner"), None),
            P(("study", "inner"), None),
            P(),
        ),
        out_specs=(P(), P()),
        check_vma=False,
    )
```

```python
import functools

import jax
import jax.numpy as jnp
from jax import lax
from jax.experimental import pallas as pl
from jax.experimental.pallas import tpu as pltpu
from jax.sharding import PartitionSpec as P

HIGHEST = lax.Precision.HIGHEST
HUB = 2
PANEL = 16


NN = (((1,), (0,)), ((), ()))
TN = (((0,), (0,)), ((), ()))
VMEM = pl.BlockSpec(memory_space=pltpu.VMEM)
SMEM = pl.BlockSpec(memory_space=pltpu.SMEM)
ANY = pl.BlockSpec(memory_space=pl.ANY)
HBM = pl.BlockSpec(memory_space=pltpu.HBM)


def call(kernel, name, out_shape, in_specs, flops, scratch_shapes=()):
    many = isinstance(out_shape, tuple)
    return pl.pallas_call(
        kernel,
        out_shape=out_shape,
        in_specs=in_specs,
        out_specs=(VMEM,) * len(out_shape) if many else VMEM,
        scratch_shapes=scratch_shapes,
        cost_estimate=pl.CostEstimate(flops=flops, bytes_accessed=1 << 20, transcendentals=0),
        compiler_params=pltpu.CompilerParams(vmem_limit_bytes=16 << 20),
        name=name,
    )


def floats(*shape):
    return jax.ShapeDtypeStruct(shape, jnp.float32)


def in_hbm(*arrays):
    return [pltpu.with_memory_space_constraint(array, pltpu.HBM) for array in arrays]


def split(x):
    high = x.astype(jnp.bfloat16)
    return high, (x - high.astype(jnp.float32)).astype(jnp.bfloat16)


def product(a, b, dims=NN):
    def one(x, y):
        return lax.dot_general(x, y, dims, preferred_element_type=jnp.float32)

    return one(a[0], b[0]) + (one(a[0], b[1]) + one(a[1], b[0]))


def exchange(block, mask):
    count = lax.axis_size("study")
    return lax.ppermute(block, "study", [(i, i ^ mask) for i in range(count)])


def send(block, source, target):
    return lax.ppermute(block, "inner", [(source, target)])


def upper_tiles(width, tile):
    count = width // tile
    return [(i, j) for i in range(count) for j in range(i, count + 1)]


def outer(a, b):
    return lax.dot_general(a, b, (((0,), (0,)), ((), ())), precision=HIGHEST, preferred_element_type=jnp.float32)


def eliminate(block, lane, tile):
    depth, wide = block.shape
    row = lax.broadcasted_iota(jnp.int32, (depth, 1), 0)
    columns = [jnp.broadcast_to(block[:, lane + k : lane + k + 1], (depth, tile)) for k in range(depth)]
    for i in range(depth):
        scale = lax.rsqrt(columns[i][i : i + 1])
        below = jnp.where(row > i, columns[i], 0.0) * scale
        for k in range(i + 1, depth):
            columns[k] = columns[k] - below * (columns[k][i : i + 1] * scale)
        final = block[i : i + 1] * jnp.tile(scale, (1, wide // tile))
        block = jnp.where(row == i, final, block - jnp.tile(below, (1, wide // tile)) * final)
    return block


def factor_kernel(total_ref, prior_ref, factor_ref, solve_ref, upper_ref, work_ref):
    width = prior_ref.shape[0]
    tile = work_ref.shape[0]
    count = width // tile
    where_tile = {ij: k for k, ij in enumerate(upper_tiles(width, tile))}
    upper = lax.broadcasted_iota(jnp.int32, (tile, tile), 0) <= lax.broadcasted_iota(jnp.int32, (tile, tile), 1)
    for i in range(count):
        rows = slice(i * tile, (i + 1) * tile)
        for j in range(i, count + 1):
            k = where_tile[i, j]
            block = total_ref[k * tile : (k + 1) * tile]
            if j < count:
                block = block + prior_ref[rows, j * tile : (j + 1) * tile]
            work_ref[:, j * tile : (j + 1) * tile] = block
        if i:
            done = slice(0, i * tile)
            work_ref[:, i * tile :] = work_ref[:, i * tile :] - outer(upper_ref[done, rows], upper_ref[done, i * tile :])
        for start in range(0, tile, PANEL):
            stop = start + PANEL
            panel = eliminate(work_ref[start:stop, i * tile :], start, tile)
            upper_ref[i * tile + start : i * tile + stop, i * tile :] = panel
            if stop < tile:
                work_ref[stop:, i * tile :] = work_ref[stop:, i * tile :] - outer(panel[:, :tile], panel)[stop:]
        for j in range(count):
            columns = slice(j * tile, (j + 1) * tile)
            if j < i:
                factor_ref[columns, rows] = jnp.zeros((tile, tile), jnp.float32)
            else:
                block = upper_ref[rows, columns]
                factor_ref[columns, rows] = (jnp.where(upper, block, 0.0) if i == j else block).T
        solve_ref[rows] = upper_ref[rows, width:]


def live_inverse(count_ref, inverse):
    slots = inverse.shape[0]
    place, places = lax.axis_index("inner"), lax.axis_size("inner")

    def live(shape, axis):
        position = lax.broadcasted_iota(jnp.int32, shape, axis) * places + place
        return (position < count_ref[0]).astype(jnp.float32)

    return inverse * live((slots, 1), 0) * live((1, slots), 1)


def picker(order_ref):
    width = order_ref.shape[1]
    return (lax.broadcasted_iota(jnp.int32, (width, width), 0) == order_ref[...]).astype(jnp.float32)


def copy_all(sources, targets, sems):
    copies = [pltpu.make_async_copy(source, target, sems.at[k]) for k, (source, target) in enumerate(zip(sources, targets))]
    for copy in copies:
        copy.start()
    return copies


def local_kernel(*refs):
    count_ref, sources, (own_ref, first_ref, last_ref), targets, sems = refs[0], refs[1:7], refs[7:10], refs[10:16], refs[16]
    mask_ref, order_ref, inverse_ref, coupling_ref, targets_ref, factor_ref = targets
    slots, reach = factor_ref.shape
    width, tile = coupling_ref.shape[1], coupling_ref.shape[1] // mask_ref.shape[1]
    sources = sources[:5] + (sources[5].at[:, :reach],)
    copies = copy_all(sources, targets, sems)
    for copy in copies[:2]:
        copy.wait()
    lane_tile = lax.broadcasted_iota(jnp.int32, (1, width), 1) // tile
    column_mask = jnp.zeros((1, width), jnp.float32)
    for t in range(width // tile):
        column_mask = jnp.where(lane_tile == t, mask_ref[0, t].astype(jnp.float32), column_mask)
    pick = picker(order_ref).astype(jnp.bfloat16)

    def ordered(x):
        return lax.dot_general(x, pick, NN, preferred_element_type=jnp.float32).astype(jnp.bfloat16)

    copies[2].wait()
    inverse = split(live_inverse(count_ref, inverse_ref[...]))
    copies[3].wait()
    high, low = split(coupling_ref[...] * column_mask)
    own = product(inverse, (ordered(high), ordered(low)))
    own_ref[:, :width] = own
    first_ref[:, slots : slots + width] = own
    last_ref[:, reach : reach + width] = own
    copies[4].wait()
    own = product(inverse, split(targets_ref[...]))
    own_ref[:, width:] = own
    first_ref[:, slots + width :] = own
    last_ref[:, reach + width :] = own
    copies[5].wait()
    steps = -product(inverse, split(factor_ref[...]))
    first_ref[:, :slots] = steps[:, :slots]
    last_ref[:, :reach] = steps


def prior_kernel(order_ref, prior_ref, ordered_ref):
    pick = picker(order_ref)
    rows = lax.dot_general(pick, prior_ref[...], TN, precision=HIGHEST, preferred_element_type=jnp.float32)
    ordered_ref[...] = jnp.dot(rows, pick, precision=HIGHEST, preferred_element_type=jnp.float32)


def gram_kernel(tile, last_hbm, own_0_hbm, first_hbm, own_last_ref, prior_ref, rows_ref, own_0_ref, first_ref, last_ref, sems):
    slots, wide = own_0_ref.shape
    copies = copy_all((own_0_hbm, first_hbm, last_hbm), (own_0_ref, first_ref, last_ref), sems)
    copies[0].wait()
    solved = [split(own_0_ref[...])]
    for ref, copy in ((first_ref, copies[1]), (own_last_ref, None), (last_ref, copies[2])):
        if copy is not None:
            copy.wait()
        done = len(solved) * slots
        stack = tuple(jnp.concatenate([x[side] for x in solved], axis=0) for side in range(2))
        step = product(split(ref[:, :done]), stack)
        solved.append(split(ref[:, ref.shape[1] - wide :] + step))
    high, low = (jnp.concatenate([x[side] for x in solved], axis=0) for side in range(2))
    count = wide // tile - 1
    where_tile = {ij: k for k, ij in enumerate(upper_tiles(count * tile, tile))}
    pair = 2
    for first in range(0, count, pair):
        left, right = slice(first * tile, (first + pair) * tile), slice(first * tile, wide)
        block = product((high[:, left], low[:, left]), (high[:, right], low[:, right]), TN)
        for i in range(first, first + pair):
            for j in range(i, count + 1):
                k = where_tile[i, j]
                a, b = (i - first) * tile, (j - first) * tile
                rows_ref[k * tile : (k + 1) * tile] = block[a : a + tile, b : b + tile]
    used = len(where_tile) * tile
    if rows_ref.shape[0] > used:
        rows_ref[used:] = jnp.zeros((rows_ref.shape[0] - used, tile), jnp.float32)


def stages():
    bits = (lax.axis_size("study") - 1).bit_length()
    return [(0, 1)] + [(low, min(2, bits - low)) for low in range(1, bits, 2)]


def pieces_of(block, low, size, me):
    count = 1 << size
    mine = (me >> low) & (count - 1)
    parts = block.reshape(count, block.shape[0] // count, block.shape[1])
    return [lax.dynamic_index_in_dim(parts, mine ^ m, 0, keepdims=False) for m in range(count)]


def total_over_studies(block, place):
    me = lax.axis_index("study")
    for low, size in stages():
        pieces = pieces_of(block, low, size, me)
        come = [exchange(pieces[m], m << low) for m in range(len(pieces) - 1, 0, -1)]
        block = sum(come, pieces[0])
    copies = [send(block, HUB, other) for other in range(lax.axis_size("inner")) if other != HUB]
    block = jnp.where(place == HUB, block, sum(copies))
    for low, size in reversed(stages()):
        pieces = [block] + [None] * ((1 << size) - 1)
        for m in range(len(pieces) - 1, 0, -1):
            pieces[m] = exchange(block, m << low)
        for bit in range(size):
            swap = ((me >> (low + bit)) & 1) == 1
            pieces = [jnp.where(swap, pieces[m ^ (1 << bit)], pieces[m]) for m in range(len(pieces))]
        block = jnp.concatenate(pieces, axis=0)
    return block


def on_device(
    trial_count_per_study,
    study_tile_mask,
    sep_order,
    stacked_study_factor,
    diagonal_block_inverses,
    coupling,
    targets,
    sep_prior,
):
    place = lax.axis_index("inner")
    slots = diagonal_block_inverses.shape[0]
    width = sep_prior.shape[0]
    tile = width // study_tile_mask.shape[1]
    wide = width + targets.shape[1]
    reach = (lax.axis_size("inner") - 1) * slots
    order = sep_order[None, :]
    own, first, last = call(
        local_kernel,
        "local",
        (floats(slots, wide), floats(slots, slots + wide), floats(slots, reach + wide)),
        [SMEM] + [HBM] * 6,
        6 * slots * slots * (reach + wide),
        [
            pltpu.SMEM((1, width // tile), jnp.int32),
            pltpu.VMEM((1, width), jnp.int32),
            pltpu.VMEM((slots, slots), jnp.float32),
            pltpu.VMEM((slots, width), jnp.float32),
            pltpu.VMEM((slots, wide - width), jnp.float32),
            pltpu.VMEM((slots, reach), jnp.float32),
            pltpu.SemaphoreType.DMA((6,)),
        ],
    )(
        trial_count_per_study,
        *in_hbm(
            study_tile_mask,
            order,
            diagonal_block_inverses,
            coupling,
            targets,
            stacked_study_factor,
        ),
    )
    first_1 = send(first, 1, HUB)
    own_0 = send(own, 0, HUB)
    last_3 = send(last, 3, HUB)
    prior = call(prior_kernel, "prior", floats(width, width), [VMEM] * 2, 24 * width**3)(order, sep_prior)
    tiles = len(upper_tiles(width, tile))
    unit = 8 * lax.axis_size("study")
    padded = -(-tiles * tile // unit) * unit
    rows = call(
        functools.partial(gram_kernel, tile),
        "gram",
        floats(padded, tile),
        [HBM] * 3 + [VMEM, ANY],
        12 * reach * width * wide,
        [
            pltpu.VMEM((slots, wide), jnp.float32),
            pltpu.VMEM((slots, slots + wide), jnp.float32),
            pltpu.VMEM((slots, reach + wide), jnp.float32),
            pltpu.SemaphoreType.DMA((3,)),
        ],
    )(*in_hbm(last_3, own_0, first_1), last, prior)
    total = total_over_studies(rows, place)
    return call(
        factor_kernel,
        "factor_and_solve",
        (floats(width, width), floats(width, tile)),
        [VMEM, VMEM],
        width**3,
        [pltpu.VMEM((width, wide), jnp.float32), pltpu.VMEM((tile, wide), jnp.float32)],
    )(total, prior)


def solution(mesh):
    return jax.shard_map(
        on_device,
        mesh=mesh,
        in_specs=(
            P("study"),
            P("study", None),
            P(),
            P(("study", "inner"), None),
            P(("study", "inner"), None),
            P(("study", "inner"), None),
            P(("study", "inner"), None),
            P(),
        ),
        out_specs=(P(), P()),
        check_vma=False,
    )
```

```python
import functools

import jax
import jax.numpy as jnp
from jax import lax
from jax.experimental import pallas as pl
from jax.experimental.pallas import tpu as pltpu
from jax.sharding import PartitionSpec as P

HIGHEST = lax.Precision.HIGHEST
HUB = 2
PANEL = 32
SPREAD = 16


NN = (((1,), (0,)), ((), ()))
TN = (((0,), (0,)), ((), ()))
VMEM = pl.BlockSpec(memory_space=pltpu.VMEM)
SMEM = pl.BlockSpec(memory_space=pltpu.SMEM)
ANY = pl.BlockSpec(memory_space=pl.ANY)
HBM = pl.BlockSpec(memory_space=pltpu.HBM)


def call(kernel, name, out_shape, in_specs, flops, scratch_shapes=()):
    many = isinstance(out_shape, tuple)
    return pl.pallas_call(
        kernel,
        out_shape=out_shape,
        in_specs=in_specs,
        out_specs=(VMEM,) * len(out_shape) if many else VMEM,
        scratch_shapes=scratch_shapes,
        cost_estimate=pl.CostEstimate(flops=flops, bytes_accessed=1 << 20, transcendentals=0),
        compiler_params=pltpu.CompilerParams(vmem_limit_bytes=16 << 20),
        name=name,
    )


def floats(*shape):
    return jax.ShapeDtypeStruct(shape, jnp.float32)


def in_hbm(*arrays):
    return [pltpu.with_memory_space_constraint(array, pltpu.HBM) for array in arrays]


def split(x):
    high = x.astype(jnp.bfloat16)
    return high, (x - high.astype(jnp.float32)).astype(jnp.bfloat16)


def product(a, b, dims=NN):
    def one(x, y):
        return lax.dot_general(x, y, dims, preferred_element_type=jnp.float32)

    return one(a[0], b[0]) + (one(a[0], b[1]) + one(a[1], b[0]))


def exchange(block, mask):
    count = lax.axis_size("study")
    return lax.ppermute(block, "study", [(i, i ^ mask) for i in range(count)])


def send(block, source, target):
    return lax.ppermute(block, "inner", [(source, target)])


def upper_tiles(width, tile):
    count = width // tile
    return [(i, j) for i in range(count) for j in range(i, count + 1)]


def outer(a, b):
    return product(split(a), split(b), TN)


def eliminate(block, lane, tile):
    depth, wide = block.shape
    row = lax.broadcasted_iota(jnp.int32, (8, 1), 0)
    groups = [block[8 * g : 8 * g + 8] for g in range(depth // 8)]
    final = []
    for first in range(0, depth, SPREAD):
        columns = [
            {g: jnp.broadcast_to(groups[g][:, lane + k : lane + k + 1], (8, tile)) for g in range(first // 8, len(groups))}
            for k in range(first, first + SPREAD)
        ]
        for i in range(SPREAD):
            group, line = divmod(first + i, 8)
            scale = lax.rsqrt(columns[i][group][line : line + 1])
            final.append(groups[group][line : line + 1] * jnp.tile(scale, (1, wide // tile)))
            below = {g: columns[i][g] * scale for g in range(group, len(groups))}
            below[group] = jnp.where(row > line, below[group], 0.0)
            if line == 7:
                del below[group]
            for k in range(i + 1, SPREAD):
                factor = columns[k][group][line : line + 1] * scale
                for g in below:
                    columns[k][g] = columns[k][g] - below[g] * factor
            for g in below:
                groups[g] = groups[g] - jnp.tile(below[g], (1, wide // tile)) * final[-1]
    return jnp.concatenate(final, axis=0)


def factor_kernel(total_ref, prior_ref, factor_ref, solve_ref, upper_ref, work_ref):
    width = prior_ref.shape[0]
    tile = work_ref.shape[0]
    count = width // tile
    where_tile = {ij: k for k, ij in enumerate(upper_tiles(width, tile))}
    upper = lax.broadcasted_iota(jnp.int32, (tile, tile), 0) <= lax.broadcasted_iota(jnp.int32, (tile, tile), 1)
    for i in range(count):
        rows = slice(i * tile, (i + 1) * tile)
        for j in range(i, count + 1):
            k = where_tile[i, j]
            block = total_ref[k * tile : (k + 1) * tile]
            if j < count:
                block = block + prior_ref[rows, j * tile : (j + 1) * tile]
            work_ref[:, j * tile : (j + 1) * tile] = block
        if i:
            done = slice(0, i * tile)
            work_ref[:, i * tile :] = work_ref[:, i * tile :] - outer(upper_ref[done, rows], upper_ref[done, i * tile :])
        ready = work_ref[:PANEL, i * tile :]
        for start in range(0, tile, PANEL):
            stop = start + PANEL
            panel = eliminate(ready, start, tile)
            upper_ref[i * tile + start : i * tile + stop, i * tile :] = panel
            if stop < tile:
                ready = work_ref[stop : stop + PANEL, i * tile :] - outer(panel[:, stop : stop + PANEL], panel)
            if stop + PANEL < tile:
                rest = slice(stop + PANEL, tile)
                work_ref[rest, i * tile :] = work_ref[rest, i * tile :] - outer(panel[:, rest], panel)
        for j in range(count):
            columns = slice(j * tile, (j + 1) * tile)
            if j < i:
                factor_ref[columns, rows] = jnp.zeros((tile, tile), jnp.float32)
            else:
                block = upper_ref[rows, columns]
                factor_ref[columns, rows] = (jnp.where(upper, block, 0.0) if i == j else block).T
        solve_ref[rows] = upper_ref[rows, width:]


def live_inverse(count_ref, inverse):
    slots = inverse.shape[0]
    place, places = lax.axis_index("inner"), lax.axis_size("inner")

    def live(shape, axis):
        position = lax.broadcasted_iota(jnp.int32, shape, axis) * places + place
        return (position < count_ref[0]).astype(jnp.float32)

    return inverse * live((slots, 1), 0) * live((1, slots), 1)


def picker(order_ref):
    width = order_ref.shape[1]
    return (lax.broadcasted_iota(jnp.int32, (width, width), 0) == order_ref[...]).astype(jnp.float32)


def copy_all(sources, targets, sems):
    copies = [pltpu.make_async_copy(source, target, sems.at[k]) for k, (source, target) in enumerate(zip(sources, targets))]
    for copy in copies:
        copy.start()
    return copies


def local_kernel(*refs):
    count_ref, sources, (own_ref, first_ref, rest_ref, last_ref), targets, sems = refs[0], refs[1:7], refs[7:11], refs[11:17], refs[17]
    mask_ref, order_ref, inverse_ref, coupling_ref, targets_ref, factor_ref = targets
    slots, reach = factor_ref.shape
    width, tile = coupling_ref.shape[1], coupling_ref.shape[1] // mask_ref.shape[1]
    sources = sources[:5] + (sources[5].at[:, :reach],)
    copies = copy_all(sources, targets, sems)
    for copy in copies[:2]:
        copy.wait()
    lane_tile = lax.broadcasted_iota(jnp.int32, (1, width), 1) // tile
    column_mask = jnp.zeros((1, width), jnp.float32)
    for t in range(width // tile):
        column_mask = jnp.where(lane_tile == t, mask_ref[0, t].astype(jnp.float32), column_mask)
    pick = picker(order_ref).astype(jnp.bfloat16)

    def ordered(x):
        return lax.dot_general(x, pick, NN, preferred_element_type=jnp.float32).astype(jnp.bfloat16)

    copies[2].wait()
    inverse = split(live_inverse(count_ref, inverse_ref[...]))
    copies[3].wait()
    high, low = split(coupling_ref[...] * column_mask)
    left = first_ref.shape[1] - slots
    own = product(inverse, (ordered(high), ordered(low)))
    own_ref[:, :width] = own
    first_ref[:, slots:] = own[:, :left]
    rest_ref[:, : width - left] = own[:, left:]
    last_ref[:, reach : reach + width] = own
    copies[4].wait()
    own = product(inverse, split(targets_ref[...]))
    own_ref[:, width:] = own
    rest_ref[:, width - left :] = own
    last_ref[:, reach + width :] = own
    copies[5].wait()
    steps = -product(inverse, split(factor_ref[...]))
    first_ref[:, :slots] = steps[:, :slots]
    last_ref[:, :reach] = steps


def prior_kernel(order_ref, prior_ref, ordered_ref):
    pick = picker(order_ref)
    rows = lax.dot_general(pick, prior_ref[...], TN, precision=HIGHEST, preferred_element_type=jnp.float32)
    ordered_ref[...] = jnp.dot(rows, pick, precision=HIGHEST, preferred_element_type=jnp.float32)


def put_tiles(block, top, side, rows_ref, tile, count, add_ref=None):
    where_tile = {ij: k for k, ij in enumerate(upper_tiles(count * tile, tile))}
    for i in range(top, top + block.shape[0] // tile):
        for j in range(max(i, side), side + block.shape[1] // tile):
            rows = slice(where_tile[i, j] * tile, (where_tile[i, j] + 1) * tile)
            a, b = (i - top) * tile, (j - side) * tile
            piece = block[a : a + tile, b : b + tile]
            rows_ref[rows] = piece if add_ref is None else piece + add_ref[rows]


def stack(pairs):
    return tuple(jnp.concatenate([pair[side] for pair in pairs], axis=0) for side in range(2))


def columns(pair, start, stop):
    return pair[0][:, start:stop], pair[1][:, start:stop]


def early_kernel(tile, left, last_hbm, own_0_hbm, first_hbm, own_last_ref, prior_ref, *refs):
    high_ref, low_ref, base_ref, chain_high_ref, chain_low_ref, rows_ref = refs[:6]
    targets, sems = refs[6:9], refs[9]
    last_ref, own_0_ref, first_ref = targets
    slots, wide = own_0_ref.shape
    count = wide // tile - 1
    copies = copy_all((last_hbm, own_0_hbm, first_hbm), targets, sems)
    cut = [slice(k * slots, (k + 1) * slots) for k in range(3)]
    for copy in copies[1:]:
        copy.wait()
    solved_0 = split(own_0_ref[...])
    part_1 = product(split(first_ref[:, :slots]), solved_0)
    part_1 = jnp.concatenate([part_1[:, :left] + first_ref[:, slots:], part_1[:, left:]], axis=1)
    known = stack([solved_0, split(part_1)])
    step_21 = split(own_last_ref[:, cut[1]])
    part_2 = own_last_ref[:, own_last_ref.shape[1] - wide :] + product(split(own_last_ref[:, : 2 * slots]), known)
    copies[0].wait()
    known = stack([known, split(part_2)])
    reach = last_ref.shape[1] - wide
    part_3 = last_ref[:, reach:] + product(split(last_ref[:, :reach]), known)
    known = stack([known, split(part_3)])
    chain_high_ref[:slots], chain_low_ref[:slots] = step_21
    chain_high_ref[slots:], chain_low_ref[slots:] = split(last_ref[:, cut[1]] + product(split(last_ref[:, cut[2]]), step_21))
    for k, part in enumerate((part_1, part_2, part_3)):
        base_ref[k * slots : (k + 1) * slots] = part[:, left:]
    high_ref[...], low_ref[...] = known[0][slots:, :left], known[1][slots:, :left]
    at = left // tile
    put_tiles(product(columns(known, 0, left), columns(known, 0, left), TN), 0, 0, rows_ref, tile, count)
    put_tiles(product(columns(solved_0, 0, left), columns(solved_0, left, wide), TN), 0, at, rows_ref, tile, count)
    put_tiles(product(columns(solved_0, left, count * tile), columns(solved_0, left, wide), TN), at, at, rows_ref, tile, count)


def gram_kernel(tile, rest_ref, high_ref, low_ref, base_ref, chain_high_ref, chain_low_ref, early_ref, rows_ref):
    slots, wide = rest_ref.shape
    left = high_ref.shape[1]
    count = (left + wide) // tile - 1
    at = left // tile
    rest = rest_ref[...]
    step = product((chain_high_ref[...], chain_low_ref[...]), split(rest))
    right = split(base_ref[...] + jnp.concatenate([rest, step], axis=0))
    put_tiles(product((high_ref[...], low_ref[...]), right, TN), 0, at, rows_ref, tile, count, early_ref)
    put_tiles(product(columns(right, 0, count * tile - left), right, TN), at, at, rows_ref, tile, count, early_ref)
    where_tile = {ij: k for k, ij in enumerate(upper_tiles(count * tile, tile))}
    for i in range(at):
        for j in range(i, at):
            rows = slice(where_tile[i, j] * tile, (where_tile[i, j] + 1) * tile)
            rows_ref[rows] = early_ref[rows]
    used = early_ref.shape[0]
    if rows_ref.shape[0] > used:
        rows_ref[used:] = jnp.zeros((rows_ref.shape[0] - used, tile), jnp.float32)


def stages():
    bits = (lax.axis_size("study") - 1).bit_length()
    return [(0, 1)] + [(low, min(2, bits - low)) for low in range(1, bits, 2)]


def pieces_of(block, low, size, me):
    count = 1 << size
    mine = (me >> low) & (count - 1)
    parts = block.reshape(count, block.shape[0] // count, block.shape[1])
    return [lax.dynamic_index_in_dim(parts, mine ^ m, 0, keepdims=False) for m in range(count)]


def total_over_studies(block, place):
    me = lax.axis_index("study")
    for low, size in stages():
        pieces = pieces_of(block, low, size, me)
        come = [exchange(pieces[m], m << low) for m in range(len(pieces) - 1, 0, -1)]
        block = sum(come, pieces[0])
    copies = [send(block, HUB, other) for other in range(lax.axis_size("inner")) if other != HUB]
    block = jnp.where(place == HUB, block, sum(copies))
    for low, size in reversed(stages()):
        pieces = [block] + [None] * ((1 << size) - 1)
        for m in range(len(pieces) - 1, 0, -1):
            pieces[m] = exchange(block, m << low)
        for bit in range(size):
            swap = ((me >> (low + bit)) & 1) == 1
            pieces = [jnp.where(swap, pieces[m ^ (1 << bit)], pieces[m]) for m in range(len(pieces))]
        block = jnp.concatenate(pieces, axis=0)
    return block


def on_device(
    trial_count_per_study,
    study_tile_mask,
    sep_order,
    stacked_study_factor,
    diagonal_block_inverses,
    coupling,
    targets,
    sep_prior,
):
    place = lax.axis_index("inner")
    slots = diagonal_block_inverses.shape[0]
    width = sep_prior.shape[0]
    tile = width // study_tile_mask.shape[1]
    wide = width + targets.shape[1]
    reach = (lax.axis_size("inner") - 1) * slots
    order = sep_order[None, :]
    left = (width // tile + 1) // 2 * tile
    own, first, rest, last = call(
        local_kernel,
        "local",
        (floats(slots, wide), floats(slots, slots + left), floats(slots, wide - left), floats(slots, reach + wide)),
        [SMEM] + [HBM] * 6,
        6 * slots * slots * (reach + wide),
        [
            pltpu.SMEM((1, width // tile), jnp.int32),
            pltpu.VMEM((1, width), jnp.int32),
            pltpu.VMEM((slots, slots), jnp.float32),
            pltpu.VMEM((slots, width), jnp.float32),
            pltpu.VMEM((slots, wide - width), jnp.float32),
            pltpu.VMEM((slots, reach), jnp.float32),
            pltpu.SemaphoreType.DMA((6,)),
        ],
    )(
        trial_count_per_study,
        *in_hbm(
            study_tile_mask,
            order,
            diagonal_block_inverses,
            coupling,
            targets,
            stacked_study_factor,
        ),
    )
    first_1 = send(first, 1, HUB)
    own_0 = send(own, 0, HUB)
    rest_1 = send(rest, 1, HUB)
    last_3 = send(last, 3, HUB)
    prior = call(prior_kernel, "prior", floats(width, width), [VMEM] * 2, 24 * width**3)(order, sep_prior)
    tiles = len(upper_tiles(width, tile))

    def halves(*shape):
        return jax.ShapeDtypeStruct(shape, jnp.bfloat16)

    early = call(
        functools.partial(early_kernel, tile, left),
        "early",
        (
            halves(reach, left),
            halves(reach, left),
            floats(reach, wide - left),
            halves(2 * slots, slots),
            halves(2 * slots, slots),
            floats(tiles * tile, tile),
        ),
        [HBM] * 3 + [VMEM, ANY],
        6 * slots * wide * (6 * slots + width),
        [
            pltpu.VMEM((slots, reach + wide), jnp.float32),
            pltpu.VMEM((slots, wide), jnp.float32),
            pltpu.VMEM((slots, slots + left), jnp.float32),
            pltpu.SemaphoreType.DMA((3,)),
        ],
    )(*in_hbm(last_3, own_0, first_1), last, prior)
    unit = 8 * lax.axis_size("study")
    padded = -(-tiles * tile // unit) * unit
    rows = call(
        functools.partial(gram_kernel, tile),
        "gram",
        floats(padded, tile),
        [VMEM] * 7,
        6 * slots * wide * (2 * slots + 3 * width),
    )(rest_1, *early)
    total = total_over_studies(rows, place)
    return call(
        factor_kernel,
        "factor_and_solve",
        (floats(width, width), floats(width, tile)),
        [VMEM, VMEM],
        width**3,
        [pltpu.VMEM((width, wide), jnp.float32), pltpu.VMEM((tile, wide), jnp.float32)],
    )(total, prior)


def solution(mesh):
    return jax.shard_map(
        on_device,
        mesh=mesh,
        in_specs=(
            P("study"),
            P("study", None),
            P(),
            P(("study", "inner"), None),
            P(("study", "inner"), None),
            P(("study", "inner"), None),
            P(("study", "inner"), None),
            P(),
        ),
        out_specs=(P(), P()),
        check_vma=False,
    )
```

```python
import functools

import jax
import jax.numpy as jnp
from jax import lax
from jax.experimental import pallas as pl
from jax.experimental.pallas import tpu as pltpu
from jax.sharding import PartitionSpec as P

HIGHEST = lax.Precision.HIGHEST
HUB = 2
PANEL = 32
SPREAD = 16


NN = (((1,), (0,)), ((), ()))
TN = (((0,), (0,)), ((), ()))
VMEM = pl.BlockSpec(memory_space=pltpu.VMEM)
SMEM = pl.BlockSpec(memory_space=pltpu.SMEM)
ANY = pl.BlockSpec(memory_space=pl.ANY)
HBM = pl.BlockSpec(memory_space=pltpu.HBM)


def call(kernel, name, out_shape, in_specs, flops, scratch_shapes=()):
    many = isinstance(out_shape, tuple)
    return pl.pallas_call(
        kernel,
        out_shape=out_shape,
        in_specs=in_specs,
        out_specs=(VMEM,) * len(out_shape) if many else VMEM,
        scratch_shapes=scratch_shapes,
        cost_estimate=pl.CostEstimate(flops=flops, bytes_accessed=1 << 20, transcendentals=0),
        compiler_params=pltpu.CompilerParams(vmem_limit_bytes=16 << 20),
        name=name,
    )


def floats(*shape):
    return jax.ShapeDtypeStruct(shape, jnp.float32)


def in_hbm(*arrays):
    return [pltpu.with_memory_space_constraint(array, pltpu.HBM) for array in arrays]


def split(x):
    high = x.astype(jnp.bfloat16)
    return high, (x - high.astype(jnp.float32)).astype(jnp.bfloat16)


def product(a, b, dims=NN):
    def one(x, y):
        return lax.dot_general(x, y, dims, preferred_element_type=jnp.float32)

    return one(a[0], b[0]) + (one(a[0], b[1]) + one(a[1], b[0]))


def exchange(block, mask):
    count = lax.axis_size("study")
    return lax.ppermute(block, "study", [(i, i ^ mask) for i in range(count)])


def send(block, source, target):
    return lax.ppermute(block, "inner", [(source, target)])


def upper_tiles(width, tile):
    count = width // tile
    return [(i, j) for i in range(count) for j in range(i, count + 1)]


def outer(a, b):
    return product(split(a), split(b), TN)


def eliminate(block, lane, tile):
    depth, wide = block.shape
    row = lax.broadcasted_iota(jnp.int32, (8, 1), 0)
    groups = [block[8 * g : 8 * g + 8] for g in range(depth // 8)]
    final = []
    for first in range(0, depth, SPREAD):
        columns = [
            {g: jnp.broadcast_to(groups[g][:, lane + k : lane + k + 1], (8, tile)) for g in range(first // 8, len(groups))}
            for k in range(first, first + SPREAD)
        ]
        for i in range(SPREAD):
            group, line = divmod(first + i, 8)
            scale = lax.rsqrt(columns[i][group][line : line + 1])
            final.append(groups[group][line : line + 1] * jnp.tile(scale, (1, wide // tile)))
            below = {g: columns[i][g] * scale for g in range(group, len(groups))}
            below[group] = jnp.where(row > line, below[group], 0.0)
            if line == 7:
                del below[group]
            for k in range(i + 1, SPREAD):
                factor = columns[k][group][line : line + 1] * scale
                for g in below:
                    columns[k][g] = columns[k][g] - below[g] * factor
            for g in below:
                groups[g] = groups[g] - jnp.tile(below[g], (1, wide // tile)) * final[-1]
    return jnp.concatenate(final, axis=0)


def factor_kernel(total_ref, prior_ref, factor_ref, solve_ref, upper_ref, work_ref):
    width = prior_ref.shape[0]
    tile = work_ref.shape[0]
    count = width // tile
    where_tile = {ij: k for k, ij in enumerate(upper_tiles(width, tile))}
    upper = lax.broadcasted_iota(jnp.int32, (tile, tile), 0) <= lax.broadcasted_iota(jnp.int32, (tile, tile), 1)
    for i in range(count):
        rows = slice(i * tile, (i + 1) * tile)
        for j in range(i, count + 1):
            k = where_tile[i, j]
            block = total_ref[k * tile : (k + 1) * tile]
            if j < count:
                block = block + prior_ref[rows, j * tile : (j + 1) * tile]
            work_ref[:, j * tile : (j + 1) * tile] = block
        if i:
            done = slice(0, i * tile)
            work_ref[:, i * tile :] = work_ref[:, i * tile :] - outer(upper_ref[done, rows], upper_ref[done, i * tile :])
        ready = work_ref[:PANEL, i * tile :]
        for start in range(0, tile, PANEL):
            stop = start + PANEL
            panel = eliminate(ready, start, tile)
            upper_ref[i * tile + start : i * tile + stop, i * tile :] = panel
            if stop < tile:
                ready = work_ref[stop : stop + PANEL, i * tile :] - outer(panel[:, stop : stop + PANEL], panel)
            if stop + PANEL < tile:
                rest = slice(stop + PANEL, tile)
                work_ref[rest, i * tile :] = work_ref[rest, i * tile :] - outer(panel[:, rest], panel)
        for j in range(count):
            columns = slice(j * tile, (j + 1) * tile)
            if j < i:
                factor_ref[columns, rows] = jnp.zeros((tile, tile), jnp.float32)
            else:
                block = upper_ref[rows, columns]
                factor_ref[columns, rows] = (jnp.where(upper, block, 0.0) if i == j else block).T
        solve_ref[rows] = upper_ref[rows, width:]


def live_inverse(count_ref, inverse):
    slots = inverse.shape[0]
    place, places = lax.axis_index("inner"), lax.axis_size("inner")

    def live(shape, axis):
        position = lax.broadcasted_iota(jnp.int32, shape, axis) * places + place
        return (position < count_ref[0]).astype(jnp.float32)

    return inverse * live((slots, 1), 0) * live((1, slots), 1)


def picker(order_ref):
    width = order_ref.shape[1]
    return (lax.broadcasted_iota(jnp.int32, (width, width), 0) == order_ref[...]).astype(jnp.float32)


def copy_all(sources, targets, sems):
    copies = [pltpu.make_async_copy(source, target, sems.at[k]) for k, (source, target) in enumerate(zip(sources, targets))]
    for copy in copies:
        copy.start()
    return copies


def local_kernel(*refs):
    count_ref, sources, (own_ref, first_ref, rest_ref, last_ref), targets, sems = refs[0], refs[1:7], refs[7:11], refs[11:17], refs[17]
    mask_ref, order_ref, inverse_ref, coupling_ref, targets_ref, factor_ref = targets
    slots, reach = factor_ref.shape
    width, tile = coupling_ref.shape[1], coupling_ref.shape[1] // mask_ref.shape[1]
    sources = sources[:5] + (sources[5].at[:, :reach],)
    copies = copy_all(sources, targets, sems)
    for copy in copies[:2]:
        copy.wait()
    lane_tile = lax.broadcasted_iota(jnp.int32, (1, width), 1) // tile
    column_mask = jnp.zeros((1, width), jnp.float32)
    for t in range(width // tile):
        column_mask = jnp.where(lane_tile == t, mask_ref[0, t].astype(jnp.float32), column_mask)
    pick = picker(order_ref).astype(jnp.bfloat16)

    def ordered(x):
        return lax.dot_general(x, pick, NN, preferred_element_type=jnp.float32).astype(jnp.bfloat16)

    copies[2].wait()
    inverse = split(live_inverse(count_ref, inverse_ref[...]))
    copies[3].wait()
    high, low = split(coupling_ref[...] * column_mask)
    left = first_ref.shape[1] - slots
    own = product(inverse, (ordered(high), ordered(low)))
    own_ref[:, :width] = own
    first_ref[:, slots:] = own[:, :left]
    rest_ref[:, : width - left] = own[:, left:]
    last_ref[:, reach:] = own[:, :left]
    copies[4].wait()
    own = product(inverse, split(targets_ref[...]))
    own_ref[:, width:] = own
    rest_ref[:, width - left :] = own
    copies[5].wait()
    steps = -product(inverse, split(factor_ref[...]))
    first_ref[:, :slots] = steps[:, :slots]
    last_ref[:, :reach] = steps


def prior_kernel(order_ref, prior_ref, ordered_ref):
    pick = picker(order_ref)
    rows = lax.dot_general(pick, prior_ref[...], TN, precision=HIGHEST, preferred_element_type=jnp.float32)
    ordered_ref[...] = jnp.dot(rows, pick, precision=HIGHEST, preferred_element_type=jnp.float32)


def put_tiles(block, top, side, rows_ref, tile, count, add_ref=None):
    where_tile = {ij: k for k, ij in enumerate(upper_tiles(count * tile, tile))}
    for i in range(top, top + block.shape[0] // tile):
        for j in range(max(i, side), side + block.shape[1] // tile):
            rows = slice(where_tile[i, j] * tile, (where_tile[i, j] + 1) * tile)
            a, b = (i - top) * tile, (j - side) * tile
            piece = block[a : a + tile, b : b + tile]
            rows_ref[rows] = piece if add_ref is None else piece + add_ref[rows]


def stack(pairs):
    return tuple(jnp.concatenate([pair[side] for pair in pairs], axis=0) for side in range(2))


def columns(pair, start, stop):
    return pair[0][:, start:stop], pair[1][:, start:stop]


def early_kernel(tile, last_hbm, own_0_hbm, first_hbm, own_last_ref, own_rest_ref, prior_ref, *refs):
    high_ref, low_ref, base_ref, chain_high_ref, chain_low_ref, rows_ref = refs[:6]
    targets, sems = refs[6:9], refs[9]
    last_ref, own_0_ref, first_ref = targets
    slots, wide = own_0_ref.shape
    left = first_ref.shape[1] - slots
    reach = last_ref.shape[1] - left
    count = wide // tile - 1
    copies = copy_all((last_hbm, own_0_hbm, first_hbm), targets, sems)
    cut = [slice(k * slots, (k + 1) * slots) for k in range(3)]
    for copy in copies[1:]:
        copy.wait()
    solved_0 = split(own_0_ref[...])
    part_1 = product(split(first_ref[:, :slots]), solved_0)
    part_1 = jnp.concatenate([part_1[:, :left] + first_ref[:, slots:], part_1[:, left:]], axis=1)
    known = stack([solved_0, split(part_1)])
    step_21 = split(own_last_ref[:, cut[1]])
    part_2 = jnp.concatenate([own_last_ref[:, reach:], own_rest_ref[...]], axis=1)
    part_2 = part_2 + product(split(own_last_ref[:, : 2 * slots]), known)
    copies[0].wait()
    known = stack([known, split(part_2)])
    part_3 = product(split(last_ref[:, :reach]), known)
    part_3 = jnp.concatenate([part_3[:, :left] + last_ref[:, reach:], part_3[:, left:]], axis=1)
    known = stack([known, split(part_3)])
    chain_high_ref[:slots], chain_low_ref[:slots] = step_21
    chain_high_ref[slots:], chain_low_ref[slots:] = split(last_ref[:, cut[1]] + product(split(last_ref[:, cut[2]]), step_21))
    for k, part in enumerate((part_1, part_2, part_3)):
        base_ref[k * slots : (k + 1) * slots] = part[:, left:]
    high_ref[...], low_ref[...] = known[0][slots:, :left], known[1][slots:, :left]
    at = left // tile
    put_tiles(product(columns(known, 0, left), columns(known, 0, left), TN), 0, 0, rows_ref, tile, count)
    put_tiles(product(columns(solved_0, 0, left), columns(solved_0, left, wide), TN), 0, at, rows_ref, tile, count)
    put_tiles(product(columns(solved_0, left, count * tile), columns(solved_0, left, wide), TN), at, at, rows_ref, tile, count)


def gram_kernel(tile, rest_ref, rest_3_ref, high_ref, low_ref, base_ref, chain_high_ref, chain_low_ref, early_ref, rows_ref):
    slots, wide = rest_ref.shape
    left = high_ref.shape[1]
    count = (left + wide) // tile - 1
    at = left // tile
    rest = rest_ref[...]
    step = product((chain_high_ref[...], chain_low_ref[...]), split(rest))
    right = jnp.concatenate([rest, step[:slots], step[slots:] + rest_3_ref[...]], axis=0)
    right = split(base_ref[...] + right)
    put_tiles(product((high_ref[...], low_ref[...]), right, TN), 0, at, rows_ref, tile, count, early_ref)
    put_tiles(product(columns(right, 0, count * tile - left), right, TN), at, at, rows_ref, tile, count, early_ref)
    where_tile = {ij: k for k, ij in enumerate(upper_tiles(count * tile, tile))}
    for i in range(at):
        for j in range(i, at):
            rows = slice(where_tile[i, j] * tile, (where_tile[i, j] + 1) * tile)
            rows_ref[rows] = early_ref[rows]
    used = early_ref.shape[0]
    if rows_ref.shape[0] > used:
        rows_ref[used:] = jnp.zeros((rows_ref.shape[0] - used, tile), jnp.float32)


def stages():
    bits = (lax.axis_size("study") - 1).bit_length()
    return [(0, 1)] + [(low, min(2, bits - low)) for low in range(1, bits, 2)]


def pieces_of(block, low, size, me):
    count = 1 << size
    mine = (me >> low) & (count - 1)
    parts = block.reshape(count, block.shape[0] // count, block.shape[1])
    return [lax.dynamic_index_in_dim(parts, mine ^ m, 0, keepdims=False) for m in range(count)]


def total_over_studies(block, place):
    me = lax.axis_index("study")
    for low, size in stages():
        pieces = pieces_of(block, low, size, me)
        come = [exchange(pieces[m], m << low) for m in range(len(pieces) - 1, 0, -1)]
        block = sum(come, pieces[0])
    copies = [send(block, HUB, other) for other in range(lax.axis_size("inner")) if other != HUB]
    block = jnp.where(place == HUB, block, sum(copies))
    for low, size in reversed(stages()):
        pieces = [block] + [None] * ((1 << size) - 1)
        for m in range(len(pieces) - 1, 0, -1):
            pieces[m] = exchange(block, m << low)
        for bit in range(size):
            swap = ((me >> (low + bit)) & 1) == 1
            pieces = [jnp.where(swap, pieces[m ^ (1 << bit)], pieces[m]) for m in range(len(pieces))]
        block = jnp.concatenate(pieces, axis=0)
    return block


def on_device(
    trial_count_per_study,
    study_tile_mask,
    sep_order,
    stacked_study_factor,
    diagonal_block_inverses,
    coupling,
    targets,
    sep_prior,
):
    place = lax.axis_index("inner")
    slots = diagonal_block_inverses.shape[0]
    width = sep_prior.shape[0]
    tile = width // study_tile_mask.shape[1]
    wide = width + targets.shape[1]
    reach = (lax.axis_size("inner") - 1) * slots
    order = sep_order[None, :]
    left = (width // tile + 1) // 2 * tile
    own, first, rest, last = call(
        local_kernel,
        "local",
        (floats(slots, wide), floats(slots, slots + left), floats(slots, wide - left), floats(slots, reach + left)),
        [SMEM] + [HBM] * 6,
        6 * slots * slots * (reach + wide),
        [
            pltpu.SMEM((1, width // tile), jnp.int32),
            pltpu.VMEM((1, width), jnp.int32),
            pltpu.VMEM((slots, slots), jnp.float32),
            pltpu.VMEM((slots, width), jnp.float32),
            pltpu.VMEM((slots, wide - width), jnp.float32),
            pltpu.VMEM((slots, reach), jnp.float32),
            pltpu.SemaphoreType.DMA((6,)),
        ],
    )(
        trial_count_per_study,
        *in_hbm(
            study_tile_mask,
            order,
            diagonal_block_inverses,
            coupling,
            targets,
            stacked_study_factor,
        ),
    )
    first_1 = send(first, 1, HUB)
    own_0 = send(own, 0, HUB)
    rest_1 = send(rest, 1, HUB)
    last_3 = send(last, 3, HUB)
    rest_3 = send(rest, 3, HUB)
    prior = call(prior_kernel, "prior", floats(width, width), [VMEM] * 2, 24 * width**3)(order, sep_prior)
    tiles = len(upper_tiles(width, tile))

    def halves(*shape):
        return jax.ShapeDtypeStruct(shape, jnp.bfloat16)

    early = call(
        functools.partial(early_kernel, tile),
        "early",
        (
            halves(reach, left),
            halves(reach, left),
            floats(reach, wide - left),
            halves(2 * slots, slots),
            halves(2 * slots, slots),
            floats(tiles * tile, tile),
        ),
        [HBM] * 3 + [VMEM, VMEM, ANY],
        6 * slots * wide * (6 * slots + width),
        [
            pltpu.VMEM((slots, reach + left), jnp.float32),
            pltpu.VMEM((slots, wide), jnp.float32),
            pltpu.VMEM((slots, slots + left), jnp.float32),
            pltpu.SemaphoreType.DMA((3,)),
        ],
    )(*in_hbm(last_3, own_0, first_1), last, rest, prior)
    unit = 8 * lax.axis_size("study")
    padded = -(-tiles * tile // unit) * unit
    rows = call(
        functools.partial(gram_kernel, tile),
        "gram",
        floats(padded, tile),
        [VMEM] * 8,
        6 * slots * wide * (2 * slots + 3 * width),
    )(rest_1, rest_3, *early)
    total = total_over_studies(rows, place)
    return call(
        factor_kernel,
        "factor_and_solve",
        (floats(width, width), floats(width, tile)),
        [VMEM, VMEM],
        width**3,
        [pltpu.VMEM((width, wide), jnp.float32), pltpu.VMEM((tile, wide), jnp.float32)],
    )(total, prior)


def solution(mesh):
    return jax.shard_map(
        on_device,
        mesh=mesh,
        in_specs=(
            P("study"),
            P("study", None),
            P(),
            P(("study", "inner"), None),
            P(("study", "inner"), None),
            P(("study", "inner"), None),
            P(("study", "inner"), None),
            P(),
        ),
        out_specs=(P(), P()),
        check_vma=False,
    )
```

```python
import functools

import jax
import jax.numpy as jnp
from jax import lax
from jax.experimental import pallas as pl
from jax.experimental.pallas import tpu as pltpu
from jax.sharding import PartitionSpec as P

HIGHEST = lax.Precision.HIGHEST
HUB = 2
SPREAD = 16


NN = (((1,), (0,)), ((), ()))
TN = (((0,), (0,)), ((), ()))
VMEM = pl.BlockSpec(memory_space=pltpu.VMEM)
SMEM = pl.BlockSpec(memory_space=pltpu.SMEM)
ANY = pl.BlockSpec(memory_space=pl.ANY)
HBM = pl.BlockSpec(memory_space=pltpu.HBM)


def call(kernel, name, out_shape, in_specs, flops, scratch_shapes=(), out_spec=VMEM):
    many = isinstance(out_shape, tuple)
    return pl.pallas_call(
        kernel,
        out_shape=out_shape,
        in_specs=in_specs,
        out_specs=(out_spec,) * len(out_shape) if many else out_spec,
        scratch_shapes=scratch_shapes,
        cost_estimate=pl.CostEstimate(flops=flops, bytes_accessed=1 << 20, transcendentals=0),
        compiler_params=pltpu.CompilerParams(vmem_limit_bytes=16 << 20),
        name=name,
    )


def floats(*shape):
    return jax.ShapeDtypeStruct(shape, jnp.float32)


def in_hbm(*arrays):
    return [pltpu.with_memory_space_constraint(array, pltpu.HBM) for array in arrays]


def split(x):
    high = x.astype(jnp.bfloat16)
    return high, (x - high.astype(jnp.float32)).astype(jnp.bfloat16)


def product(a, b, dims=NN):
    def one(x, y):
        return lax.dot_general(x, y, dims, preferred_element_type=jnp.float32)

    return one(a[0], b[0]) + (one(a[0], b[1]) + one(a[1], b[0]))


def exchange(block, mask):
    count = lax.axis_size("study")
    return lax.ppermute(block, "study", [(i, i ^ mask) for i in range(count)])


def send(block, source, target):
    return lax.ppermute(block, "inner", [(source, target)])


def upper_tiles(width, tile):
    count = width // tile
    return [(i, j) for i in range(count) for j in range(i, count + 1)]


def eliminate(block, behind, lane, tile):
    wide = block.shape[1]
    row = lax.broadcasted_iota(jnp.int32, (8, 1), 0)
    groups = [rows[8 * g : 8 * g + 8] for rows in (block, behind) if rows is not None for g in range(SPREAD // 8)]
    spread = [[jnp.broadcast_to(rows[:, lane + k : lane + k + 1], (8, tile)) for rows in groups] for k in range(SPREAD)]
    final = []
    for i in range(SPREAD):
        group, line = divmod(i, 8)
        scale = lax.rsqrt(spread[i][group][line : line + 1])
        final.append(groups[group][line : line + 1] * jnp.tile(scale, (1, wide // tile)))
        below = {g: spread[i][g] * scale for g in range(group, len(groups))}
        below[group] = jnp.where(row > line, below[group], 0.0)
        if line == 7:
            del below[group]
        for k in range(i + 1, SPREAD):
            factor = spread[k][group][line : line + 1] * scale
            for g in below:
                spread[k][g] = spread[k][g] - below[g] * factor
        for g in below:
            groups[g] = groups[g] - jnp.tile(below[g], (1, wide // tile)) * final[-1]
    final = jnp.concatenate(final, axis=0)
    return final, None if behind is None else jnp.concatenate(groups[SPREAD // 8 :], axis=0)


def factor_kernel(total_ref, prior_ref, factor_hbm, solve_hbm, upper_ref, work_ref, factor_ref, sems):
    width = prior_ref.shape[0]
    tile = work_ref.shape[1] - width
    count = width // tile
    where_tile = {ij: k for k, ij in enumerate(upper_tiles(width, tile))}
    upper = lax.broadcasted_iota(jnp.int32, (tile, tile), 0) <= lax.broadcasted_iota(jnp.int32, (tile, tile), 1)
    cut = [slice(i * tile, (i + 1) * tile) for i in range(count + 1)]

    def given(i, j):
        block = total_ref[where_tile[i, j] * tile : (where_tile[i, j] + 1) * tile]
        return block + prior_ref[cut[i], cut[j]] if j < count else block

    def given_row(i):
        return jnp.concatenate([given(i, j) for j in range(i, count + 1)], axis=1)

    copies = []
    work_ref[cut[0]] = given_row(0)
    for i in range(count):
        base = i * tile
        ready = work_ref[base : base + SPREAD, base:]
        behind = work_ref[base + SPREAD : base + 2 * SPREAD, base:]
        for start in range(0, tile, SPREAD):
            final, ready = eliminate(ready, behind, start, tile)
            upper_ref[base + start : base + start + SPREAD, base:] = final
            after, rest, behind = start + 2 * SPREAD, start + 3 * SPREAD, None
            if after < tile:
                final = split(final)
                behind = work_ref[base + after : base + rest, base:] - product(columns(final, after, rest), final, TN)
            if rest < tile:
                later = slice(base + rest, base + tile)
                work_ref[later, base:] = work_ref[later, base:] - product(columns(final, rest, tile), final, TN)
        final = split(upper_ref[cut[i], base:])
        for k in range(i + 1, count):
            at = (k - i) * tile
            old = work_ref[cut[k], k * tile :] if i else given_row(k)
            step = product(columns(final, at, at + tile), columns(final, at, width + tile - base), TN)
            work_ref[cut[k], k * tile :] = old - step
        for j in range(count):
            if j < i:
                factor_ref[cut[j], cut[i]] = jnp.zeros((tile, tile), jnp.float32)
            else:
                block = upper_ref[cut[i], cut[j]]
                factor_ref[cut[j], cut[i]] = (jnp.where(upper, block, 0.0) if i == j else block).T
        copies += copy_all(
            (factor_ref.at[:, cut[i]], upper_ref.at[cut[i], width:]),
            (factor_hbm.at[:, cut[i]], solve_hbm.at[cut[i]]),
            sems.at[i],
        )
    for copy in copies:
        copy.wait()


def live_inverse(count_ref, inverse):
    slots = inverse.shape[0]
    place, places = lax.axis_index("inner"), lax.axis_size("inner")

    def live(shape, axis):
        position = lax.broadcasted_iota(jnp.int32, shape, axis) * places + place
        return (position < count_ref[0]).astype(jnp.float32)

    return inverse * live((slots, 1), 0) * live((1, slots), 1)


def picker(order_ref):
    width = order_ref.shape[1]
    return (lax.broadcasted_iota(jnp.int32, (width, width), 0) == order_ref[...]).astype(jnp.float32)


def copy_all(sources, targets, sems):
    copies = [pltpu.make_async_copy(source, target, sems.at[k]) for k, (source, target) in enumerate(zip(sources, targets))]
    for copy in copies:
        copy.start()
    return copies


def local_kernel(*refs):
    count_ref, sources, (own_ref, first_ref, rest_ref, last_ref), targets, sems = refs[0], refs[1:7], refs[7:11], refs[11:17], refs[17]
    mask_ref, order_ref, inverse_ref, coupling_ref, targets_ref, factor_ref = targets
    slots, reach = factor_ref.shape
    width, tile = coupling_ref.shape[1], coupling_ref.shape[1] // mask_ref.shape[1]
    sources = sources[:5] + (sources[5].at[:, :reach],)
    copies = copy_all(sources, targets, sems)
    for copy in copies[:2]:
        copy.wait()
    lane_tile = lax.broadcasted_iota(jnp.int32, (1, width), 1) // tile
    column_mask = jnp.zeros((1, width), jnp.float32)
    for t in range(width // tile):
        column_mask = jnp.where(lane_tile == t, mask_ref[0, t].astype(jnp.float32), column_mask)
    pick = picker(order_ref).astype(jnp.bfloat16)

    def ordered(x):
        return lax.dot_general(x, pick, NN, preferred_element_type=jnp.float32).astype(jnp.bfloat16)

    copies[2].wait()
    inverse = split(live_inverse(count_ref, inverse_ref[...]))
    copies[3].wait()
    high, low = split(coupling_ref[...] * column_mask)
    left = first_ref.shape[1] - slots
    own = product(inverse, (ordered(high), ordered(low)))
    own_ref[:, :width] = own
    first_ref[:, slots:] = own[:, :left]
    rest_ref[:, : width - left] = own[:, left:]
    last_ref[:, reach:] = own[:, :left]
    copies[4].wait()
    own = product(inverse, split(targets_ref[...]))
    own_ref[:, width:] = own
    rest_ref[:, width - left :] = own
    copies[5].wait()
    steps = -product(inverse, split(factor_ref[...]))
    first_ref[:, :slots] = steps[:, :slots]
    last_ref[:, :reach] = steps


def prior_kernel(order_ref, prior_ref, ordered_ref):
    pick = picker(order_ref)
    rows = lax.dot_general(pick, prior_ref[...], TN, precision=HIGHEST, preferred_element_type=jnp.float32)
    ordered_ref[...] = jnp.dot(rows, pick, precision=HIGHEST, preferred_element_type=jnp.float32)


def put_tiles(block, top, side, rows_ref, tile, count, add_ref=None):
    where_tile = {ij: k for k, ij in enumerate(upper_tiles(count * tile, tile))}
    for i in range(top, top + block.shape[0] // tile):
        for j in range(max(i, side), side + block.shape[1] // tile):
            rows = slice(where_tile[i, j] * tile, (where_tile[i, j] + 1) * tile)
            a, b = (i - top) * tile, (j - side) * tile
            piece = block[a : a + tile, b : b + tile]
            rows_ref[rows] = piece if add_ref is None else piece + add_ref[rows]


def stack(pairs):
    return tuple(jnp.concatenate([pair[side] for pair in pairs], axis=0) for side in range(2))


def columns(pair, start, stop):
    return pair[0][:, start:stop], pair[1][:, start:stop]


def early_kernel(tile, last_hbm, own_0_hbm, first_hbm, own_last_ref, own_rest_ref, prior_ref, *refs):
    high_ref, low_ref, base_ref, chain_high_ref, chain_low_ref, rows_ref = refs[:6]
    targets, sems = refs[6:9], refs[9]
    last_ref, own_0_ref, first_ref = targets
    slots, wide = own_0_ref.shape
    left = first_ref.shape[1] - slots
    reach = last_ref.shape[1] - left
    count = wide // tile - 1
    copies = copy_all((last_hbm, own_0_hbm, first_hbm), targets, sems)
    cut = [slice(k * slots, (k + 1) * slots) for k in range(3)]
    for copy in copies[1:]:
        copy.wait()
    solved_0 = split(own_0_ref[...])
    part_1 = product(split(first_ref[:, :slots]), solved_0)
    part_1 = jnp.concatenate([part_1[:, :left] + first_ref[:, slots:], part_1[:, left:]], axis=1)
    known = stack([solved_0, split(part_1)])
    step_21 = split(own_last_ref[:, cut[1]])
    part_2 = jnp.concatenate([own_last_ref[:, reach:], own_rest_ref[...]], axis=1)
    part_2 = part_2 + product(split(own_last_ref[:, : 2 * slots]), known)
    copies[0].wait()
    known = stack([known, split(part_2)])
    part_3 = product(split(last_ref[:, :reach]), known)
    part_3 = jnp.concatenate([part_3[:, :left] + last_ref[:, reach:], part_3[:, left:]], axis=1)
    known = stack([known, split(part_3)])
    chain_high_ref[:slots], chain_low_ref[:slots] = step_21
    chain_high_ref[slots:], chain_low_ref[slots:] = split(last_ref[:, cut[1]] + product(split(last_ref[:, cut[2]]), step_21))
    for k, part in enumerate((part_1, part_2, part_3)):
        base_ref[k * slots : (k + 1) * slots] = part[:, left:]
    high_ref[...], low_ref[...] = known[0][slots:, :left], known[1][slots:, :left]
    at = left // tile
    put_tiles(product(columns(known, 0, left), columns(known, 0, left), TN), 0, 0, rows_ref, tile, count)
    put_tiles(product(columns(solved_0, 0, left), columns(solved_0, left, wide), TN), 0, at, rows_ref, tile, count)
    put_tiles(product(columns(solved_0, left, count * tile), columns(solved_0, left, wide), TN), at, at, rows_ref, tile, count)


def gram_kernel(tile, rest_hbm, rest_3_hbm, high_ref, low_ref, base_ref, chain_high_ref, chain_low_ref, early_ref, *refs):
    rows_ref, rest_ref, rest_3_ref, sems = refs
    slots, wide = rest_ref.shape
    left = high_ref.shape[1]
    count = (left + wide) // tile - 1
    at = left // tile
    copies = copy_all((rest_hbm, rest_3_hbm), (rest_ref, rest_3_ref), sems)
    where_tile = {ij: k for k, ij in enumerate(upper_tiles(count * tile, tile))}
    for i in range(at):
        for j in range(i, at):
            rows = slice(where_tile[i, j] * tile, (where_tile[i, j] + 1) * tile)
            rows_ref[rows] = early_ref[rows]
    used = early_ref.shape[0]
    if rows_ref.shape[0] > used:
        rows_ref[used:] = jnp.zeros((rows_ref.shape[0] - used, tile), jnp.float32)
    for copy in copies:
        copy.wait()
    rest = rest_ref[...]
    step = product((chain_high_ref[...], chain_low_ref[...]), split(rest))
    right = jnp.concatenate([rest, step[:slots], step[slots:] + rest_3_ref[...]], axis=0)
    right = split(base_ref[...] + right)
    put_tiles(product((high_ref[...], low_ref[...]), right, TN), 0, at, rows_ref, tile, count, early_ref)
    put_tiles(product(columns(right, 0, count * tile - left), right, TN), at, at, rows_ref, tile, count, early_ref)


def stages():
    bits = (lax.axis_size("study") - 1).bit_length()
    return [(0, 1)] + [(low, min(2, bits - low)) for low in range(1, bits, 2)]


def pieces_of(block, low, size, me):
    count = 1 << size
    mine = (me >> low) & (count - 1)
    parts = block.reshape(count, block.shape[0] // count, block.shape[1])
    return [lax.dynamic_index_in_dim(parts, mine ^ m, 0, keepdims=False) for m in range(count)]


def total_over_studies(block, place):
    me = lax.axis_index("study")
    for low, size in stages():
        pieces = pieces_of(block, low, size, me)
        come = [exchange(pieces[m], m << low) for m in range(len(pieces) - 1, 0, -1)]
        block = sum(come, pieces[0])
    copies = [send(block, HUB, other) for other in range(lax.axis_size("inner")) if other != HUB]
    block = jnp.where(place == HUB, block, sum(copies))
    for low, size in reversed(stages()):
        pieces = [block] + [None] * ((1 << size) - 1)
        for m in range(len(pieces) - 1, 0, -1):
            pieces[m] = exchange(block, m << low)
        for bit in range(size):
            swap = ((me >> (low + bit)) & 1) == 1
            pieces = [jnp.where(swap, pieces[m ^ (1 << bit)], pieces[m]) for m in range(len(pieces))]
        block = jnp.concatenate(pieces, axis=0)
    return block


def on_device(
    trial_count_per_study,
    study_tile_mask,
    sep_order,
    stacked_study_factor,
    diagonal_block_inverses,
    coupling,
    targets,
    sep_prior,
):
    place = lax.axis_index("inner")
    slots = diagonal_block_inverses.shape[0]
    width = sep_prior.shape[0]
    tile = width // study_tile_mask.shape[1]
    wide = width + targets.shape[1]
    reach = (lax.axis_size("inner") - 1) * slots
    order = sep_order[None, :]
    left = (width // tile + 1) // 2 * tile
    own, first, rest, last = call(
        local_kernel,
        "local",
        tuple(floats(slots, size) for size in (wide, slots + left, wide - left, reach + left)),
        [SMEM] + [HBM] * 6,
        6 * slots * slots * (reach + wide),
        [
            pltpu.SMEM((1, width // tile), jnp.int32),
            pltpu.VMEM((1, width), jnp.int32),
            pltpu.VMEM((slots, slots), jnp.float32),
            pltpu.VMEM((slots, width), jnp.float32),
            pltpu.VMEM((slots, wide - width), jnp.float32),
            pltpu.VMEM((slots, reach), jnp.float32),
            pltpu.SemaphoreType.DMA((6,)),
        ],
    )(
        trial_count_per_study,
        *in_hbm(
            study_tile_mask,
            order,
            diagonal_block_inverses,
            coupling,
            targets,
            stacked_study_factor,
        ),
    )
    first_1 = send(first, 1, HUB)
    own_0 = send(own, 0, HUB)
    rest_1 = send(rest, 1, HUB)
    last_3 = send(last, 3, HUB)
    rest_3 = send(rest, 3, HUB)
    prior = call(prior_kernel, "prior", floats(width, width), [VMEM] * 2, 24 * width**3)(order, sep_prior)
    tiles = len(upper_tiles(width, tile))

    def halves(*shape):
        return jax.ShapeDtypeStruct(shape, jnp.bfloat16)

    early = call(
        functools.partial(early_kernel, tile),
        "early",
        (
            halves(reach, left),
            halves(reach, left),
            floats(reach, wide - left),
            halves(2 * slots, slots),
            halves(2 * slots, slots),
            floats(tiles * tile, tile),
        ),
        [HBM] * 3 + [VMEM, VMEM, ANY],
        6 * slots * wide * (6 * slots + width),
        [
            pltpu.VMEM((slots, reach + left), jnp.float32),
            pltpu.VMEM((slots, wide), jnp.float32),
            pltpu.VMEM((slots, slots + left), jnp.float32),
            pltpu.SemaphoreType.DMA((3,)),
        ],
    )(*in_hbm(last_3, own_0, first_1), last, rest, prior)
    unit = 8 * lax.axis_size("study")
    padded = -(-tiles * tile // unit) * unit
    rows = call(
        functools.partial(gram_kernel, tile),
        "gram",
        floats(padded, tile),
        [HBM] * 2 + [VMEM] * 6,
        6 * slots * wide * (2 * slots + 3 * width),
        [
            pltpu.VMEM((slots, wide - left), jnp.float32),
            pltpu.VMEM((slots, wide - left), jnp.float32),
            pltpu.SemaphoreType.DMA((2,)),
        ],
    )(*in_hbm(rest_1, rest_3), *early)
    total = total_over_studies(rows, place)
    return call(
        factor_kernel,
        "factor_and_solve",
        (floats(width, width), floats(width, tile)),
        [VMEM, VMEM],
        width**3,
        [
            pltpu.VMEM((width, wide), jnp.float32),
            pltpu.VMEM((width, wide), jnp.float32),
            pltpu.VMEM((width, width), jnp.float32),
            pltpu.SemaphoreType.DMA((width // tile, 2)),
        ],
        out_spec=HBM,
    )(total, prior)


def solution(mesh):
    return jax.shard_map(
        on_device,
        mesh=mesh,
        in_specs=(
            P("study"),
            P("study", None),
            P(),
            P(("study", "inner"), None),
            P(("study", "inner"), None),
            P(("study", "inner"), None),
            P(("study", "inner"), None),
            P(),
        ),
        out_specs=(P(), P()),
        check_vma=False,
    )
```

```python
import functools

import jax
import jax.numpy as jnp
from jax import lax
from jax.experimental import pallas as pl
from jax.experimental.pallas import tpu as pltpu
from jax.sharding import PartitionSpec as P

HIGHEST = lax.Precision.HIGHEST
HUB = 2
SPREAD = 16


NN = (((1,), (0,)), ((), ()))
TN = (((0,), (0,)), ((), ()))
VMEM = pl.BlockSpec(memory_space=pltpu.VMEM)
SMEM = pl.BlockSpec(memory_space=pltpu.SMEM)
ANY = pl.BlockSpec(memory_space=pl.ANY)
HBM = pl.BlockSpec(memory_space=pltpu.HBM)


def call(kernel, name, out_shape, in_specs, flops, scratch_shapes=(), out_spec=VMEM):
    many = isinstance(out_shape, tuple)
    return pl.pallas_call(
        kernel,
        out_shape=out_shape,
        in_specs=in_specs,
        out_specs=(out_spec,) * len(out_shape) if many else out_spec,
        scratch_shapes=scratch_shapes,
        cost_estimate=pl.CostEstimate(flops=flops, bytes_accessed=1 << 20, transcendentals=0),
        compiler_params=pltpu.CompilerParams(vmem_limit_bytes=16 << 20),
        name=name,
    )


def floats(*shape):
    return jax.ShapeDtypeStruct(shape, jnp.float32)


def in_hbm(*arrays):
    return [pltpu.with_memory_space_constraint(array, pltpu.HBM) for array in arrays]


def split(x):
    high = x.astype(jnp.bfloat16)
    return high, (x - high.astype(jnp.float32)).astype(jnp.bfloat16)


def product(a, b, dims=NN):
    def one(x, y):
        return lax.dot_general(x, y, dims, preferred_element_type=jnp.float32)

    return one(a[0], b[0]) + (one(a[0], b[1]) + one(a[1], b[0]))


def exchange(block, mask):
    count = lax.axis_size("study")
    return lax.ppermute(block, "study", [(i, i ^ mask) for i in range(count)])


def send(block, source, target):
    return lax.ppermute(block, "inner", [(source, target)])


def packed_tiles(width, tile):
    places, used = {}, 0
    for i in range(width // tile):
        for j in range(i, width // tile + 1):
            if i == j and i % 2:
                places[i, j] = places[i - 1, i - 1]
            else:
                places[i, j] = used
                used += 1
    return {ij: slice(k * tile, (k + 1) * tile) for ij, k in places.items()}, used


def grid_of(tile):
    return tuple(lax.broadcasted_iota(jnp.int32, (tile, tile), axis) for axis in range(2))


def eliminate(block, behind, lane, tile):
    wide = block.shape[1]
    row = lax.broadcasted_iota(jnp.int32, (8, 1), 0)
    groups = [rows[8 * g : 8 * g + 8] for rows in (block, behind) if rows is not None for g in range(SPREAD // 8)]
    spread = [[jnp.broadcast_to(rows[:, lane + k : lane + k + 1], (8, tile)) for rows in groups] for k in range(SPREAD)]
    final = []
    for i in range(SPREAD):
        group, line = divmod(i, 8)
        scale = lax.rsqrt(spread[i][group][line : line + 1])
        final.append(groups[group][line : line + 1] * jnp.tile(scale, (1, wide // tile)))
        below = {g: spread[i][g] * scale for g in range(group, len(groups))}
        below[group] = jnp.where(row > line, below[group], 0.0)
        if line == 7:
            del below[group]
        for k in range(i + 1, SPREAD):
            factor = spread[k][group][line : line + 1] * scale
            for g in below:
                spread[k][g] = spread[k][g] - below[g] * factor
        for g in below:
            groups[g] = groups[g] - jnp.tile(below[g], (1, wide // tile)) * final[-1]
    final = jnp.concatenate(final, axis=0)
    return final, None if behind is None else jnp.concatenate(groups[SPREAD // 8 :], axis=0)


def factor_kernel(total_ref, prior_ref, factor_hbm, solve_hbm, upper_ref, work_ref, factor_ref, sems):
    width = prior_ref.shape[0]
    tile = work_ref.shape[1] - width
    count = width // tile
    place, used = packed_tiles(width, tile)
    row, column = grid_of(tile)
    upper = row <= column
    cut = [slice(i * tile, (i + 1) * tile) for i in range(count + 1)]

    def given(i, j):
        block = total_ref[place[i, j]]
        if i == j and i % 2:
            at = used * tile + i // 2
            block = jnp.where(upper, jnp.where(row == column, total_ref[at : at + 1], block.T), block)
        elif i == j:
            block = jnp.where(upper, block, block.T)
        return block + prior_ref[cut[i], cut[j]] if j < count else block

    def given_row(i):
        return jnp.concatenate([given(i, j) for j in range(i, count + 1)], axis=1)

    copies = []
    work_ref[cut[0]] = given_row(0)
    for i in range(count):
        base = i * tile
        ready = work_ref[base : base + SPREAD, base:]
        behind = work_ref[base + SPREAD : base + 2 * SPREAD, base:]
        for start in range(0, tile, SPREAD):
            final, ready = eliminate(ready, behind, start, tile)
            upper_ref[base + start : base + start + SPREAD, base:] = final
            after, rest, behind = start + 2 * SPREAD, start + 3 * SPREAD, None
            if after < tile:
                final = split(final)
                behind = work_ref[base + after : base + rest, base:] - product(columns(final, after, rest), final, TN)
            if rest < tile:
                later = slice(base + rest, base + tile)
                work_ref[later, base:] = work_ref[later, base:] - product(columns(final, rest, tile), final, TN)
        final = split(upper_ref[cut[i], base:])
        for k in range(i + 1, count):
            at = (k - i) * tile
            old = work_ref[cut[k], k * tile :] if i else given_row(k)
            step = product(columns(final, at, at + tile), columns(final, at, width + tile - base), TN)
            work_ref[cut[k], k * tile :] = old - step
        for j in range(count):
            if j < i:
                factor_ref[cut[j], cut[i]] = jnp.zeros((tile, tile), jnp.float32)
            else:
                block = upper_ref[cut[i], cut[j]]
                factor_ref[cut[j], cut[i]] = (jnp.where(upper, block, 0.0) if i == j else block).T
        copies += copy_all(
            (factor_ref.at[:, cut[i]], upper_ref.at[cut[i], width:]),
            (factor_hbm.at[:, cut[i]], solve_hbm.at[cut[i]]),
            sems.at[i],
        )
    for copy in copies:
        copy.wait()


def live_inverse(count_ref, inverse):
    slots = inverse.shape[0]
    place, places = lax.axis_index("inner"), lax.axis_size("inner")

    def live(shape, axis):
        position = lax.broadcasted_iota(jnp.int32, shape, axis) * places + place
        return (position < count_ref[0]).astype(jnp.float32)

    return inverse * live((slots, 1), 0) * live((1, slots), 1)


def picker(order_ref):
    width = order_ref.shape[1]
    return (lax.broadcasted_iota(jnp.int32, (width, width), 0) == order_ref[...]).astype(jnp.float32)


def copy_all(sources, targets, sems):
    copies = [pltpu.make_async_copy(source, target, sems.at[k]) for k, (source, target) in enumerate(zip(sources, targets))]
    for copy in copies:
        copy.start()
    return copies


def local_kernel(*refs):
    count_ref, sources, (own_ref, first_ref, rest_ref, last_ref), targets, sems = refs[0], refs[1:7], refs[7:11], refs[11:17], refs[17]
    mask_ref, order_ref, inverse_ref, coupling_ref, targets_ref, factor_ref = targets
    slots, reach = factor_ref.shape
    width, tile = coupling_ref.shape[1], coupling_ref.shape[1] // mask_ref.shape[1]
    sources = sources[:5] + (sources[5].at[:, :reach],)
    copies = copy_all(sources, targets, sems)
    for copy in copies[:2]:
        copy.wait()
    lane_tile = lax.broadcasted_iota(jnp.int32, (1, width), 1) // tile
    column_mask = jnp.zeros((1, width), jnp.float32)
    for t in range(width // tile):
        column_mask = jnp.where(lane_tile == t, mask_ref[0, t].astype(jnp.float32), column_mask)
    pick = picker(order_ref).astype(jnp.bfloat16)

    def ordered(x):
        return lax.dot_general(x, pick, NN, preferred_element_type=jnp.float32).astype(jnp.bfloat16)

    copies[2].wait()
    inverse = split(live_inverse(count_ref, inverse_ref[...]))
    copies[3].wait()
    high, low = split(coupling_ref[...] * column_mask)
    left = first_ref.shape[1] - slots
    own = product(inverse, (ordered(high), ordered(low)))
    own_ref[:, :width] = own
    first_ref[:, slots:] = own[:, :left]
    rest_ref[:, : width - left] = own[:, left:]
    last_ref[:, reach:] = own[:, :left]
    copies[4].wait()
    own = product(inverse, split(targets_ref[...]))
    own_ref[:, width:] = own
    rest_ref[:, width - left :] = own
    copies[5].wait()
    steps = -product(inverse, split(factor_ref[...]))
    first_ref[:, :slots] = steps[:, :slots]
    last_ref[:, :reach] = steps


def prior_kernel(order_ref, prior_ref, ordered_ref):
    pick = picker(order_ref)
    rows = lax.dot_general(pick, prior_ref[...], TN, precision=HIGHEST, preferred_element_type=jnp.float32)
    ordered_ref[...] = jnp.dot(rows, pick, precision=HIGHEST, preferred_element_type=jnp.float32)


def put_tiles(block, top, side, rows_ref, tile, count, add_ref=None):
    place, used = packed_tiles(count * tile, tile)
    row, column = grid_of(tile)

    def piece(i, j):
        a, b = (i - top) * tile, (j - side) * tile
        return block[a : a + tile, b : b + tile]

    def put(rows, value):
        rows_ref[rows] = value if add_ref is None else value + add_ref[rows]

    stop = top + block.shape[0] // tile
    for i in range(top, stop):
        for j in range(max(i, side), side + block.shape[1] // tile):
            if i != j:
                put(place[i, j], piece(i, j))
            elif i % 2:
                at = used * tile + i // 2
                put(slice(at, at + 1), jnp.sum(jnp.where(row == column, piece(i, i), 0.0), axis=0, keepdims=True))
            else:
                put(place[i, i], jnp.where(row <= column, piece(i, i), piece(i + 1, i + 1)) if i + 1 < stop else piece(i, i))


def stack(pairs):
    return tuple(jnp.concatenate([pair[side] for pair in pairs], axis=0) for side in range(2))


def columns(pair, start, stop):
    return pair[0][:, start:stop], pair[1][:, start:stop]


def early_kernel(tile, last_hbm, own_0_hbm, first_hbm, own_last_ref, own_rest_ref, prior_ref, *refs):
    high_ref, low_ref, base_ref, chain_high_ref, chain_low_ref, rows_ref = refs[:6]
    targets, sems = refs[6:9], refs[9]
    last_ref, own_0_ref, first_ref = targets
    slots, wide = own_0_ref.shape
    left = first_ref.shape[1] - slots
    reach = last_ref.shape[1] - left
    count = wide // tile - 1
    copies = copy_all((last_hbm, own_0_hbm, first_hbm), targets, sems)
    cut = [slice(k * slots, (k + 1) * slots) for k in range(3)]
    for copy in copies[1:]:
        copy.wait()
    solved_0 = split(own_0_ref[...])
    part_1 = product(split(first_ref[:, :slots]), solved_0)
    part_1 = jnp.concatenate([part_1[:, :left] + first_ref[:, slots:], part_1[:, left:]], axis=1)
    known = stack([solved_0, split(part_1)])
    step_21 = split(own_last_ref[:, cut[1]])
    part_2 = jnp.concatenate([own_last_ref[:, reach:], own_rest_ref[...]], axis=1)
    part_2 = part_2 + product(split(own_last_ref[:, : 2 * slots]), known)
    copies[0].wait()
    known = stack([known, split(part_2)])
    part_3 = product(split(last_ref[:, :reach]), known)
    part_3 = jnp.concatenate([part_3[:, :left] + last_ref[:, reach:], part_3[:, left:]], axis=1)
    known = stack([known, split(part_3)])
    chain_high_ref[:slots], chain_low_ref[:slots] = step_21
    chain_high_ref[slots:], chain_low_ref[slots:] = split(last_ref[:, cut[1]] + product(split(last_ref[:, cut[2]]), step_21))
    for k, part in enumerate((part_1, part_2, part_3)):
        base_ref[k * slots : (k + 1) * slots] = part[:, left:]
    high_ref[...], low_ref[...] = known[0][slots:, :left], known[1][slots:, :left]
    at = left // tile
    put_tiles(product(columns(known, 0, left), columns(known, 0, left), TN), 0, 0, rows_ref, tile, count)
    put_tiles(product(columns(solved_0, 0, left), columns(solved_0, left, wide), TN), 0, at, rows_ref, tile, count)
    put_tiles(product(columns(solved_0, left, count * tile), columns(solved_0, left, wide), TN), at, at, rows_ref, tile, count)


def gram_kernel(tile, rest_hbm, rest_3_hbm, high_ref, low_ref, base_ref, chain_high_ref, chain_low_ref, early_ref, *refs):
    rows_ref, rest_ref, rest_3_ref, sems = refs
    slots, wide = rest_ref.shape
    left = high_ref.shape[1]
    count = (left + wide) // tile - 1
    at = left // tile
    copies = copy_all((rest_hbm, rest_3_hbm), (rest_ref, rest_3_ref), sems)
    place, used = packed_tiles(count * tile, tile)
    rows_ref[used * tile :] = jnp.zeros((rows_ref.shape[0] - used * tile, tile), jnp.float32)
    done = [place[i, j] for i in range(at) for j in range(i, at) if i < j or i % 2 == 0]
    for rows in done + [slice(used * tile + i // 2, used * tile + i // 2 + 1) for i in range(1, at, 2)]:
        rows_ref[rows] = early_ref[rows]
    for copy in copies:
        copy.wait()
    rest = rest_ref[...]
    step = product((chain_high_ref[...], chain_low_ref[...]), split(rest))
    right = jnp.concatenate([rest, step[:slots], step[slots:] + rest_3_ref[...]], axis=0)
    right = split(base_ref[...] + right)
    put_tiles(product((high_ref[...], low_ref[...]), right, TN), 0, at, rows_ref, tile, count, early_ref)
    put_tiles(product(columns(right, 0, count * tile - left), right, TN), at, at, rows_ref, tile, count, early_ref)


def stages():
    bits = (lax.axis_size("study") - 1).bit_length()
    return [(0, 1)] + [(low, min(2, bits - low)) for low in range(1, bits, 2)]


def pieces_of(block, low, size, me):
    count = 1 << size
    mine = (me >> low) & (count - 1)
    parts = block.reshape(count, block.shape[0] // count, block.shape[1])
    return [lax.dynamic_index_in_dim(parts, mine ^ m, 0, keepdims=False) for m in range(count)]


def total_over_studies(block, place):
    me = lax.axis_index("study")
    for low, size in stages():
        pieces = pieces_of(block, low, size, me)
        come = [exchange(pieces[m], m << low) for m in range(len(pieces) - 1, 0, -1)]
        block = sum(come, pieces[0])
    copies = [send(block, HUB, other) for other in range(lax.axis_size("inner")) if other != HUB]
    block = jnp.where(place == HUB, block, sum(copies))
    for low, size in reversed(stages()):
        pieces = [block] + [None] * ((1 << size) - 1)
        for m in range(len(pieces) - 1, 0, -1):
            pieces[m] = exchange(block, m << low)
        for bit in range(size):
            swap = ((me >> (low + bit)) & 1) == 1
            pieces = [jnp.where(swap, pieces[m ^ (1 << bit)], pieces[m]) for m in range(len(pieces))]
        block = jnp.concatenate(pieces, axis=0)
    return block


def on_device(
    trial_count_per_study,
    study_tile_mask,
    sep_order,
    stacked_study_factor,
    diagonal_block_inverses,
    coupling,
    targets,
    sep_prior,
):
    place = lax.axis_index("inner")
    slots = diagonal_block_inverses.shape[0]
    width = sep_prior.shape[0]
    tile = width // study_tile_mask.shape[1]
    wide = width + targets.shape[1]
    reach = (lax.axis_size("inner") - 1) * slots
    order = sep_order[None, :]
    left = (width // tile + 1) // 2 * tile
    own, first, rest, last = call(
        local_kernel,
        "local",
        tuple(floats(slots, size) for size in (wide, slots + left, wide - left, reach + left)),
        [SMEM] + [HBM] * 6,
        6 * slots * slots * (reach + wide),
        [
            pltpu.SMEM((1, width // tile), jnp.int32),
            pltpu.VMEM((1, width), jnp.int32),
            pltpu.VMEM((slots, slots), jnp.float32),
            pltpu.VMEM((slots, width), jnp.float32),
            pltpu.VMEM((slots, wide - width), jnp.float32),
            pltpu.VMEM((slots, reach), jnp.float32),
            pltpu.SemaphoreType.DMA((6,)),
        ],
    )(
        trial_count_per_study,
        *in_hbm(
            study_tile_mask,
            order,
            diagonal_block_inverses,
            coupling,
            targets,
            stacked_study_factor,
        ),
    )
    first_1 = send(first, 1, HUB)
    own_0 = send(own, 0, HUB)
    rest_1 = send(rest, 1, HUB)
    last_3 = send(last, 3, HUB)
    rest_3 = send(rest, 3, HUB)
    prior = call(prior_kernel, "prior", floats(width, width), [VMEM] * 2, 24 * width**3)(order, sep_prior)
    packed = packed_tiles(width, tile)[1] * tile + 8

    def halves(*shape):
        return jax.ShapeDtypeStruct(shape, jnp.bfloat16)

    early = call(
        functools.partial(early_kernel, tile),
        "early",
        (
            halves(reach, left),
            halves(reach, left),
            floats(reach, wide - left),
            halves(2 * slots, slots),
            halves(2 * slots, slots),
            floats(packed, tile),
        ),
        [HBM] * 3 + [VMEM, VMEM, ANY],
        6 * slots * wide * (6 * slots + width),
        [
            pltpu.VMEM((slots, reach + left), jnp.float32),
            pltpu.VMEM((slots, wide), jnp.float32),
            pltpu.VMEM((slots, slots + left), jnp.float32),
            pltpu.SemaphoreType.DMA((3,)),
        ],
    )(*in_hbm(last_3, own_0, first_1), last, rest, prior)
    unit = 8 * lax.axis_size("study")
    padded = -(-packed // unit) * unit
    rows = call(
        functools.partial(gram_kernel, tile),
        "gram",
        floats(padded, tile),
        [HBM] * 2 + [VMEM] * 6,
        6 * slots * wide * (2 * slots + 3 * width),
        [
            pltpu.VMEM((slots, wide - left), jnp.float32),
            pltpu.VMEM((slots, wide - left), jnp.float32),
            pltpu.SemaphoreType.DMA((2,)),
        ],
    )(*in_hbm(rest_1, rest_3), *early)
    total = total_over_studies(rows, place)
    return call(
        factor_kernel,
        "factor_and_solve",
        (floats(width, width), floats(width, tile)),
        [VMEM, VMEM],
        width**3,
        [
            pltpu.VMEM((width, wide), jnp.float32),
            pltpu.VMEM((width, wide), jnp.float32),
            pltpu.VMEM((width, width), jnp.float32),
            pltpu.SemaphoreType.DMA((width // tile, 2)),
        ],
        out_spec=HBM,
    )(total, prior)


def solution(mesh):
    return jax.shard_map(
        on_device,
        mesh=mesh,
        in_specs=(
            P("study"),
            P("study", None),
            P(),
            P(("study", "inner"), None),
            P(("study", "inner"), None),
            P(("study", "inner"), None),
            P(("study", "inner"), None),
            P(),
        ),
        out_specs=(P(), P()),
        check_vma=False,
    )
```

```python
import functools

import jax
import jax.numpy as jnp
from jax import lax
from jax.experimental import pallas as pl
from jax.experimental.pallas import tpu as pltpu
from jax.sharding import PartitionSpec as P

HIGHEST = lax.Precision.HIGHEST
HUB = 2
SPREAD = 16


NN = (((1,), (0,)), ((), ()))
TN = (((0,), (0,)), ((), ()))
VMEM = pl.BlockSpec(memory_space=pltpu.VMEM)
SMEM = pl.BlockSpec(memory_space=pltpu.SMEM)
ANY = pl.BlockSpec(memory_space=pl.ANY)
HBM = pl.BlockSpec(memory_space=pltpu.HBM)


def call(kernel, name, out_shape, in_specs, flops, scratch_shapes=(), out_spec=VMEM):
    many = isinstance(out_shape, tuple)
    return pl.pallas_call(
        kernel,
        out_shape=out_shape,
        in_specs=in_specs,
        out_specs=(out_spec,) * len(out_shape) if many else out_spec,
        scratch_shapes=scratch_shapes,
        cost_estimate=pl.CostEstimate(flops=flops, bytes_accessed=1 << 20, transcendentals=0),
        compiler_params=pltpu.CompilerParams(vmem_limit_bytes=16 << 20),
        name=name,
    )


def floats(*shape):
    return jax.ShapeDtypeStruct(shape, jnp.float32)


def in_hbm(*arrays):
    return [pltpu.with_memory_space_constraint(array, pltpu.HBM) for array in arrays]


def split(x):
    high = x.astype(jnp.bfloat16)
    return high, (x - high.astype(jnp.float32)).astype(jnp.bfloat16)


def product(a, b, dims=NN):
    def one(x, y):
        return lax.dot_general(x, y, dims, preferred_element_type=jnp.float32)

    return one(a[0], b[0]) + (one(a[0], b[1]) + one(a[1], b[0]))


def exchange(block, mask):
    count = lax.axis_size("study")
    return lax.ppermute(block, "study", [(i, i ^ mask) for i in range(count)])


def send(block, source, target):
    return lax.ppermute(block, "inner", [(source, target)])


def packed_tiles(width, tile):
    places, used = {}, 0
    for i in range(width // tile):
        for j in range(i, width // tile + 1):
            if i == j and i % 2:
                places[i, j] = places[i - 1, i - 1]
            else:
                places[i, j] = used
                used += 1
    return {ij: slice(k * tile, (k + 1) * tile) for ij, k in places.items()}, used


def grid_of(tile):
    return tuple(lax.broadcasted_iota(jnp.int32, (tile, tile), axis) for axis in range(2))


def eliminate(block, behind, lane, tile):
    wide = block.shape[1]
    row = lax.broadcasted_iota(jnp.int32, (8, 1), 0)
    groups = [rows[8 * g : 8 * g + 8] for rows in (block, behind) if rows is not None for g in range(SPREAD // 8)]
    spread = [[jnp.broadcast_to(rows[:, lane + k : lane + k + 1], (8, tile)) for rows in groups] for k in range(SPREAD)]
    final = []
    for i in range(SPREAD):
        group, line = divmod(i, 8)
        scale = lax.rsqrt(spread[i][group][line : line + 1])
        final.append(groups[group][line : line + 1] * jnp.tile(scale, (1, wide // tile)))
        below = {g: spread[i][g] * scale for g in range(group, len(groups))}
        below[group] = jnp.where(row > line, below[group], 0.0)
        if line == 7:
            del below[group]
        for k in range(i + 1, SPREAD):
            factor = spread[k][group][line : line + 1] * scale
            for g in below:
                spread[k][g] = spread[k][g] - below[g] * factor
        for g in below:
            groups[g] = groups[g] - jnp.tile(below[g], (1, wide // tile)) * final[-1]
    final = jnp.concatenate(final, axis=0)
    return final, None if behind is None else jnp.concatenate(groups[SPREAD // 8 :], axis=0)


def factor_kernel(total_ref, prior_ref, factor_hbm, solve_hbm, upper_ref, work_ref, factor_ref, sems):
    width = prior_ref.shape[0]
    tile = work_ref.shape[1] - width
    count = width // tile
    place, used = packed_tiles(width, tile)
    row, column = grid_of(tile)
    upper = row <= column
    cut = [slice(i * tile, (i + 1) * tile) for i in range(count + 1)]

    def given(i, j):
        block = total_ref[place[i, j]]
        if i == j and i % 2:
            at = used * tile + i // 2
            block = jnp.where(upper, jnp.where(row == column, total_ref[at : at + 1], block.T), block)
        elif i == j:
            block = jnp.where(upper, block, block.T)
        return block + prior_ref[cut[i], cut[j]] if j < count else block

    def given_row(i):
        return jnp.concatenate([given(i, j) for j in range(i, count + 1)], axis=1)

    copies = []
    work_ref[cut[0]] = given_row(0)
    for i in range(count):
        base = i * tile
        ready = work_ref[base : base + SPREAD, base:]
        behind = work_ref[base + SPREAD : base + 2 * SPREAD, base:]
        for start in range(0, tile, SPREAD):
            final, ready = eliminate(ready, behind, start, tile)
            upper_ref[base + start : base + start + SPREAD, base:] = final
            after, rest, behind = start + 2 * SPREAD, start + 3 * SPREAD, None
            if after < tile:
                final = split(final)
                behind = work_ref[base + after : base + rest, base:] - product(columns(final, after, rest), final, TN)
            if rest < tile:
                later = slice(base + rest, base + tile)
                work_ref[later, base:] = work_ref[later, base:] - product(columns(final, rest, tile), final, TN)
        final = split(upper_ref[cut[i], base:])
        for k in range(i + 1, count):
            at = (k - i) * tile
            old = work_ref[cut[k], k * tile :] if i else given_row(k)
            step = product(columns(final, at, at + tile), columns(final, at, width + tile - base), TN)
            work_ref[cut[k], k * tile :] = old - step
        for j in range(count):
            if j < i:
                factor_ref[cut[j], cut[i]] = jnp.zeros((tile, tile), jnp.float32)
            else:
                block = upper_ref[cut[i], cut[j]]
                factor_ref[cut[j], cut[i]] = (jnp.where(upper, block, 0.0) if i == j else block).T
        copies += copy_all(
            (factor_ref.at[:, cut[i]], upper_ref.at[cut[i], width:]),
            (factor_hbm.at[:, cut[i]], solve_hbm.at[cut[i]]),
            sems.at[i],
        )
    for copy in copies:
        copy.wait()


def live_inverse(count_ref, inverse):
    slots = inverse.shape[0]
    place, places = lax.axis_index("inner"), lax.axis_size("inner")

    def live(shape, axis):
        position = lax.broadcasted_iota(jnp.int32, shape, axis) * places + place
        return (position < count_ref[0]).astype(jnp.float32)

    return inverse * live((slots, 1), 0) * live((1, slots), 1)


def picker(order_ref):
    width = order_ref.shape[1]
    return (lax.broadcasted_iota(jnp.int32, (width, width), 0) == order_ref[...]).astype(jnp.float32)


def copy_all(sources, targets, sems):
    copies = [pltpu.make_async_copy(source, target, sems.at[k]) for k, (source, target) in enumerate(zip(sources, targets))]
    for copy in copies:
        copy.start()
    return copies


def own_kernel(count_ref, mask_hbm, order_hbm, inverse_hbm, coupling_hbm, targets_hbm, own_ref, *refs):
    sources = (mask_hbm, order_hbm, inverse_hbm, coupling_hbm, targets_hbm)
    targets, sems = refs[:5], refs[5]
    mask_ref, order_ref, inverse_ref, coupling_ref, targets_ref = targets
    width, tile = coupling_ref.shape[1], coupling_ref.shape[1] // mask_ref.shape[1]
    copies = copy_all(sources, targets, sems)
    for copy in copies[:2]:
        copy.wait()
    lane_tile = lax.broadcasted_iota(jnp.int32, (1, width), 1) // tile
    column_mask = jnp.zeros((1, width), jnp.float32)
    for t in range(width // tile):
        column_mask = jnp.where(lane_tile == t, mask_ref[0, t].astype(jnp.float32), column_mask)
    pick = picker(order_ref).astype(jnp.bfloat16)

    def ordered(x):
        return lax.dot_general(x, pick, NN, preferred_element_type=jnp.float32).astype(jnp.bfloat16)

    copies[2].wait()
    inverse = split(live_inverse(count_ref, inverse_ref[...]))
    copies[3].wait()
    high, low = split(coupling_ref[...] * column_mask)
    own_ref[:, :width] = product(inverse, (ordered(high), ordered(low)))
    copies[4].wait()
    own_ref[:, width:] = product(inverse, split(targets_ref[...]))


def steps_kernel(count_ref, inverse_ref, factor_ref, own_ref, first_ref, rest_ref, last_ref):
    slots = inverse_ref.shape[0]
    left = first_ref.shape[1] - slots
    reach = last_ref.shape[1] - left
    inverse = split(-live_inverse(count_ref, inverse_ref[...]))
    steps = product(inverse, split(factor_ref[:, :reach]))
    first_ref[:, :slots] = steps[:, :slots]
    last_ref[:, :reach] = steps
    first_ref[:, slots:] = own_ref[:, :left]
    last_ref[:, reach:] = own_ref[:, :left]
    rest_ref[...] = own_ref[:, left:]


def prior_kernel(order_ref, prior_ref, after_ref, ordered_ref):
    pick = picker(order_ref)
    rows = lax.dot_general(pick, prior_ref[...], TN, precision=HIGHEST, preferred_element_type=jnp.float32)
    ordered_ref[...] = jnp.dot(rows, pick, precision=HIGHEST, preferred_element_type=jnp.float32)


def put_tiles(block, top, side, rows_ref, tile, count, add_ref=None):
    place, used = packed_tiles(count * tile, tile)
    row, column = grid_of(tile)

    def piece(i, j):
        a, b = (i - top) * tile, (j - side) * tile
        return block[a : a + tile, b : b + tile]

    def put(rows, value):
        rows_ref[rows] = value if add_ref is None else value + add_ref[rows]

    stop = top + block.shape[0] // tile
    for i in range(top, stop):
        for j in range(max(i, side), side + block.shape[1] // tile):
            if i != j:
                put(place[i, j], piece(i, j))
            elif i % 2:
                at = used * tile + i // 2
                put(slice(at, at + 1), jnp.sum(jnp.where(row == column, piece(i, i), 0.0), axis=0, keepdims=True))
            else:
                put(place[i, i], jnp.where(row <= column, piece(i, i), piece(i + 1, i + 1)) if i + 1 < stop else piece(i, i))


def stack(pairs):
    return tuple(jnp.concatenate([pair[side] for pair in pairs], axis=0) for side in range(2))


def columns(pair, start, stop):
    return pair[0][:, start:stop], pair[1][:, start:stop]


def early_kernel(tile, last_hbm, own_0_hbm, first_hbm, own_last_ref, own_rest_ref, prior_ref, *refs):
    high_ref, low_ref, base_ref, chain_high_ref, chain_low_ref, rows_ref = refs[:6]
    targets, sems = refs[6:9], refs[9]
    last_ref, own_0_ref, first_ref = targets
    slots, wide = own_0_ref.shape
    left = first_ref.shape[1] - slots
    reach = last_ref.shape[1] - left
    count = wide // tile - 1
    copies = copy_all((last_hbm, own_0_hbm, first_hbm), targets, sems)
    cut = [slice(k * slots, (k + 1) * slots) for k in range(3)]
    for copy in copies[1:]:
        copy.wait()
    solved_0 = split(own_0_ref[...])
    part_1 = product(split(first_ref[:, :slots]), solved_0)
    part_1 = jnp.concatenate([part_1[:, :left] + first_ref[:, slots:], part_1[:, left:]], axis=1)
    known = stack([solved_0, split(part_1)])
    step_21 = split(own_last_ref[:, cut[1]])
    part_2 = jnp.concatenate([own_last_ref[:, reach:], own_rest_ref[...]], axis=1)
    part_2 = part_2 + product(split(own_last_ref[:, : 2 * slots]), known)
    copies[0].wait()
    known = stack([known, split(part_2)])
    part_3 = product(split(last_ref[:, :reach]), known)
    part_3 = jnp.concatenate([part_3[:, :left] + last_ref[:, reach:], part_3[:, left:]], axis=1)
    known = stack([known, split(part_3)])
    chain_high_ref[:slots], chain_low_ref[:slots] = step_21
    chain_high_ref[slots:], chain_low_ref[slots:] = split(last_ref[:, cut[1]] + product(split(last_ref[:, cut[2]]), step_21))
    for k, part in enumerate((part_1, part_2, part_3)):
        base_ref[k * slots : (k + 1) * slots] = part[:, left:]
    high_ref[...], low_ref[...] = known[0][slots:, :left], known[1][slots:, :left]
    at = left // tile
    put_tiles(product(columns(known, 0, left), columns(known, 0, left), TN), 0, 0, rows_ref, tile, count)
    put_tiles(product(columns(solved_0, 0, left), columns(solved_0, left, wide), TN), 0, at, rows_ref, tile, count)
    put_tiles(product(columns(solved_0, left, count * tile), columns(solved_0, left, wide), TN), at, at, rows_ref, tile, count)


def gram_kernel(tile, rest_hbm, rest_3_hbm, high_ref, low_ref, base_ref, chain_high_ref, chain_low_ref, early_ref, *refs):
    rows_ref, rest_ref, rest_3_ref, sems = refs
    slots, wide = rest_ref.shape
    left = high_ref.shape[1]
    count = (left + wide) // tile - 1
    at = left // tile
    copies = copy_all((rest_hbm, rest_3_hbm), (rest_ref, rest_3_ref), sems)
    place, used = packed_tiles(count * tile, tile)
    rows_ref[used * tile :] = jnp.zeros((rows_ref.shape[0] - used * tile, tile), jnp.float32)
    done = [place[i, j] for i in range(at) for j in range(i, at) if i < j or i % 2 == 0]
    for rows in done + [slice(used * tile + i // 2, used * tile + i // 2 + 1) for i in range(1, at, 2)]:
        rows_ref[rows] = early_ref[rows]
    for copy in copies:
        copy.wait()
    rest = rest_ref[...]
    step = product((chain_high_ref[...], chain_low_ref[...]), split(rest))
    right = jnp.concatenate([rest, step[:slots], step[slots:] + rest_3_ref[...]], axis=0)
    right = split(base_ref[...] + right)
    put_tiles(product((high_ref[...], low_ref[...]), right, TN), 0, at, rows_ref, tile, count, early_ref)
    put_tiles(product(columns(right, 0, count * tile - left), right, TN), at, at, rows_ref, tile, count, early_ref)


def stages():
    bits = (lax.axis_size("study") - 1).bit_length()
    return [(0, 1)] + [(low, min(2, bits - low)) for low in range(1, bits, 2)]


def pieces_of(block, low, size, me):
    count = 1 << size
    mine = (me >> low) & (count - 1)
    parts = block.reshape(count, block.shape[0] // count, block.shape[1])
    return [lax.dynamic_index_in_dim(parts, mine ^ m, 0, keepdims=False) for m in range(count)]


def total_over_studies(block, place):
    me = lax.axis_index("study")
    for low, size in stages():
        pieces = pieces_of(block, low, size, me)
        come = [exchange(pieces[m], m << low) for m in range(len(pieces) - 1, 0, -1)]
        block = sum(come, pieces[0])
    copies = [send(block, HUB, other) for other in range(lax.axis_size("inner")) if other != HUB]
    block = jnp.where(place == HUB, block, sum(copies))
    for low, size in reversed(stages()):
        pieces = [block] + [None] * ((1 << size) - 1)
        for m in range(len(pieces) - 1, 0, -1):
            pieces[m] = exchange(block, m << low)
        for bit in range(size):
            swap = ((me >> (low + bit)) & 1) == 1
            pieces = [jnp.where(swap, pieces[m ^ (1 << bit)], pieces[m]) for m in range(len(pieces))]
        block = jnp.concatenate(pieces, axis=0)
    return block


def on_device(
    trial_count_per_study,
    study_tile_mask,
    sep_order,
    stacked_study_factor,
    diagonal_block_inverses,
    coupling,
    targets,
    sep_prior,
):
    place = lax.axis_index("inner")
    slots = diagonal_block_inverses.shape[0]
    width = sep_prior.shape[0]
    tile = width // study_tile_mask.shape[1]
    wide = width + targets.shape[1]
    reach = (lax.axis_size("inner") - 1) * slots
    order = sep_order[None, :]
    left = (width // tile + 1) // 2 * tile
    own = call(
        own_kernel,
        "own",
        floats(slots, wide),
        [SMEM] + [HBM] * 5,
        6 * slots * slots * wide,
        [
            pltpu.SMEM((1, width // tile), jnp.int32),
            pltpu.VMEM((1, width), jnp.int32),
            pltpu.VMEM((slots, slots), jnp.float32),
            pltpu.VMEM((slots, width), jnp.float32),
            pltpu.VMEM((slots, wide - width), jnp.float32),
            pltpu.SemaphoreType.DMA((5,)),
        ],
    )(
        trial_count_per_study,
        *in_hbm(study_tile_mask, order, diagonal_block_inverses, coupling, targets),
    )
    first, rest, last = call(
        steps_kernel,
        "steps",
        tuple(floats(slots, size) for size in (slots + left, wide - left, reach + left)),
        [SMEM] + [VMEM] * 3,
        6 * slots * slots * reach,
    )(trial_count_per_study, diagonal_block_inverses, stacked_study_factor, own)
    first_1 = send(first, 1, HUB)
    own_0 = send(own, 0, HUB)
    rest_1 = send(rest, 1, HUB)
    last_3 = send(last, 3, HUB)
    rest_3 = send(rest, 3, HUB)
    prior = call(prior_kernel, "prior", floats(width, width), [VMEM, VMEM, ANY], 36 * width**3)(
        order, sep_prior, own_0
    )
    packed = packed_tiles(width, tile)[1] * tile + 8

    def halves(*shape):
        return jax.ShapeDtypeStruct(shape, jnp.bfloat16)

    early = call(
        functools.partial(early_kernel, tile),
        "early",
        (
            halves(reach, left),
            halves(reach, left),
            floats(reach, wide - left),
            halves(2 * slots, slots),
            halves(2 * slots, slots),
            floats(packed, tile),
        ),
        [HBM] * 3 + [VMEM, VMEM, ANY],
        60 * slots * wide * (6 * slots + width),
        [
            pltpu.VMEM((slots, reach + left), jnp.float32),
            pltpu.VMEM((slots, wide), jnp.float32),
            pltpu.VMEM((slots, slots + left), jnp.float32),
            pltpu.SemaphoreType.DMA((3,)),
        ],
    )(*in_hbm(last_3, own_0, first_1), last, rest, prior)
    unit = 8 * lax.axis_size("study")
    padded = -(-packed // unit) * unit
    rows = call(
        functools.partial(gram_kernel, tile),
        "gram",
        floats(padded, tile),
        [HBM] * 2 + [VMEM] * 6,
        6 * slots * wide * (2 * slots + 3 * width),
        [
            pltpu.VMEM((slots, wide - left), jnp.float32),
            pltpu.VMEM((slots, wide - left), jnp.float32),
            pltpu.SemaphoreType.DMA((2,)),
        ],
    )(*in_hbm(rest_1, rest_3), *early)
    total = total_over_studies(rows, place)
    return call(
        factor_kernel,
        "factor_and_solve",
        (floats(width, width), floats(width, tile)),
        [VMEM, VMEM],
        width**3,
        [
            pltpu.VMEM((width, wide), jnp.float32),
            pltpu.VMEM((width, wide), jnp.float32),
            pltpu.VMEM((width, width), jnp.float32),
            pltpu.SemaphoreType.DMA((width // tile, 2)),
        ],
        out_spec=HBM,
    )(total, prior)


def solution(mesh):
    return jax.shard_map(
        on_device,
        mesh=mesh,
        in_specs=(
            P("study"),
            P("study", None),
            P(),
            P(("study", "inner"), None),
            P(("study", "inner"), None),
            P(("study", "inner"), None),
            P(("study", "inner"), None),
            P(),
        ),
        out_specs=(P(), P()),
        check_vma=False,
    )
```

```python
import functools

import jax
import jax.numpy as jnp
from jax import lax
from jax.experimental import pallas as pl
from jax.experimental.pallas import tpu as pltpu
from jax.sharding import PartitionSpec as P

HIGHEST = lax.Precision.HIGHEST
HUB = 2
SPREAD = 16


NN = (((1,), (0,)), ((), ()))
TN = (((0,), (0,)), ((), ()))
VMEM = pl.BlockSpec(memory_space=pltpu.VMEM)
SMEM = pl.BlockSpec(memory_space=pltpu.SMEM)
ANY = pl.BlockSpec(memory_space=pl.ANY)
HBM = pl.BlockSpec(memory_space=pltpu.HBM)


def call(kernel, name, out_shape, in_specs, flops, scratch_shapes=(), out_spec=VMEM):
    many = isinstance(out_shape, tuple)
    return pl.pallas_call(
        kernel,
        out_shape=out_shape,
        in_specs=in_specs,
        out_specs=(out_spec,) * len(out_shape) if many else out_spec,
        scratch_shapes=scratch_shapes,
        cost_estimate=pl.CostEstimate(flops=flops, bytes_accessed=1 << 20, transcendentals=0),
        compiler_params=pltpu.CompilerParams(vmem_limit_bytes=16 << 20),
        name=name,
    )


def floats(*shape):
    return jax.ShapeDtypeStruct(shape, jnp.float32)


def in_hbm(*arrays):
    return [pltpu.with_memory_space_constraint(array, pltpu.HBM) for array in arrays]


def split(x):
    high = x.astype(jnp.bfloat16)
    return high, (x - high.astype(jnp.float32)).astype(jnp.bfloat16)


def product(a, b, dims=NN):
    def one(x, y):
        return lax.dot_general(x, y, dims, preferred_element_type=jnp.float32)

    return one(a[0], b[0]) + (one(a[0], b[1]) + one(a[1], b[0]))


def exchange(block, mask):
    count = lax.axis_size("study")
    return lax.ppermute(block, "study", [(i, i ^ mask) for i in range(count)])


def send(block, source, target):
    return lax.ppermute(block, "inner", [(source, target)])


def packed_tiles(width, tile):
    places, used = {}, 0
    for i in range(width // tile):
        for j in range(i, width // tile + 1):
            if i == j and i % 2:
                places[i, j] = places[i - 1, i - 1]
            else:
                places[i, j] = used
                used += 1
    return {ij: slice(k * tile, (k + 1) * tile) for ij, k in places.items()}, used


def grid_of(tile):
    return tuple(lax.broadcasted_iota(jnp.int32, (tile, tile), axis) for axis in range(2))


def eliminate(block, behind, lane, tile):
    wide = block.shape[1]
    row = lax.broadcasted_iota(jnp.int32, (8, 1), 0)
    groups = [rows[8 * g : 8 * g + 8] for rows in (block, behind) if rows is not None for g in range(SPREAD // 8)]
    spread = [[jnp.broadcast_to(rows[:, lane + k : lane + k + 1], (8, tile)) for rows in groups] for k in range(SPREAD)]
    final = []
    for i in range(SPREAD):
        group, line = divmod(i, 8)
        scale = lax.rsqrt(spread[i][group][line : line + 1])
        final.append(groups[group][line : line + 1] * jnp.tile(scale, (1, wide // tile)))
        below = {g: spread[i][g] * scale for g in range(group, len(groups))}
        below[group] = jnp.where(row > line, below[group], 0.0)
        if line == 7:
            del below[group]
        for k in range(i + 1, SPREAD):
            factor = spread[k][group][line : line + 1] * scale
            for g in below:
                spread[k][g] = spread[k][g] - below[g] * factor
        for g in below:
            groups[g] = groups[g] - jnp.tile(below[g], (1, wide // tile)) * final[-1]
    final = jnp.concatenate(final, axis=0)
    return final, None if behind is None else jnp.concatenate(groups[SPREAD // 8 :], axis=0)


def factor_kernel(total_ref, prior_ref, factor_hbm, solve_hbm, upper_ref, work_ref, factor_ref, sems):
    width = prior_ref.shape[0]
    tile = work_ref.shape[1] - width
    count = width // tile
    place, used = packed_tiles(width, tile)
    row, column = grid_of(tile)
    upper = row <= column
    cut = [slice(i * tile, (i + 1) * tile) for i in range(count + 1)]

    def given(i, j):
        block = total_ref[place[i, j]]
        if i == j and i % 2:
            at = used * tile + i // 2
            block = jnp.where(upper, jnp.where(row == column, total_ref[at : at + 1], block.T), block)
        elif i == j:
            block = jnp.where(upper, block, block.T)
        return block + prior_ref[cut[i], cut[j]] if j < count else block

    def given_row(i):
        return jnp.concatenate([given(i, j) for j in range(i, count + 1)], axis=1)

    copies = []
    work_ref[cut[0]] = given_row(0)
    for i in range(count):
        base = i * tile
        ready = work_ref[base : base + SPREAD, base:]
        behind = work_ref[base + SPREAD : base + 2 * SPREAD, base:]
        for start in range(0, tile, SPREAD):
            final, ready = eliminate(ready, behind, start, tile)
            upper_ref[base + start : base + start + SPREAD, base:] = final
            after, rest, behind = start + 2 * SPREAD, start + 3 * SPREAD, None
            if after < tile:
                final = split(final)
                behind = work_ref[base + after : base + rest, base:] - product(columns(final, after, rest), final, TN)
            if rest < tile:
                later = slice(base + rest, base + tile)
                work_ref[later, base:] = work_ref[later, base:] - product(columns(final, rest, tile), final, TN)
        final = split(upper_ref[cut[i], base:])
        for k in range(i + 1, count):
            at = (k - i) * tile
            old = work_ref[cut[k], k * tile :] if i else given_row(k)
            step = product(columns(final, at, at + tile), columns(final, at, width + tile - base), TN)
            work_ref[cut[k], k * tile :] = old - step
        for j in range(count):
            if j < i:
                factor_ref[cut[j], cut[i]] = jnp.zeros((tile, tile), jnp.float32)
            else:
                block = upper_ref[cut[i], cut[j]]
                factor_ref[cut[j], cut[i]] = (jnp.where(upper, block, 0.0) if i == j else block).T
        copies += copy_all(
            (factor_ref.at[:, cut[i]], upper_ref.at[cut[i], width:]),
            (factor_hbm.at[:, cut[i]], solve_hbm.at[cut[i]]),
            sems.at[i],
        )
    for copy in copies:
        copy.wait()


def live_inverse(count_ref, inverse):
    slots = inverse.shape[0]
    place, places = lax.axis_index("inner"), lax.axis_size("inner")

    def live(shape, axis):
        position = lax.broadcasted_iota(jnp.int32, shape, axis) * places + place
        return (position < count_ref[0]).astype(jnp.float32)

    return inverse * live((slots, 1), 0) * live((1, slots), 1)


def picker(order_ref):
    width = order_ref.shape[1]
    return (lax.broadcasted_iota(jnp.int32, (width, width), 0) == order_ref[...]).astype(jnp.float32)


def copy_all(sources, targets, sems):
    copies = [pltpu.make_async_copy(source, target, sems.at[k]) for k, (source, target) in enumerate(zip(sources, targets))]
    for copy in copies:
        copy.start()
    return copies


def own_kernel(count_ref, mask_hbm, order_hbm, inverse_hbm, coupling_hbm, targets_hbm, own_ref, *refs):
    sources = (mask_hbm, order_hbm, inverse_hbm, coupling_hbm, targets_hbm)
    targets, sems = refs[:5], refs[5]
    mask_ref, order_ref, inverse_ref, coupling_ref, targets_ref = targets
    width, tile = coupling_ref.shape[1], coupling_ref.shape[1] // mask_ref.shape[1]
    copies = copy_all(sources, targets, sems)
    for copy in copies[:2]:
        copy.wait()
    lane_tile = lax.broadcasted_iota(jnp.int32, (1, width), 1) // tile
    column_mask = jnp.zeros((1, width), jnp.float32)
    for t in range(width // tile):
        column_mask = jnp.where(lane_tile == t, mask_ref[0, t].astype(jnp.float32), column_mask)
    pick = picker(order_ref).astype(jnp.bfloat16)

    def ordered(x):
        return lax.dot_general(x, pick, NN, preferred_element_type=jnp.float32).astype(jnp.bfloat16)

    copies[2].wait()
    inverse = split(live_inverse(count_ref, inverse_ref[...]))
    copies[3].wait()
    high, low = split(coupling_ref[...] * column_mask)
    own_ref[:, :width] = product(inverse, (ordered(high), ordered(low)))
    copies[4].wait()
    own_ref[:, width:] = product(inverse, split(targets_ref[...]))


def steps_kernel(count_ref, inverse_ref, factor_ref, own_ref, first_ref, rest_ref, last_ref):
    slots = inverse_ref.shape[0]
    left = first_ref.shape[1] - slots
    reach = last_ref.shape[1] - left
    inverse = split(-live_inverse(count_ref, inverse_ref[...]))
    steps = product(inverse, split(factor_ref[:, :reach]))
    first_ref[:, :slots] = steps[:, :slots]
    last_ref[:, :reach] = steps
    first_ref[:, slots:] = own_ref[:, :left]
    last_ref[:, reach:] = own_ref[:, :left]
    rest_ref[...] = own_ref[:, left:]


def prior_kernel(order_ref, prior_ref, after_ref, ordered_ref):
    pick = picker(order_ref)
    rows = lax.dot_general(pick, prior_ref[...], TN, precision=HIGHEST, preferred_element_type=jnp.float32)
    ordered_ref[...] = jnp.dot(rows, pick, precision=HIGHEST, preferred_element_type=jnp.float32)


def put_tiles(block, top, side, rows_ref, tile, count, add_ref=None):
    place, used = packed_tiles(count * tile, tile)
    row, column = grid_of(tile)

    def piece(i, j):
        a, b = (i - top) * tile, (j - side) * tile
        return block[a : a + tile, b : b + tile]

    def put(rows, value):
        rows_ref[rows] = value if add_ref is None else value + add_ref[rows]

    stop = top + block.shape[0] // tile
    for i in range(top, stop):
        for j in range(max(i, side), side + block.shape[1] // tile):
            if i != j:
                put(place[i, j], piece(i, j))
            elif i % 2:
                at = used * tile + i // 2
                put(slice(at, at + 1), jnp.sum(jnp.where(row == column, piece(i, i), 0.0), axis=0, keepdims=True))
                if i == top:
                    rows = place[i, i]
                    old = rows_ref[rows] if add_ref is None else add_ref[rows]
                    rows_ref[rows] = jnp.where(row <= column, old, piece(i, i) if add_ref is None else old + piece(i, i))
            else:
                put(place[i, i], jnp.where(row <= column, piece(i, i), piece(i + 1, i + 1)) if i + 1 < stop else piece(i, i))


def stack(pairs):
    return tuple(jnp.concatenate([pair[side] for pair in pairs], axis=0) for side in range(2))


def columns(pair, start, stop):
    return pair[0][:, start:stop], pair[1][:, start:stop]


def early_kernel(tile, last_hbm, own_0_hbm, first_hbm, own_last_ref, own_rest_ref, prior_ref, *refs):
    high_ref, low_ref, base_ref, chain_high_ref, chain_low_ref, rows_ref = refs[:6]
    targets, sems = refs[6:9], refs[9]
    last_ref, own_0_ref, first_ref = targets
    slots, wide = own_0_ref.shape
    left = first_ref.shape[1] - slots
    reach = last_ref.shape[1] - left
    count = wide // tile - 1
    copies = copy_all((last_hbm, own_0_hbm, first_hbm), targets, sems)
    cut = [slice(k * slots, (k + 1) * slots) for k in range(3)]
    for copy in copies[1:]:
        copy.wait()
    solved_0 = split(own_0_ref[...])
    part_1 = product(split(first_ref[:, :slots]), solved_0)
    part_1 = jnp.concatenate([part_1[:, :left] + first_ref[:, slots:], part_1[:, left:]], axis=1)
    known = stack([solved_0, split(part_1)])
    step_21 = split(own_last_ref[:, cut[1]])
    part_2 = jnp.concatenate([own_last_ref[:, reach:], own_rest_ref[...]], axis=1)
    part_2 = part_2 + product(split(own_last_ref[:, : 2 * slots]), known)
    copies[0].wait()
    known = stack([known, split(part_2)])
    part_3 = product(split(last_ref[:, :reach]), known)
    part_3 = jnp.concatenate([part_3[:, :left] + last_ref[:, reach:], part_3[:, left:]], axis=1)
    known = stack([known, split(part_3)])
    chain_high_ref[:slots], chain_low_ref[:slots] = step_21
    chain_high_ref[slots:], chain_low_ref[slots:] = split(last_ref[:, cut[1]] + product(split(last_ref[:, cut[2]]), step_21))
    for k, part in enumerate((part_1, part_2, part_3)):
        base_ref[k * slots : (k + 1) * slots] = part[:, left:]
    high_ref[...], low_ref[...] = known[0][slots:, :left], known[1][slots:, :left]
    at = left // tile
    put_tiles(product(columns(known, 0, left), columns(known, 0, left), TN), 0, 0, rows_ref, tile, count)
    put_tiles(product(columns(solved_0, 0, left), columns(solved_0, left, wide), TN), 0, at, rows_ref, tile, count)
    put_tiles(product(columns(solved_0, left, count * tile), columns(solved_0, left, wide), TN), at, at, rows_ref, tile, count)


def gram_kernel(tile, rest_hbm, rest_3_hbm, high_ref, low_ref, base_ref, chain_high_ref, chain_low_ref, early_ref, *refs):
    rows_ref, rest_ref, rest_3_ref, sems = refs
    slots, wide = rest_ref.shape
    left = high_ref.shape[1]
    count = (left + wide) // tile - 1
    at = left // tile
    copies = copy_all((rest_hbm, rest_3_hbm), (rest_ref, rest_3_ref), sems)
    place, used = packed_tiles(count * tile, tile)
    rows_ref[used * tile :] = jnp.zeros((rows_ref.shape[0] - used * tile, tile), jnp.float32)
    done = [place[i, j] for i in range(at) for j in range(i, at) if i < j or i % 2 == 0]
    for rows in done + [slice(used * tile + i // 2, used * tile + i // 2 + 1) for i in range(1, at, 2)]:
        rows_ref[rows] = early_ref[rows]
    for copy in copies:
        copy.wait()
    rest = rest_ref[...]
    step = product((chain_high_ref[...], chain_low_ref[...]), split(rest))
    right = jnp.concatenate([rest, step[:slots], step[slots:] + rest_3_ref[...]], axis=0)
    right = split(base_ref[...] + right)
    put_tiles(product((high_ref[...], low_ref[...]), right, TN), 0, at, rows_ref, tile, count, early_ref)
    put_tiles(product(columns(right, 0, count * tile - left), right, TN), at, at, rows_ref, tile, count, early_ref)


def stages():
    bits = (lax.axis_size("study") - 1).bit_length()
    return [(0, 1)] + [(low, min(2, bits - low)) for low in range(1, bits, 2)]


def pieces_of(block, low, size, me):
    count = 1 << size
    mine = (me >> low) & (count - 1)
    parts = block.reshape(count, block.shape[0] // count, block.shape[1])
    return [lax.dynamic_index_in_dim(parts, mine ^ m, 0, keepdims=False) for m in range(count)]


def total_over_studies(block, place):
    me = lax.axis_index("study")
    for low, size in stages():
        pieces = pieces_of(block, low, size, me)
        come = [exchange(pieces[m], m << low) for m in range(len(pieces) - 1, 0, -1)]
        block = sum(come, pieces[0])
    copies = [send(block, HUB, other) for other in range(lax.axis_size("inner")) if other != HUB]
    block = jnp.where(place == HUB, block, sum(copies))
    for low, size in reversed(stages()):
        pieces = [block] + [None] * ((1 << size) - 1)
        for m in range(len(pieces) - 1, 0, -1):
            pieces[m] = exchange(block, m << low)
        for bit in range(size):
            swap = ((me >> (low + bit)) & 1) == 1
            pieces = [jnp.where(swap, pieces[m ^ (1 << bit)], pieces[m]) for m in range(len(pieces))]
        block = jnp.concatenate(pieces, axis=0)
    return block


def on_device(
    trial_count_per_study,
    study_tile_mask,
    sep_order,
    stacked_study_factor,
    diagonal_block_inverses,
    coupling,
    targets,
    sep_prior,
):
    place = lax.axis_index("inner")
    slots = diagonal_block_inverses.shape[0]
    width = sep_prior.shape[0]
    tile = width // study_tile_mask.shape[1]
    wide = width + targets.shape[1]
    reach = (lax.axis_size("inner") - 1) * slots
    order = sep_order[None, :]
    left = width - tile
    own = call(
        own_kernel,
        "own",
        floats(slots, wide),
        [SMEM] + [HBM] * 5,
        6 * slots * slots * wide,
        [
            pltpu.SMEM((1, width // tile), jnp.int32),
            pltpu.VMEM((1, width), jnp.int32),
            pltpu.VMEM((slots, slots), jnp.float32),
            pltpu.VMEM((slots, width), jnp.float32),
            pltpu.VMEM((slots, wide - width), jnp.float32),
            pltpu.SemaphoreType.DMA((5,)),
        ],
    )(
        trial_count_per_study,
        *in_hbm(study_tile_mask, order, diagonal_block_inverses, coupling, targets),
    )
    first, rest, last = call(
        steps_kernel,
        "steps",
        tuple(floats(slots, size) for size in (slots + left, wide - left, reach + left)),
        [SMEM] + [VMEM] * 3,
        6 * slots * slots * reach,
    )(trial_count_per_study, diagonal_block_inverses, stacked_study_factor, own)
    first_1 = send(first, 1, HUB)
    own_0 = send(own, 0, HUB)
    rest_1 = send(rest, 1, HUB)
    last_3 = send(last, 3, HUB)
    rest_3 = send(rest, 3, HUB)
    prior = call(prior_kernel, "prior", floats(width, width), [VMEM, VMEM, ANY], 44 * width**3)(
        order, sep_prior, own_0
    )
    packed = packed_tiles(width, tile)[1] * tile + 8

    def halves(*shape):
        return jax.ShapeDtypeStruct(shape, jnp.bfloat16)

    early = call(
        functools.partial(early_kernel, tile),
        "early",
        (
            halves(reach, left),
            halves(reach, left),
            floats(reach, wide - left),
            halves(2 * slots, slots),
            halves(2 * slots, slots),
            floats(packed, tile),
        ),
        [HBM] * 3 + [VMEM, VMEM, ANY],
        60 * slots * wide * (6 * slots + width),
        [
            pltpu.VMEM((slots, reach + left), jnp.float32),
            pltpu.VMEM((slots, wide), jnp.float32),
            pltpu.VMEM((slots, slots + left), jnp.float32),
            pltpu.SemaphoreType.DMA((3,)),
        ],
    )(*in_hbm(last_3, own_0, first_1), last, rest, prior)
    unit = 8 * lax.axis_size("study")
    padded = -(-packed // unit) * unit
    rows = call(
        functools.partial(gram_kernel, tile),
        "gram",
        floats(padded, tile),
        [HBM] * 2 + [VMEM] * 6,
        6 * slots * wide * (2 * slots + 3 * width),
        [
            pltpu.VMEM((slots, wide - left), jnp.float32),
            pltpu.VMEM((slots, wide - left), jnp.float32),
            pltpu.SemaphoreType.DMA((2,)),
        ],
    )(*in_hbm(rest_1, rest_3), *early)
    total = total_over_studies(rows, place)
    return call(
        factor_kernel,
        "factor_and_solve",
        (floats(width, width), floats(width, tile)),
        [VMEM, VMEM],
        width**3,
        [
            pltpu.VMEM((width, wide), jnp.float32),
            pltpu.VMEM((width, wide), jnp.float32),
            pltpu.VMEM((width, width), jnp.float32),
            pltpu.SemaphoreType.DMA((width // tile, 2)),
        ],
        out_spec=HBM,
    )(total, prior)


def solution(mesh):
    return jax.shard_map(
        on_device,
        mesh=mesh,
        in_specs=(
            P("study"),
            P("study", None),
            P(),
            P(("study", "inner"), None),
            P(("study", "inner"), None),
            P(("study", "inner"), None),
            P(("study", "inner"), None),
            P(),
        ),
        out_specs=(P(), P()),
        check_vma=False,
    )
```

```python
import functools

import jax
import jax.numpy as jnp
from jax import lax
from jax.experimental import pallas as pl
from jax.experimental.pallas import tpu as pltpu
from jax.sharding import PartitionSpec as P

HIGHEST = lax.Precision.HIGHEST
HUB = 2
SPREAD = 16


NN = (((1,), (0,)), ((), ()))
TN = (((0,), (0,)), ((), ()))
VMEM = pl.BlockSpec(memory_space=pltpu.VMEM)
SMEM = pl.BlockSpec(memory_space=pltpu.SMEM)
ANY = pl.BlockSpec(memory_space=pl.ANY)
HBM = pl.BlockSpec(memory_space=pltpu.HBM)


def call(kernel, name, out_shape, in_specs, flops, scratch_shapes=(), out_spec=VMEM):
    many = isinstance(out_shape, tuple)
    return pl.pallas_call(
        kernel,
        out_shape=out_shape,
        in_specs=in_specs,
        out_specs=(out_spec,) * len(out_shape) if many else out_spec,
        scratch_shapes=scratch_shapes,
        cost_estimate=pl.CostEstimate(flops=flops, bytes_accessed=1 << 20, transcendentals=0),
        compiler_params=pltpu.CompilerParams(vmem_limit_bytes=16 << 20),
        name=name,
    )


def floats(*shape):
    return jax.ShapeDtypeStruct(shape, jnp.float32)


def in_hbm(*arrays):
    return [pltpu.with_memory_space_constraint(array, pltpu.HBM) for array in arrays]


def split(x):
    high = x.astype(jnp.bfloat16)
    return high, (x - high.astype(jnp.float32)).astype(jnp.bfloat16)


def product(a, b, dims=NN):
    def one(x, y):
        return lax.dot_general(x, y, dims, preferred_element_type=jnp.float32)

    return one(a[0], b[0]) + (one(a[0], b[1]) + one(a[1], b[0]))


def exchange(block, mask):
    count = lax.axis_size("study")
    return lax.ppermute(block, "study", [(i, i ^ mask) for i in range(count)])


def send(block, source, target):
    return lax.ppermute(block, "inner", [(source, target)])


def packed_tiles(width, tile):
    places, used = {}, 0
    for i in range(width // tile):
        for j in range(i, width // tile + 1):
            if i == j and i % 2:
                places[i, j] = places[i - 1, i - 1]
            else:
                places[i, j] = used
                used += 1
    return {ij: slice(k * tile, (k + 1) * tile) for ij, k in places.items()}, used


def grid_of(tile):
    return tuple(lax.broadcasted_iota(jnp.int32, (tile, tile), axis) for axis in range(2))


def eliminate(block, behind, lane, tile):
    wide = block.shape[1]
    row = lax.broadcasted_iota(jnp.int32, (8, 1), 0)
    groups = [rows[8 * g : 8 * g + 8] for rows in (block, behind) if rows is not None for g in range(SPREAD // 8)]
    spread = [[jnp.broadcast_to(rows[:, lane + k : lane + k + 1], (8, tile)) for rows in groups] for k in range(SPREAD)]
    final = []
    for i in range(SPREAD):
        group, line = divmod(i, 8)
        scale = lax.rsqrt(spread[i][group][line : line + 1])
        final.append(groups[group][line : line + 1] * jnp.tile(scale, (1, wide // tile)))
        below = {g: spread[i][g] * scale for g in range(group, len(groups))}
        below[group] = jnp.where(row > line, below[group], 0.0)
        if line == 7:
            del below[group]
        for k in range(i + 1, SPREAD):
            factor = spread[k][group][line : line + 1] * scale
            for g in below:
                spread[k][g] = spread[k][g] - below[g] * factor
        for g in below:
            groups[g] = groups[g] - jnp.tile(below[g], (1, wide // tile)) * final[-1]
    final = jnp.concatenate(final, axis=0)
    return final, None if behind is None else jnp.concatenate(groups[SPREAD // 8 :], axis=0)


def factor_kernel(total_ref, prior_ref, factor_hbm, solve_hbm, upper_ref, work_ref, factor_ref, sems):
    width = prior_ref.shape[0]
    tile = work_ref.shape[1] - width
    count = width // tile
    place, used = packed_tiles(width, tile)
    row, column = grid_of(tile)
    upper = row <= column
    cut = [slice(i * tile, (i + 1) * tile) for i in range(count + 1)]

    def given(i, j):
        block = total_ref[place[i, j]]
        if i == j and i % 2:
            at = used * tile + i // 2
            block = jnp.where(upper, jnp.where(row == column, total_ref[at : at + 1], block.T), block)
        elif i == j:
            block = jnp.where(upper, block, block.T)
        return block + prior_ref[cut[i], cut[j]] if j < count else block

    def given_row(i):
        return jnp.concatenate([given(i, j) for j in range(i, count + 1)], axis=1)

    copies = []
    work_ref[cut[0]] = given_row(0)
    for i in range(count):
        base = i * tile
        ready = work_ref[base : base + SPREAD, base:]
        behind = work_ref[base + SPREAD : base + 2 * SPREAD, base:]
        for start in range(0, tile, SPREAD):
            final, ready = eliminate(ready, behind, start, tile)
            upper_ref[base + start : base + start + SPREAD, base:] = final
            after, rest, behind = start + 2 * SPREAD, start + 3 * SPREAD, None
            if after < tile:
                final = split(final)
                behind = work_ref[base + after : base + rest, base:] - product(columns(final, after, rest), final, TN)
            if rest < tile:
                later = slice(base + rest, base + tile)
                work_ref[later, base:] = work_ref[later, base:] - product(columns(final, rest, tile), final, TN)
        final = split(upper_ref[cut[i], base:])
        for k in range(i + 1, count):
            at = (k - i) * tile
            old = work_ref[cut[k], k * tile :] if i else given_row(k)
            step = product(columns(final, at, at + tile), columns(final, at, width + tile - base), TN)
            work_ref[cut[k], k * tile :] = old - step
        for j in range(count):
            if j < i:
                factor_ref[cut[j], cut[i]] = jnp.zeros((tile, tile), jnp.float32)
            else:
                block = upper_ref[cut[i], cut[j]]
                factor_ref[cut[j], cut[i]] = (jnp.where(upper, block, 0.0) if i == j else block).T
        copies += copy_all(
            (factor_ref.at[:, cut[i]], upper_ref.at[cut[i], width:]),
            (factor_hbm.at[:, cut[i]], solve_hbm.at[cut[i]]),
            sems.at[i],
        )
    for copy in copies:
        copy.wait()


def live_inverse(count_ref, inverse):
    slots = inverse.shape[0]
    place, places = lax.axis_index("inner"), lax.axis_size("inner")

    def live(shape, axis):
        position = lax.broadcasted_iota(jnp.int32, shape, axis) * places + place
        return (position < count_ref[0]).astype(jnp.float32)

    return inverse * live((slots, 1), 0) * live((1, slots), 1)


def picker(order_ref):
    width = order_ref.shape[1]
    return (lax.broadcasted_iota(jnp.int32, (width, width), 0) == order_ref[...]).astype(jnp.float32)


def copy_all(sources, targets, sems):
    copies = [pltpu.make_async_copy(source, target, sems.at[k]) for k, (source, target) in enumerate(zip(sources, targets))]
    for copy in copies:
        copy.start()
    return copies


def own_kernel(count_ref, mask_hbm, order_hbm, inverse_hbm, coupling_hbm, targets_hbm, own_ref, *refs):
    sources = (mask_hbm, order_hbm, inverse_hbm, coupling_hbm, targets_hbm)
    targets, sems = refs[:5], refs[5]
    mask_ref, order_ref, inverse_ref, coupling_ref, targets_ref = targets
    width, tile = coupling_ref.shape[1], coupling_ref.shape[1] // mask_ref.shape[1]
    copies = copy_all(sources, targets, sems)
    for copy in copies[:2]:
        copy.wait()
    lane_tile = lax.broadcasted_iota(jnp.int32, (1, width), 1) // tile
    column_mask = jnp.zeros((1, width), jnp.float32)
    for t in range(width // tile):
        column_mask = jnp.where(lane_tile == t, mask_ref[0, t].astype(jnp.float32), column_mask)
    pick = picker(order_ref).astype(jnp.bfloat16)

    def ordered(x):
        return lax.dot_general(x, pick, NN, preferred_element_type=jnp.float32).astype(jnp.bfloat16)

    copies[2].wait()
    inverse = split(live_inverse(count_ref, inverse_ref[...]))
    copies[3].wait()
    high, low = split(coupling_ref[...] * column_mask)
    own_ref[:, :width] = product(inverse, (ordered(high), ordered(low)))
    copies[4].wait()
    own_ref[:, width:] = product(inverse, split(targets_ref[...]))


def steps_kernel(count_ref, inverse_ref, factor_ref, own_ref, first_ref, rest_ref, last_ref):
    slots = inverse_ref.shape[0]
    left = first_ref.shape[1] - slots
    reach = last_ref.shape[1] - left
    inverse = split(-live_inverse(count_ref, inverse_ref[...]))
    steps = product(inverse, split(factor_ref[:, :reach]))
    first_ref[:, :slots] = steps[:, :slots]
    last_ref[:, :reach] = steps
    first_ref[:, slots:] = own_ref[:, :left]
    last_ref[:, reach:] = own_ref[:, :left]
    rest_ref[...] = own_ref[:, left:]


def prior_kernel(order_ref, prior_ref, after_ref, ordered_ref):
    pick = picker(order_ref)
    rows = lax.dot_general(pick, prior_ref[...], TN, precision=HIGHEST, preferred_element_type=jnp.float32)
    ordered_ref[...] = jnp.dot(rows, pick, precision=HIGHEST, preferred_element_type=jnp.float32)


def put_tiles(block, top, side, rows_ref, tile, count, add_ref=None):
    place, used = packed_tiles(count * tile, tile)
    row, column = grid_of(tile)

    def piece(i, j):
        a, b = (i - top) * tile, (j - side) * tile
        return block[a : a + tile, b : b + tile]

    def put(rows, value):
        rows_ref[rows] = value if add_ref is None else value + add_ref[rows]

    stop = top + block.shape[0] // tile
    for i in range(top, stop):
        for j in range(max(i, side), side + block.shape[1] // tile):
            if i != j:
                put(place[i, j], piece(i, j))
            elif i % 2:
                at = used * tile + i // 2
                put(slice(at, at + 1), jnp.sum(jnp.where(row == column, piece(i, i), 0.0), axis=0, keepdims=True))
                if i == top:
                    rows = place[i, i]
                    old = rows_ref[rows] if add_ref is None else add_ref[rows]
                    rows_ref[rows] = jnp.where(row <= column, old, piece(i, i) if add_ref is None else old + piece(i, i))
            else:
                put(place[i, i], jnp.where(row <= column, piece(i, i), piece(i + 1, i + 1)) if i + 1 < stop else piece(i, i))


def stack(pairs):
    return tuple(jnp.concatenate([pair[side] for pair in pairs], axis=0) for side in range(2))


def columns(pair, start, stop):
    return pair[0][:, start:stop], pair[1][:, start:stop]


def early_kernel(tile, last_hbm, own_0_hbm, first_hbm, own_last_ref, own_rest_ref, prior_ref, *refs):
    high_ref, low_ref, base_ref, chain_high_ref, chain_low_ref, rows_ref = refs[:6]
    targets, sems = refs[6:9], refs[9]
    last_ref, own_0_ref, first_ref = targets
    slots, wide = own_0_ref.shape
    left = first_ref.shape[1] - slots
    reach = last_ref.shape[1] - left
    count = wide // tile - 1
    copies = copy_all((last_hbm, own_0_hbm, first_hbm), targets, sems)
    cut = [slice(k * slots, (k + 1) * slots) for k in range(3)]
    for copy in copies[1:]:
        copy.wait()
    solved_0 = split(own_0_ref[...])
    part_1 = product(split(first_ref[:, :slots]), solved_0)
    part_1 = jnp.concatenate([part_1[:, :left] + first_ref[:, slots:], part_1[:, left:]], axis=1)
    known = stack([solved_0, split(part_1)])
    step_21 = split(own_last_ref[:, cut[1]])
    part_2 = jnp.concatenate([own_last_ref[:, reach:], own_rest_ref[...]], axis=1)
    part_2 = part_2 + product(split(own_last_ref[:, : 2 * slots]), known)
    copies[0].wait()
    known = stack([known, split(part_2)])
    part_3 = product(split(last_ref[:, :reach]), known)
    part_3 = jnp.concatenate([part_3[:, :left] + last_ref[:, reach:], part_3[:, left:]], axis=1)
    known = stack([known, split(part_3)])
    chain_high_ref[:slots], chain_low_ref[:slots] = step_21
    chain_high_ref[slots:], chain_low_ref[slots:] = split(last_ref[:, cut[1]] + product(split(last_ref[:, cut[2]]), step_21))
    for k, part in enumerate((part_1, part_2, part_3)):
        base_ref[k * slots : (k + 1) * slots] = part[:, left:]
    high_ref[...], low_ref[...] = known[0][slots:, :left], known[1][slots:, :left]
    at = left // tile
    put_tiles(product(columns(known, 0, left), columns(known, 0, left), TN), 0, 0, rows_ref, tile, count)
    put_tiles(product(columns(solved_0, 0, left), columns(solved_0, left, wide), TN), 0, at, rows_ref, tile, count)
    put_tiles(product(columns(solved_0, left, count * tile), columns(solved_0, left, wide), TN), at, at, rows_ref, tile, count)


def gram_kernel(tile, rest_hbm, rest_3_hbm, high_ref, low_ref, base_ref, chain_high_ref, chain_low_ref, early_ref, *refs):
    rows_ref, rest_ref, rest_3_ref, sems = refs
    slots, wide = rest_ref.shape
    left = high_ref.shape[1]
    count = (left + wide) // tile - 1
    at = left // tile
    copies = copy_all((rest_hbm, rest_3_hbm), (rest_ref, rest_3_ref), sems)
    place, used = packed_tiles(count * tile, tile)
    rows_ref[used * tile :] = jnp.zeros((rows_ref.shape[0] - used * tile, tile), jnp.float32)
    done = [place[i, j] for i in range(at) for j in range(i, at) if i < j or i % 2 == 0]
    for rows in done + [slice(used * tile + i // 2, used * tile + i // 2 + 1) for i in range(1, at, 2)]:
        rows_ref[rows] = early_ref[rows]
    for copy in copies:
        copy.wait()
    rest = rest_ref[...]
    step = product((chain_high_ref[...], chain_low_ref[...]), split(rest))
    right = jnp.concatenate([rest, step[:slots], step[slots:] + rest_3_ref[...]], axis=0)
    right = split(base_ref[...] + right)
    put_tiles(product((high_ref[...], low_ref[...]), right, TN), 0, at, rows_ref, tile, count, early_ref)
    put_tiles(product(columns(right, 0, count * tile - left), right, TN), at, at, rows_ref, tile, count, early_ref)


def stages():
    bits = (lax.axis_size("study") - 1).bit_length()
    return [(0, 1)] + [(low, min(2, bits - low)) for low in range(1, bits, 2)]


def pieces_of(block, low, size, me):
    count = 1 << size
    mine = (me >> low) & (count - 1)
    parts = block.reshape(count, block.shape[0] // count, block.shape[1])
    return [lax.dynamic_index_in_dim(parts, mine ^ m, 0, keepdims=False) for m in range(count)]


def total_over_studies(block, place):
    me = lax.axis_index("study")
    for low, size in stages():
        pieces = pieces_of(block, low, size, me)
        come = [exchange(pieces[m], m << low) for m in range(len(pieces) - 1, 0, -1)]
        block = sum(come, pieces[0])
    others = [*range(HUB + 1, lax.axis_size("inner")), *range(HUB)]
    copies = [send(block, HUB, other) for other in others]
    block = jnp.where(place == HUB, block, sum(copies))
    for low, size in reversed(stages()):
        pieces = [block] + [None] * ((1 << size) - 1)
        for m in range(len(pieces) - 1, 0, -1):
            pieces[m] = exchange(block, m << low)
        for bit in range(size):
            swap = ((me >> (low + bit)) & 1) == 1
            pieces = [jnp.where(swap, pieces[m ^ (1 << bit)], pieces[m]) for m in range(len(pieces))]
        block = jnp.concatenate(pieces, axis=0)
    return block


def on_device(
    trial_count_per_study,
    study_tile_mask,
    sep_order,
    stacked_study_factor,
    diagonal_block_inverses,
    coupling,
    targets,
    sep_prior,
):
    place = lax.axis_index("inner")
    slots = diagonal_block_inverses.shape[0]
    width = sep_prior.shape[0]
    tile = width // study_tile_mask.shape[1]
    wide = width + targets.shape[1]
    reach = (lax.axis_size("inner") - 1) * slots
    order = sep_order[None, :]
    left = width - tile
    own = call(
        own_kernel,
        "own",
        floats(slots, wide),
        [SMEM] + [HBM] * 5,
        6 * slots * slots * wide,
        [
            pltpu.SMEM((1, width // tile), jnp.int32),
            pltpu.VMEM((1, width), jnp.int32),
            pltpu.VMEM((slots, slots), jnp.float32),
            pltpu.VMEM((slots, width), jnp.float32),
            pltpu.VMEM((slots, wide - width), jnp.float32),
            pltpu.SemaphoreType.DMA((5,)),
        ],
    )(
        trial_count_per_study,
        *in_hbm(study_tile_mask, order, diagonal_block_inverses, coupling, targets),
    )
    first, rest, last = call(
        steps_kernel,
        "steps",
        tuple(floats(slots, size) for size in (slots + left, wide - left, reach + left)),
        [SMEM] + [VMEM] * 3,
        6 * slots * slots * reach,
    )(trial_count_per_study, diagonal_block_inverses, stacked_study_factor, own)
    first_1 = send(first, 1, HUB)
    own_0 = send(own, 0, HUB)
    rest_1 = send(rest, 1, HUB)
    last_3 = send(last, 3, HUB)
    rest_3 = send(rest, 3, HUB)
    prior = call(prior_kernel, "prior", floats(width, width), [VMEM, VMEM, ANY], 44 * width**3)(
        order, sep_prior, own_0
    )
    packed = packed_tiles(width, tile)[1] * tile + 8

    def halves(*shape):
        return jax.ShapeDtypeStruct(shape, jnp.bfloat16)

    early = call(
        functools.partial(early_kernel, tile),
        "early",
        (
            halves(reach, left),
            halves(reach, left),
            floats(reach, wide - left),
            halves(2 * slots, slots),
            halves(2 * slots, slots),
            floats(packed, tile),
        ),
        [HBM] * 3 + [VMEM, VMEM, ANY],
        60 * slots * wide * (6 * slots + width),
        [
            pltpu.VMEM((slots, reach + left), jnp.float32),
            pltpu.VMEM((slots, wide), jnp.float32),
            pltpu.VMEM((slots, slots + left), jnp.float32),
            pltpu.SemaphoreType.DMA((3,)),
        ],
    )(*in_hbm(last_3, own_0, first_1), last, rest, prior)
    unit = 8 * lax.axis_size("study")
    padded = -(-packed // unit) * unit
    rows = call(
        functools.partial(gram_kernel, tile),
        "gram",
        floats(padded, tile),
        [HBM] * 2 + [VMEM] * 6,
        6 * slots * wide * (2 * slots + 3 * width),
        [
            pltpu.VMEM((slots, wide - left), jnp.float32),
            pltpu.VMEM((slots, wide - left), jnp.float32),
            pltpu.SemaphoreType.DMA((2,)),
        ],
    )(*in_hbm(rest_1, rest_3), *early)
    total = total_over_studies(rows, place)
    return call(
        factor_kernel,
        "factor_and_solve",
        (floats(width, width), floats(width, tile)),
        [VMEM, VMEM],
        width**3,
        [
            pltpu.VMEM((width, wide), jnp.float32),
            pltpu.VMEM((width, wide), jnp.float32),
            pltpu.VMEM((width, width), jnp.float32),
            pltpu.SemaphoreType.DMA((width // tile, 2)),
        ],
        out_spec=HBM,
    )(total, prior)


def solution(mesh):
    return jax.shard_map(
        on_device,
        mesh=mesh,
        in_specs=(
            P("study"),
            P("study", None),
            P(),
            P(("study", "inner"), None),
            P(("study", "inner"), None),
            P(("study", "inner"), None),
            P(("study", "inner"), None),
            P(),
        ),
        out_specs=(P(), P()),
        check_vma=False,
    )
```

```python
import functools

import jax
import jax.numpy as jnp
from jax import lax
from jax.experimental import pallas as pl
from jax.experimental.pallas import tpu as pltpu
from jax.sharding import PartitionSpec as P

HIGHEST = lax.Precision.HIGHEST
HUB = 2
SPREAD = 16


NN = (((1,), (0,)), ((), ()))
TN = (((0,), (0,)), ((), ()))
VMEM = pl.BlockSpec(memory_space=pltpu.VMEM)
SMEM = pl.BlockSpec(memory_space=pltpu.SMEM)
ANY = pl.BlockSpec(memory_space=pl.ANY)
HBM = pl.BlockSpec(memory_space=pltpu.HBM)


def call(kernel, name, out_shape, in_specs, flops, scratch_shapes=(), out_spec=VMEM):
    many = isinstance(out_shape, tuple)
    return pl.pallas_call(
        kernel,
        out_shape=out_shape,
        in_specs=in_specs,
        out_specs=(out_spec,) * len(out_shape) if many else out_spec,
        scratch_shapes=scratch_shapes,
        cost_estimate=pl.CostEstimate(flops=flops, bytes_accessed=1 << 20, transcendentals=0),
        compiler_params=pltpu.CompilerParams(vmem_limit_bytes=16 << 20),
        name=name,
    )


def floats(*shape):
    return jax.ShapeDtypeStruct(shape, jnp.float32)


def in_hbm(*arrays):
    return [pltpu.with_memory_space_constraint(array, pltpu.HBM) for array in arrays]


def split(x):
    high = x.astype(jnp.bfloat16)
    return high, (x - high.astype(jnp.float32)).astype(jnp.bfloat16)


def product(a, b, dims=NN):
    def one(x, y):
        return lax.dot_general(x, y, dims, preferred_element_type=jnp.float32)

    return one(a[0], b[0]) + (one(a[0], b[1]) + one(a[1], b[0]))


def exchange(block, mask):
    count = lax.axis_size("study")
    return lax.ppermute(block, "study", [(i, i ^ mask) for i in range(count)])


def send(block, source, target):
    return lax.ppermute(block, "inner", [(source, target)])


def packed_tiles(width, tile):
    places, used = {}, 0
    for i in range(width // tile):
        for j in range(i, width // tile + 1):
            if i == j and i % 2:
                places[i, j] = places[i - 1, i - 1]
            else:
                places[i, j] = used
                used += 1
    return {ij: slice(k * tile, (k + 1) * tile) for ij, k in places.items()}, used


def grid_of(tile):
    return tuple(lax.broadcasted_iota(jnp.int32, (tile, tile), axis) for axis in range(2))


def eliminate(block, behind, lane, tile):
    wide = block.shape[1]
    row = lax.broadcasted_iota(jnp.int32, (8, 1), 0)
    groups = [rows[8 * g : 8 * g + 8] for rows in (block, behind) if rows is not None for g in range(SPREAD // 8)]
    spread = [[jnp.broadcast_to(rows[:, lane + k : lane + k + 1], (8, tile)) for rows in groups] for k in range(SPREAD)]
    final = []
    for i in range(SPREAD):
        group, line = divmod(i, 8)
        scale = lax.rsqrt(spread[i][group][line : line + 1])
        final.append(groups[group][line : line + 1] * jnp.tile(scale, (1, wide // tile)))
        below = {g: spread[i][g] * scale for g in range(group, len(groups))}
        below[group] = jnp.where(row > line, below[group], 0.0)
        if line == 7:
            del below[group]
        for k in range(i + 1, SPREAD):
            factor = spread[k][group][line : line + 1] * scale
            for g in below:
                spread[k][g] = spread[k][g] - below[g] * factor
        for g in below:
            groups[g] = groups[g] - jnp.tile(below[g], (1, wide // tile)) * final[-1]
    final = jnp.concatenate(final, axis=0)
    return final, None if behind is None else jnp.concatenate(groups[SPREAD // 8 :], axis=0)


def factor_kernel(total_ref, prior_ref, factor_hbm, solve_hbm, upper_ref, work_ref, factor_ref, sems):
    width = prior_ref.shape[0]
    tile = work_ref.shape[1] - width
    count = width // tile
    place, used = packed_tiles(width, tile)
    row, column = grid_of(tile)
    upper = row <= column
    cut = [slice(i * tile, (i + 1) * tile) for i in range(count + 1)]

    def given(i, j):
        block = total_ref[place[i, j]]
        if i == j and i % 2:
            at = used * tile + i // 2
            block = jnp.where(upper, jnp.where(row == column, total_ref[at : at + 1], block.T), block)
        elif i == j:
            block = jnp.where(upper, block, block.T)
        return block + prior_ref[cut[i], cut[j]] if j < count else block

    def given_row(i):
        return jnp.concatenate([given(i, j) for j in range(i, count + 1)], axis=1)

    copies = []
    work_ref[cut[0]] = given_row(0)
    for i in range(count):
        base = i * tile
        ready = work_ref[base : base + SPREAD, base:]
        behind = work_ref[base + SPREAD : base + 2 * SPREAD, base:]
        for start in range(0, tile, SPREAD):
            final, ready = eliminate(ready, behind, start, tile)
            upper_ref[base + start : base + start + SPREAD, base:] = final
            after, rest, behind = start + 2 * SPREAD, start + 3 * SPREAD, None
            if after < tile:
                final = split(final)
                behind = work_ref[base + after : base + rest, base:] - product(columns(final, after, rest), final, TN)
            if rest < tile:
                later = slice(base + rest, base + tile)
                work_ref[later, base:] = work_ref[later, base:] - product(columns(final, rest, tile), final, TN)
        final = split(upper_ref[cut[i], base:])
        for k in range(i + 1, count):
            at = (k - i) * tile
            old = work_ref[cut[k], k * tile :] if i else given_row(k)
            step = product(columns(final, at, at + tile), columns(final, at, width + tile - base), TN)
            work_ref[cut[k], k * tile :] = old - step
        for j in range(count):
            if j < i:
                factor_ref[cut[j], cut[i]] = jnp.zeros((tile, tile), jnp.float32)
            else:
                block = upper_ref[cut[i], cut[j]]
                factor_ref[cut[j], cut[i]] = (jnp.where(upper, block, 0.0) if i == j else block).T
        copies += copy_all(
            (factor_ref.at[:, cut[i]], upper_ref.at[cut[i], width:]),
            (factor_hbm.at[:, cut[i]], solve_hbm.at[cut[i]]),
            sems.at[i],
        )
    for copy in copies:
        copy.wait()


def live_inverse(count_ref, inverse):
    slots = inverse.shape[0]
    place, places = lax.axis_index("inner"), lax.axis_size("inner")

    def live(shape, axis):
        position = lax.broadcasted_iota(jnp.int32, shape, axis) * places + place
        return (position < count_ref[0]).astype(jnp.float32)

    return inverse * live((slots, 1), 0) * live((1, slots), 1)


def picker(order_ref):
    width = order_ref.shape[1]
    return (lax.broadcasted_iota(jnp.int32, (width, width), 0) == order_ref[...]).astype(jnp.float32)


def copy_all(sources, targets, sems):
    copies = [pltpu.make_async_copy(source, target, sems.at[k]) for k, (source, target) in enumerate(zip(sources, targets))]
    for copy in copies:
        copy.start()
    return copies


def own_kernel(count_ref, mask_hbm, order_hbm, inverse_hbm, coupling_hbm, targets_hbm, own_ref, *refs):
    sources = (mask_hbm, order_hbm, inverse_hbm, coupling_hbm, targets_hbm)
    targets, sems = refs[:5], refs[5]
    mask_ref, order_ref, inverse_ref, coupling_ref, targets_ref = targets
    width, tile = coupling_ref.shape[1], coupling_ref.shape[1] // mask_ref.shape[1]
    copies = copy_all(sources, targets, sems)
    for copy in copies[:2]:
        copy.wait()
    lane_tile = lax.broadcasted_iota(jnp.int32, (1, width), 1) // tile
    column_mask = jnp.zeros((1, width), jnp.float32)
    for t in range(width // tile):
        column_mask = jnp.where(lane_tile == t, mask_ref[0, t].astype(jnp.float32), column_mask)
    pick = picker(order_ref).astype(jnp.bfloat16)

    def ordered(x):
        return lax.dot_general(x, pick, NN, preferred_element_type=jnp.float32).astype(jnp.bfloat16)

    copies[2].wait()
    inverse = split(live_inverse(count_ref, inverse_ref[...]))
    copies[3].wait()
    high, low = split(coupling_ref[...] * column_mask)
    own_ref[:, :width] = product(inverse, (ordered(high), ordered(low)))
    copies[4].wait()
    own_ref[:, width:] = product(inverse, split(targets_ref[...]))


def steps_kernel(count_ref, inverse_ref, factor_ref, own_ref, first_ref, rest_ref, last_ref):
    slots = inverse_ref.shape[0]
    left = first_ref.shape[1] - slots
    reach = last_ref.shape[1] - left
    inverse = split(-live_inverse(count_ref, inverse_ref[...]))
    steps = product(inverse, split(factor_ref[:, :reach]))
    first_ref[:, :slots] = steps[:, :slots]
    last_ref[:, :reach] = steps
    first_ref[:, slots:] = own_ref[:, :left]
    last_ref[:, reach:] = own_ref[:, :left]
    rest_ref[...] = own_ref[:, left:]


def prior_kernel(order_ref, prior_ref, after_ref, ordered_ref):
    pick = picker(order_ref)
    rows = lax.dot_general(pick, prior_ref[...], TN, precision=HIGHEST, preferred_element_type=jnp.float32)
    ordered_ref[...] = jnp.dot(rows, pick, precision=HIGHEST, preferred_element_type=jnp.float32)


def put_tiles(block, top, side, rows_ref, tile, count, add_ref=None):
    place, used = packed_tiles(count * tile, tile)
    row, column = grid_of(tile)

    def piece(i, j):
        a, b = (i - top) * tile, (j - side) * tile
        return block[a : a + tile, b : b + tile]

    def put(rows, value):
        rows_ref[rows] = value if add_ref is None else value + add_ref[rows]

    stop = top + block.shape[0] // tile
    for i in range(top, stop):
        for j in range(max(i, side), side + block.shape[1] // tile):
            if i != j:
                put(place[i, j], piece(i, j))
            elif i % 2:
                at = used * tile + i // 2
                put(slice(at, at + 1), jnp.sum(jnp.where(row == column, piece(i, i), 0.0), axis=0, keepdims=True))
                if i == top:
                    rows = place[i, i]
                    old = rows_ref[rows] if add_ref is None else add_ref[rows]
                    rows_ref[rows] = jnp.where(row <= column, old, piece(i, i) if add_ref is None else old + piece(i, i))
            else:
                put(place[i, i], jnp.where(row <= column, piece(i, i), piece(i + 1, i + 1)) if i + 1 < stop else piece(i, i))


def stack(pairs):
    return tuple(jnp.concatenate([pair[side] for pair in pairs], axis=0) for side in range(2))


def columns(pair, start, stop):
    return pair[0][:, start:stop], pair[1][:, start:stop]


def early_kernel(tile, last_hbm, own_0_hbm, first_hbm, own_last_ref, own_rest_ref, prior_ref, *refs):
    high_ref, low_ref, base_ref, chain_high_ref, chain_low_ref, rows_ref = refs[:6]
    targets, sems = refs[6:9], refs[9]
    last_ref, own_0_ref, first_ref = targets
    slots, wide = own_0_ref.shape
    left = first_ref.shape[1] - slots
    reach = last_ref.shape[1] - left
    count = wide // tile - 1
    copies = copy_all((last_hbm, own_0_hbm, first_hbm), targets, sems)
    cut = [slice(k * slots, (k + 1) * slots) for k in range(3)]
    for copy in copies[1:]:
        copy.wait()
    solved_0 = split(own_0_ref[...])
    part_1 = product(split(first_ref[:, :slots]), solved_0)
    part_1 = jnp.concatenate([part_1[:, :left] + first_ref[:, slots:], part_1[:, left:]], axis=1)
    known = stack([solved_0, split(part_1)])
    step_21 = split(own_last_ref[:, cut[1]])
    part_2 = jnp.concatenate([own_last_ref[:, reach:], own_rest_ref[...]], axis=1)
    part_2 = part_2 + product(split(own_last_ref[:, : 2 * slots]), known)
    copies[0].wait()
    known = stack([known, split(part_2)])
    part_3 = product(split(last_ref[:, :reach]), known)
    part_3 = jnp.concatenate([part_3[:, :left] + last_ref[:, reach:], part_3[:, left:]], axis=1)
    known = stack([known, split(part_3)])
    chain_high_ref[:slots], chain_low_ref[:slots] = step_21
    chain_high_ref[slots:], chain_low_ref[slots:] = split(last_ref[:, cut[1]] + product(split(last_ref[:, cut[2]]), step_21))
    for k, part in enumerate((part_1, part_2, part_3)):
        base_ref[k * slots : (k + 1) * slots] = part[:, left:]
    high_ref[...], low_ref[...] = known[0][slots:, :left], known[1][slots:, :left]
    at = left // tile
    put_tiles(product(columns(known, 0, left), columns(known, 0, left), TN), 0, 0, rows_ref, tile, count)
    put_tiles(product(columns(solved_0, 0, left), columns(solved_0, left, wide), TN), 0, at, rows_ref, tile, count)
    put_tiles(product(columns(solved_0, left, count * tile), columns(solved_0, left, wide), TN), at, at, rows_ref, tile, count)


def gram_kernel(tile, rest_hbm, rest_3_hbm, high_ref, low_ref, base_ref, chain_high_ref, chain_low_ref, early_ref, *refs):
    rows_ref, rest_ref, rest_3_ref, sems = refs
    slots, wide = rest_ref.shape
    left = high_ref.shape[1]
    count = (left + wide) // tile - 1
    at = left // tile
    copies = copy_all((rest_hbm, rest_3_hbm), (rest_ref, rest_3_ref), sems)
    place, used = packed_tiles(count * tile, tile)
    rows_ref[used * tile :] = jnp.zeros((rows_ref.shape[0] - used * tile, tile), jnp.float32)
    done = [place[i, j] for i in range(at) for j in range(i, at) if i < j or i % 2 == 0]
    for rows in done + [slice(used * tile + i // 2, used * tile + i // 2 + 1) for i in range(1, at, 2)]:
        rows_ref[rows] = early_ref[rows]
    for copy in copies:
        copy.wait()
    rest = rest_ref[...]
    step = product((chain_high_ref[...], chain_low_ref[...]), split(rest))
    right = jnp.concatenate([rest, step[:slots], step[slots:] + rest_3_ref[...]], axis=0)
    right = split(base_ref[...] + right)
    put_tiles(product((high_ref[...], low_ref[...]), right, TN), 0, at, rows_ref, tile, count, early_ref)
    put_tiles(product(columns(right, 0, count * tile - left), right, TN), at, at, rows_ref, tile, count, early_ref)


def stages():
    bits = (lax.axis_size("study") - 1).bit_length()
    return [(0, 1)] + [(low, min(2, bits - low)) for low in range(1, bits, 2)]


def pieces_of(block, low, size, me):
    count = 1 << size
    mine = (me >> low) & (count - 1)
    parts = block.reshape(count, block.shape[0] // count, block.shape[1])
    return [lax.dynamic_index_in_dim(parts, mine ^ m, 0, keepdims=False) for m in range(count)]


def total_over_studies(block, place):
    me = lax.axis_index("study")
    for low, size in stages():
        pieces = pieces_of(block, low, size, me)
        come = [exchange(pieces[m], m << low) for m in range(1, len(pieces))]
        block = sum(come, pieces[0])
    others = [*range(HUB + 1, lax.axis_size("inner")), *range(HUB)]
    copies = [send(block, HUB, other) for other in others]
    block = jnp.where(place == HUB, block, sum(copies))
    for low, size in reversed(stages()):
        pieces = [block] + [None] * ((1 << size) - 1)
        for m in range(len(pieces) - 1, 0, -1):
            pieces[m] = exchange(block, m << low)
        for bit in range(size):
            swap = ((me >> (low + bit)) & 1) == 1
            pieces = [jnp.where(swap, pieces[m ^ (1 << bit)], pieces[m]) for m in range(len(pieces))]
        block = jnp.concatenate(pieces, axis=0)
    return block


def on_device(
    trial_count_per_study,
    study_tile_mask,
    sep_order,
    stacked_study_factor,
    diagonal_block_inverses,
    coupling,
    targets,
    sep_prior,
):
    place = lax.axis_index("inner")
    slots = diagonal_block_inverses.shape[0]
    width = sep_prior.shape[0]
    tile = width // study_tile_mask.shape[1]
    wide = width + targets.shape[1]
    reach = (lax.axis_size("inner") - 1) * slots
    order = sep_order[None, :]
    left = width - tile
    own = call(
        own_kernel,
        "own",
        floats(slots, wide),
        [SMEM] + [HBM] * 5,
        6 * slots * slots * wide,
        [
            pltpu.SMEM((1, width // tile), jnp.int32),
            pltpu.VMEM((1, width), jnp.int32),
            pltpu.VMEM((slots, slots), jnp.float32),
            pltpu.VMEM((slots, width), jnp.float32),
            pltpu.VMEM((slots, wide - width), jnp.float32),
            pltpu.SemaphoreType.DMA((5,)),
        ],
    )(
        trial_count_per_study,
        *in_hbm(study_tile_mask, order, diagonal_block_inverses, coupling, targets),
    )
    first, rest, last = call(
        steps_kernel,
        "steps",
        tuple(floats(slots, size) for size in (slots + left, wide - left, reach + left)),
        [SMEM] + [VMEM] * 3,
        6 * slots * slots * reach,
    )(trial_count_per_study, diagonal_block_inverses, stacked_study_factor, own)
    first_1 = send(first, 1, HUB)
    own_0 = send(own, 0, HUB)
    rest_1 = send(rest, 1, HUB)
    last_3 = send(last, 3, HUB)
    rest_3 = send(rest, 3, HUB)
    prior = call(prior_kernel, "prior", floats(width, width), [VMEM, VMEM, ANY], 44 * width**3)(
        order, sep_prior, own_0
    )
    packed = packed_tiles(width, tile)[1] * tile + 8

    def halves(*shape):
        return jax.ShapeDtypeStruct(shape, jnp.bfloat16)

    early = call(
        functools.partial(early_kernel, tile),
        "early",
        (
            halves(reach, left),
            halves(reach, left),
            floats(reach, wide - left),
            halves(2 * slots, slots),
            halves(2 * slots, slots),
            floats(packed, tile),
        ),
        [HBM] * 3 + [VMEM, VMEM, ANY],
        60 * slots * wide * (6 * slots + width),
        [
            pltpu.VMEM((slots, reach + left), jnp.float32),
            pltpu.VMEM((slots, wide), jnp.float32),
            pltpu.VMEM((slots, slots + left), jnp.float32),
            pltpu.SemaphoreType.DMA((3,)),
        ],
    )(*in_hbm(last_3, own_0, first_1), last, rest, prior)
    unit = 8 * lax.axis_size("study")
    padded = -(-packed // unit) * unit
    rows = call(
        functools.partial(gram_kernel, tile),
        "gram",
        floats(padded, tile),
        [HBM] * 2 + [VMEM] * 6,
        6 * slots * wide * (2 * slots + 3 * width),
        [
            pltpu.VMEM((slots, wide - left), jnp.float32),
            pltpu.VMEM((slots, wide - left), jnp.float32),
            pltpu.SemaphoreType.DMA((2,)),
        ],
    )(*in_hbm(rest_1, rest_3), *early)
    total = total_over_studies(rows, place)
    return call(
        factor_kernel,
        "factor_and_solve",
        (floats(width, width), floats(width, tile)),
        [VMEM, VMEM],
        width**3,
        [
            pltpu.VMEM((width, wide), jnp.float32),
            pltpu.VMEM((width, wide), jnp.float32),
            pltpu.VMEM((width, width), jnp.float32),
            pltpu.SemaphoreType.DMA((width // tile, 2)),
        ],
        out_spec=HBM,
    )(total, prior)


def solution(mesh):
    return jax.shard_map(
        on_device,
        mesh=mesh,
        in_specs=(
            P("study"),
            P("study", None),
            P(),
            P(("study", "inner"), None),
            P(("study", "inner"), None),
            P(("study", "inner"), None),
            P(("study", "inner"), None),
            P(),
        ),
        out_specs=(P(), P()),
        check_vma=False,
    )
```
